32 devices in a mesh: dp: 4 (over y, x), ctx: 8 (over z, core).
Axes of the slice: x: 2, y: 2, z: 4, core: 2. Of those that a mesh axis runs over, the one named last changes fastest.
Arguments:
- tokens: bfloat16 [4, 1024, 2048], P('dp', 'ctx'), may hold values from -6 to 6
- positions: int32 [4, 1024], P('dp', 'ctx'), may hold values from 0 to 1023, as said below
- norm_gain: float32 [2048], replicated, may hold values from 0.5 to 1.5
- norm_bias: float32 [2048], replicated, may hold values from -1.8 to 1.8
- qkv_weight: bfloat16 [2048, 6144], P('ctx'), may hold values from -0.125 to 0.125
- qkv_bias: float32 [6144], replicated, may hold values from -1.8 to 1.8
- dense_weight: bfloat16 [2048, 2048], P('ctx'), may hold values from -2 to 2
- dense_bias: float32 [2048], replicated, may hold values from -1.8 to 1.8
- up_weight: bfloat16 [2048, 8192], P('ctx'), may hold values from -0.125 to 0.125
- up_bias: float32 [8192], replicated, may hold values from -1.8 to 1.8
- down_weight: bfloat16 [8192, 2048], P('ctx'), may hold values from -0.0625 to 0.0625
- down_bias: float32 [2048], replicated, may hold values from -1.8 to 1.8
- clip_limit: int32 [32], replicated, may hold values from 3 to 11
- cotangent: bfloat16 [4, 1024, 2048], P('dp', 'ctx'), may hold values from -6 to 6
Outputs:
- layer_out: bfloat16 [4, 1024, 2048], P('dp', 'ctx')
- tokens_grad: float32 [4, 1024, 2048], P('dp', 'ctx')
- norm_gain_grad: float32 [2048], replicated
- norm_bias_grad: float32 [2048], replicated
- qkv_weight_grad: float32 [2048, 6144], P('ctx')
- qkv_bias_grad: float32 [6144], replicated
- dense_weight_grad: float32 [2048, 2048], P('ctx')
- dense_bias_grad: float32 [2048], replicated
- up_weight_grad: float32 [2048, 8192], P('ctx')
- up_bias_grad: float32 [8192], replicated
- down_weight_grad: float32 [8192, 2048], P('ctx')
- down_bias_grad: float32 [2048], replicated
- head_maxima: float32 [32], replicated
- clipped_weight: float32 [2048, 4096], P('ctx')
- clipped_bias: float32 [4096], replicated
The draws below stay inside these ranges and needn't reach their ends.
Inputs may be any that keep to these rules, and one draw needn't show every extreme that they name: `positions`: within each sequence the ids rise by one from 0 at its first token and return to 0 at the first token of each packed document; the first sequence holds a single document.
All inputs are finite; a program needn't handle non-finite values.
Results may differ from the reference program's by a relative error of at most 0.017.
Values may be sent and summed in bfloat16 or wider, within the bound.
No kernel may reach another device: no remote copies, remote signals or barrier semaphores. Data moves between devices by JAX's collectives and lax.ppermute only.
A program may use at most 512 MiB of HBM per device.

```python
import jax
import jax.numpy as jnp
from jax import lax

D = 2048
HEADS = 32
HEAD_DIM = 64
ROT = 32
FF = 8192
NSEQ = 4
SEQ_LEN = 1024


def draw_positions(key, part):
    doc_flags = jax.random.randint(key, (NSEQ, SEQ_LEN), 0, max(2, SEQ_LEN // 4))
    seq_index = jnp.broadcast_to(jnp.arange(NSEQ, dtype=jnp.int32)[:, None], (NSEQ, SEQ_LEN))
    doc_flags = jnp.where(seq_index == 0, 1, doc_flags)
    time_index = jnp.broadcast_to(jnp.arange(SEQ_LEN, dtype=jnp.int32), (NSEQ, SEQ_LEN))
    starts = jnp.where((doc_flags == 0) | (time_index == 0), time_index, 0)
    return (time_index - lax.cummax(starts, axis=1)).astype(jnp.int32)


def with_ends(values, stream_key, low, largest):
    index_at = [jax.random.randint(jax.random.fold_in(stream_key, axis), (), 0, length) for axis, length in enumerate(values.shape)]
    main_axis = values.shape.index(max(values.shape))
    neighbour = index_at[:main_axis] + [(index_at[main_axis] + 1) % values.shape[main_axis]] + index_at[main_axis + 1:]
    return values.at[tuple(index_at)].set(low).at[tuple(neighbour)].set(largest)


def levels(stream_key, dims, cuts, low, high):
    level = 1.0
    for position, parts in cuts:
        draws = jax.random.uniform(jax.random.fold_in(jax.random.fold_in(stream_key, 6), position), (parts,), jnp.float32, low / len(cuts), high / len(cuts))
        level = level * jnp.repeat(jnp.exp(draws), dims[position] // parts).reshape((-1,) + (1,) * (len(dims) - 1 - position))
    return level


def bell_draw(rng, shape, spread, bound, pieces=(), kind=jnp.bfloat16):
    values = spread * jax.random.normal(rng, shape, jnp.float32)
    if pieces:
        values = values * levels(rng, shape, pieces, -0.22, 0.18)
    return jnp.clip(values, -bound, bound).astype(kind)


def setup_inputs(seed: int = 0) -> dict:
    key_list = jax.random.split(jax.random.key(seed), 15)
    return {
        "tokens": bell_draw(key_list[0], (NSEQ, SEQ_LEN, D), 1.0, 6.0, ((0, 4), (1, 8))),
        "positions": draw_positions(jax.random.fold_in(key_list[14], 71), 0),
        "norm_gain": jnp.clip(1.0 + 0.1 * jax.random.normal(key_list[2], (D,), jnp.float32), 0.5, 1.5),
        "norm_bias": bell_draw(key_list[3], (D,), 0.3, 1.8, (), jnp.float32),
        "qkv_weight": bell_draw(key_list[4], (D, 3 * D), D ** -0.5, 0.125, ((0, 8),)),
        "qkv_bias": bell_draw(key_list[5], (3 * D,), 0.3, 1.8, (), jnp.float32),
        "dense_weight": bell_draw(key_list[6], (D, D), (max(1, D * 4 // SEQ_LEN)) ** -0.5, 2.0, ((0, 8),)),
        "dense_bias": bell_draw(key_list[7], (D,), 0.3, 1.8, (), jnp.float32),
        "up_weight": bell_draw(key_list[8], (D, FF), D ** -0.5, 0.125, ((0, 8),)),
        "up_bias": bell_draw(key_list[9], (FF,), 0.3, 1.8, (), jnp.float32),
        "down_weight": bell_draw(key_list[10], (FF, D), FF ** -0.5, 0.0625, ((0, 8),)),
        "down_bias": bell_draw(key_list[11], (D,), 0.3, 1.8, (), jnp.float32),
        "clip_limit": with_ends(jax.random.randint(key_list[12], (HEADS,), 3, 12), jax.random.fold_in(key_list[12], 1), 3, 11).astype(jnp.int32),
        "cotangent": bell_draw(key_list[13], (NSEQ, SEQ_LEN, D), 1.0, 6.0, ((0, 4), (1, 8))),
    }


epsilon = 1e-05
masked_score = -1e+30
rope_base = 10000.0
highest = lax.Precision.HIGHEST

@jax.custom_vjp
def low(v):
    return lax.optimization_barrier(v.astype(jnp.bfloat16)).astype(jnp.float32)

@jax.custom_vjp
def low_back(v):
    return v

def low_keep(v):
    return (low(v), None)

def low_pass(kept, grad):
    return (grad,)

def back_keep(v):
    return (v, None)

def back_low(kept, grad):
    return (low(grad),)
low.defvjp(low_keep, low_pass)
low_back.defvjp(back_keep, back_low)

def product(left, right):
    return jnp.dot(left, right, precision=highest, preferred_element_type=jnp.float32)

def rotary_tables(positions):
    half_rot = ROT // 2
    frequency = rope_base ** (-(jnp.arange(half_rot, dtype=jnp.float32) * 2.0 / ROT))
    angles = positions.astype(jnp.float32)[..., None] * frequency
    cosine = jnp.cos(angles)
    sine_part = jnp.sin(angles)
    return (jnp.concatenate([cosine, cosine], -1)[..., None, :], jnp.concatenate([sine_part, sine_part], -1)[..., None, :])

def rotate(values, cosine, sine_part):
    half_rot = ROT // 2
    turned = values[..., :ROT]
    swapped = jnp.concatenate([-turned[..., half_rot:], turned[..., :half_rot]], -1)
    return jnp.concatenate([turned * cosine + swapped * sine_part, values[..., ROT:]], -1)

def attend(queries, keys, values):
    length = queries.shape[0]
    block_len = 512 if length % 512 == 0 else length
    block_count = length // block_len
    score_scale = HEAD_DIM ** (-0.5)
    key_index = jnp.arange(length).astype(jnp.int32)

    def one_block(block_item):
        query_block, first_row = block_item
        scores = low_back(jnp.einsum('qhd,khd->hqk', query_block, keys, precision=highest) * score_scale)
        query_index = first_row + jnp.arange(block_len).astype(jnp.int32)
        allowed = query_index[:, None] >= key_index[None, :]
        scores = jnp.where(allowed, scores, masked_score)
        row_max = lax.optimization_barrier(jnp.max(scores, axis=-1, keepdims=True))
        expo_scores = jnp.exp(scores - row_max)
        probs = expo_scores / lax.optimization_barrier(jnp.sum(expo_scores, axis=-1, keepdims=True))
        attended = jnp.einsum('hqk,khd->qhd', low(probs), values, precision=highest)
        return (attended, lax.optimization_barrier(jnp.max(row_max[..., 0], axis=-1)))
    blocks = queries.reshape(block_count, block_len, HEADS, HEAD_DIM)
    firsts = (jnp.arange(block_count) * block_len).astype(jnp.int32)
    attended, maxima = lax.map(jax.checkpoint(one_block), (blocks, firsts))
    return (attended.reshape(length, HEADS, HEAD_DIM), lax.optimization_barrier(jnp.max(maxima, axis=0)))

def layer_seq(tokens, positions, norm_gain, norm_bias, qkv_weight, qkv_bias, dense_weight, dense_bias, up_weight, up_bias, down_weight, down_bias):
    length = tokens.shape[0]
    centre = tokens - lax.optimization_barrier(jnp.mean(tokens, axis=-1, keepdims=True))
    normed = centre * lax.rsqrt(lax.optimization_barrier(jnp.mean(centre * centre, axis=-1, keepdims=True)) + epsilon)
    hidden = low(normed * norm_gain + norm_bias)
    joined = low_back(product(hidden, qkv_weight) + qkv_bias)
    cosine, sine_part = rotary_tables(positions)
    queries = low(rotate(joined[:, :D].reshape(length, HEADS, HEAD_DIM), cosine, sine_part))
    keys = low(rotate(joined[:, D:2 * D].reshape(length, HEADS, HEAD_DIM), cosine, sine_part))
    values = low(joined[:, 2 * D:].reshape(length, HEADS, HEAD_DIM))
    attended, maxima = attend(queries, keys, values)
    attended = low(low_back(attended.reshape(length, D)))
    upward = low_back(product(hidden, up_weight) + up_bias)
    activated = low(jax.nn.gelu(upward, approximate=True))
    result = tokens + (product(attended, dense_weight) + dense_bias) + (product(activated, down_weight) + down_bias)
    return (result, maxima)

def reference(tokens, positions, norm_gain, norm_bias, qkv_weight, qkv_bias, dense_weight, dense_bias, up_weight, up_bias, down_weight, down_bias, clip_limit, cotangent):
    params = tuple((array_in.astype(jnp.float32) for array_in in (norm_gain, norm_bias, qkv_weight, qkv_bias, dense_weight, dense_bias, up_weight, up_bias, down_weight, down_bias)))

    def forward(inputs, *weights):

        def one_seq(unused_carry, seq_item):
            seq_tokens, seq_positions = seq_item
            result, maxima = jax.checkpoint(layer_seq)(seq_tokens, seq_positions, *weights)
            return (unused_carry, (result, maxima))
        unused_carry, (results, maxima) = lax.scan(one_seq, jnp.zeros((), jnp.float32), (inputs, positions))
        return (results, lax.optimization_barrier(jnp.max(maxima, axis=0)))
    results, pullback, maxima = jax.vjp(forward, tokens.astype(jnp.float32), *params, has_aux=True)
    grads_all = pullback(cotangent.astype(jnp.float32))
    limits = clip_limit.astype(jnp.float32)
    factor = limits / jnp.maximum(maxima, limits)
    column_scale = jnp.tile(jnp.repeat(jnp.sqrt(factor), HEAD_DIM), 2)
    clipped_weight = qkv_weight[:, :2 * D].astype(jnp.float32) * column_scale
    clipped_bias = qkv_bias[:2 * D].astype(jnp.float32) * column_scale
    return (results.astype(jnp.bfloat16), grads_all[0], grads_all[1], grads_all[2], grads_all[3], grads_all[4], grads_all[5], grads_all[6], grads_all[7], grads_all[8], grads_all[9], grads_all[10], maxima, clipped_weight, clipped_bias)
```

```python
from functools import partial

import jax
import jax.numpy as jnp
from jax import lax
from jax.sharding import PartitionSpec as P

ROT = 32
EPSILON = 1e-05
MASKED = -1e30
ROPE_BASE = 10000.0
BF16 = jnp.bfloat16
F32 = jnp.float32


def rotary_tables(positions):
    half_rot = ROT // 2
    frequency = ROPE_BASE ** (-(jnp.arange(half_rot, dtype=F32) * 2.0 / ROT))
    angles = positions.astype(F32)[..., None] * frequency
    cosine = jnp.cos(angles)
    sine = jnp.sin(angles)
    return (
        jnp.concatenate([cosine, cosine], -1)[..., None, :],
        jnp.concatenate([sine, sine], -1)[..., None, :],
    )


def rotate(values, cosine, sine):
    half_rot = ROT // 2
    turned = values[..., :ROT]
    swapped = jnp.concatenate([-turned[..., half_rot:], turned[..., :half_rot]], -1)
    return jnp.concatenate([turned * cosine + swapped * sine, values[..., ROT:]], -1)


def rotate_back(gradient, cosine, sine):
    half_rot = ROT // 2
    turned = gradient[..., :ROT]
    scaled = turned * sine
    swapped = jnp.concatenate([scaled[..., half_rot:], -scaled[..., :half_rot]], -1)
    return jnp.concatenate([turned * cosine + swapped, gradient[..., ROT:]], -1)


def dot(left, right, contract):
    return lax.dot_general(
        left, right, ((contract[:1], contract[1:]), ((), ())), preferred_element_type=F32
    )


def per_device(
    tokens,
    positions,
    norm_gain,
    norm_bias,
    qkv_weight,
    qkv_bias,
    dense_weight,
    dense_bias,
    up_weight,
    up_bias,
    down_weight,
    down_bias,
    clip_limit,
    cotangent,
):
    seqs, stretch, width = tokens.shape
    heads = clip_limit.shape[0]
    head_dim = width // heads
    rows = seqs * stretch
    parts = lax.axis_size("ctx")
    part = lax.axis_index("ctx")
    own_heads = heads // parts
    own = own_heads * head_dim
    own_rows = qkv_weight.shape[0]
    own_ff = down_weight.shape[0]
    length = stretch * parts
    all_rows = seqs * length
    scale = head_dim ** (-0.5)

    pieces = jnp.concatenate(
        [
            qkv_weight.reshape(own_rows, 3, parts, own)
            .transpose(2, 0, 1, 3)
            .reshape(parts, own_rows, 3 * own),
            up_weight.reshape(own_rows, parts, own_ff).transpose(1, 0, 2),
        ],
        axis=2,
    )
    in_weight = lax.all_to_all(pieces, "ctx", split_axis=0, concat_axis=0, tiled=True).reshape(
        width, 3 * own + own_ff
    )

    grad_rows = lax.all_gather(cotangent, "ctx", axis=1, tiled=True).reshape(all_rows, width)
    inputs = tokens.reshape(rows, width).astype(F32)
    centre = inputs - jnp.mean(inputs, axis=-1, keepdims=True)
    inv_std = lax.rsqrt(jnp.mean(centre * centre, axis=-1, keepdims=True) + EPSILON)
    normed = centre * inv_std
    hidden_local = (normed * norm_gain + norm_bias).astype(BF16)
    hidden = lax.all_gather(
        hidden_local.reshape(seqs, stretch, width), "ctx", axis=1, tiled=True
    ).reshape(all_rows, width)
    all_positions = lax.all_gather(positions, "ctx", axis=1, tiled=True)

    qkv_own_bias = lax.dynamic_slice_in_dim(
        qkv_bias.reshape(3, parts, own), part, 1, axis=1
    ).reshape(3 * own)
    up_own_bias = lax.dynamic_slice_in_dim(up_bias, part * own_ff, own_ff)

    projected = dot(hidden, in_weight, (1, 0))
    joined = projected[:, : 3 * own] + qkv_own_bias
    upward = projected[:, 3 * own :] + up_own_bias
    cosine, sine = rotary_tables(all_positions)
    shaped = joined.reshape(seqs, length, 3, own_heads, head_dim)
    queries = rotate(shaped[:, :, 0], cosine, sine).astype(BF16)
    keys = rotate(shaped[:, :, 1], cosine, sine).astype(BF16)
    values = shaped[:, :, 2].astype(BF16)
    place = jnp.arange(length, dtype=jnp.int32)
    allowed = place[:, None] >= place[None, :]
    scores = (
        jnp.einsum("sqhd,skhd->shqk", queries, keys, preferred_element_type=F32) * scale
    )
    scores = jnp.where(allowed, scores, MASKED)
    row_max = jnp.max(scores, axis=-1, keepdims=True)
    expo = jnp.exp(scores - row_max)
    row_sum = jnp.sum(expo, axis=-1, keepdims=True)
    probs = expo / row_sum
    probs_low = probs.astype(BF16)
    mixed = jnp.einsum("shqk,skhd->sqhd", probs_low, values, preferred_element_type=F32)
    attended = mixed.reshape(all_rows, own).astype(BF16)
    own_maxima = jnp.max(row_max, axis=(0, 2, 3))
    slots = lax.dynamic_update_slice_in_dim(
        jnp.full((heads,), MASKED, F32), own_maxima, part * own_heads, axis=0
    )
    head_maxima = lax.pmax(slots, ("dp", "ctx"))

    activated = jax.nn.gelu(upward, approximate=True).astype(BF16)
    branch = dot(attended, dense_weight, (1, 0)) + dot(activated, down_weight, (1, 0))
    branch_sum = lax.psum_scatter(
        branch.astype(BF16).reshape(seqs, length, width), "ctx", scatter_dimension=1, tiled=True
    ).reshape(rows, width)
    layer_out = (inputs + branch_sum.astype(F32) + dense_bias + down_bias).astype(BF16)

    mixed_grad = dot(grad_rows, dense_weight, (1, 1)).astype(BF16)
    act_grad = dot(grad_rows, down_weight, (1, 1))
    dense_grad = dot(attended, grad_rows, (0, 0))
    down_grad = dot(activated, grad_rows, (0, 0))
    out_bias_grad = jnp.sum(cotangent.reshape(rows, width).astype(F32), axis=0)
    unused_value, gelu_back = jax.vjp(partial(jax.nn.gelu, approximate=True), upward)
    up_low = gelu_back(act_grad)[0].astype(BF16)

    mixed_low = mixed_grad.reshape(seqs, length, own_heads, head_dim)
    value_grad = jnp.einsum("shqk,sqhd->skhd", probs_low, mixed_low, preferred_element_type=F32)
    prob_grad = jnp.einsum("sqhd,skhd->shqk", mixed_low, values, preferred_element_type=F32)
    delta = jnp.sum(probs * prob_grad, axis=-1, keepdims=True)
    score_grad = (probs * (prob_grad - delta)).astype(BF16)
    query_grad = (
        jnp.einsum("shqk,skhd->sqhd", score_grad, keys, preferred_element_type=F32) * scale
    )
    key_grad = (
        jnp.einsum("shqk,sqhd->skhd", score_grad, queries, preferred_element_type=F32) * scale
    )
    joined_low = (
        jnp.stack(
            [
                rotate_back(query_grad, cosine, sine),
                rotate_back(key_grad, cosine, sine),
                value_grad,
            ],
            axis=2,
        )
        .reshape(all_rows, 3 * own)
        .astype(BF16)
    )

    both = jnp.concatenate([joined_low, up_low], axis=1)
    hidden_part = dot(both, in_weight, (1, 1))
    hidden_grad = (
        lax.psum_scatter(
            hidden_part.astype(BF16).reshape(seqs, length, width),
            "ctx",
            scatter_dimension=1,
            tiled=True,
        )
        .reshape(rows, width)
        .astype(F32)
    )
    in_grad = dot(hidden, both, (0, 0)).astype(BF16)
    in_quarter = lax.psum_scatter(
        in_grad.reshape(parts, own_rows, 3 * own + own_ff),
        "dp",
        scatter_dimension=1,
        tiled=True,
    )
    in_quarter = lax.all_to_all(in_quarter, "ctx", split_axis=0, concat_axis=0, tiled=True)
    in_rows = lax.all_gather(in_quarter.transpose(1, 0, 2), "dp", axis=0, tiled=True)
    qkv_grad = (
        in_rows[:, :, : 3 * own]
        .reshape(own_rows, parts, 3, own)
        .transpose(0, 2, 1, 3)
        .reshape(own_rows, 3 * width)
        .astype(F32)
    )
    up_grad = in_rows[:, :, 3 * own :].reshape(own_rows, parts * own_ff).astype(F32)
    out_grad = lax.psum(jnp.concatenate([dense_grad, down_grad], axis=0).astype(BF16), "dp")

    gain_part = jnp.sum(hidden_grad * normed, axis=0)
    shift_part = jnp.sum(hidden_grad, axis=0)
    scaled = hidden_grad * norm_gain
    tokens_grad = cotangent.reshape(rows, width).astype(F32) + inv_std * (
        scaled
        - jnp.mean(scaled, axis=-1, keepdims=True)
        - normed * jnp.mean(scaled * normed, axis=-1, keepdims=True)
    )
    qkv_bias_part = lax.dynamic_update_slice(
        jnp.zeros((3, parts, own), F32),
        jnp.sum(joined_low.astype(F32), axis=0).reshape(3, 1, own),
        (0, part, 0),
    ).reshape(3 * width)
    up_bias_part = lax.dynamic_update_slice(
        jnp.zeros((parts * own_ff,), F32), jnp.sum(up_low.astype(F32), axis=0), (part * own_ff,)
    )
    gain_grad, shift_grad, qkv_bias_grad, out_bias_grad, up_bias_grad = lax.psum(
        (gain_part, shift_part, qkv_bias_part, out_bias_grad, up_bias_part), ("dp", "ctx")
    )
    limits = clip_limit.astype(F32)
    factor = limits / jnp.maximum(head_maxima, limits)
    column_scale = jnp.tile(jnp.repeat(jnp.sqrt(factor), head_dim), 2)
    clipped_weight = qkv_weight[:, : 2 * width].astype(F32) * column_scale
    clipped_bias = qkv_bias[: 2 * width] * column_scale
    return (
        layer_out.reshape(seqs, stretch, width),
        tokens_grad.reshape(seqs, stretch, width),
        gain_grad,
        shift_grad,
        qkv_grad,
        qkv_bias_grad,
        out_grad[:own].astype(F32),
        out_bias_grad,
        up_grad,
        up_bias_grad,
        out_grad[own:].astype(F32),
        out_bias_grad,
        head_maxima,
        clipped_weight,
        clipped_bias,
    )


def solution(mesh):
    rows = P("dp", "ctx", None)
    weight = P("ctx", None)
    in_specs = (rows, P("dp", "ctx"), P(), P()) + (weight, P()) * 4 + (P(), rows)
    out_specs = (
        (rows, rows, P(), P()) + (weight, P()) * 4 + (P(), weight, P())
    )
    return jax.shard_map(
        per_device, mesh=mesh, in_specs=in_specs, out_specs=out_specs, check_vma=False
    )
```

```python
from functools import partial

import jax
import jax.numpy as jnp
from jax import lax
from jax.experimental import pallas as pl
from jax.experimental.pallas import tpu as pltpu
from jax.sharding import PartitionSpec as P

ROT = 32
EPSILON = 1e-05
MASKED = -1e30
ROPE_BASE = 10000.0
BF16 = jnp.bfloat16
F32 = jnp.float32
LANES = 128
HEAD = 64


def dot(left, right, contract):
    return lax.dot_general(
        left, right, ((contract[:1], contract[1:]), ((), ())), preferred_element_type=F32
    )


def swap(value, axis, bit):
    return lax.ppermute(value, axis, [(i, i ^ bit) for i in range(lax.axis_size(axis))])


def bits_of(axis):
    return [1 << i for i in range(lax.axis_size(axis).bit_length() - 1)]


def all_sum(value, axes):
    for axis in axes:
        for bit in bits_of(axis):
            value = value + swap(value, axis, bit)
    return value


def all_rows(value, axis):
    index = lax.axis_index(axis)
    for bit in bits_of(axis):
        other = swap(value, axis, bit)
        upper = (index & bit) != 0
        value = jnp.where(
            upper, jnp.concatenate([other, value], 0), jnp.concatenate([value, other], 0)
        )
    return value


def take(value, start, size, axis):
    return lax.dynamic_slice_in_dim(value, start, size, axis)


def first_place(index):
    return (index & 1) * 2 + (index >> 1)


def my_part(value, axis):
    index = lax.axis_index("dp")
    size = value.shape[axis] // 8
    return jnp.concatenate(
        [
            take(value, first_place(index) * size, size, axis),
            take(value, (4 + index) * size, size, axis),
        ],
        axis,
    )


def after(value, *others):
    return lax.optimization_barrier((value, others))[0]


def along_both(pair):
    return swap(pair[0], "dp", 1), swap(pair[1], "dp", 2)


def plus(left, right):
    return (left.astype(F32) + right.astype(F32)).astype(BF16)


def outgoing(value, axis):
    index = lax.axis_index("dp")
    size = value.shape[axis] // 8
    return (
        take(value, (1 - (index & 1)) * 2 * size, 2 * size, axis),
        take(value, (4 + (1 - (index >> 1)) * 2) * size, 2 * size, axis),
    )


def first_sums(value, received, axis):
    index = lax.axis_index("dp")
    size = value.shape[axis] // 8
    return (
        plus(take(value, (index & 1) * 2 * size, 2 * size, axis), received[0]),
        plus(take(value, (4 + (index >> 1) * 2) * size, 2 * size, axis), received[1]),
    )


def outgoing_again(sums, axis):
    index = lax.axis_index("dp")
    size = sums[0].shape[axis] // 2
    return (
        take(sums[1], (1 - (index & 1)) * size, size, axis),
        take(sums[0], (1 - (index >> 1)) * size, size, axis),
    )


def second_sums(sums, received, axis):
    index = lax.axis_index("dp")
    size = sums[0].shape[axis] // 2
    return jnp.concatenate(
        [
            plus(take(sums[0], (index >> 1) * size, size, axis), received[1]),
            plus(take(sums[1], (index & 1) * size, size, axis), received[0]),
        ],
        axis,
    )


def forwarded(received, axis):
    half = received[0].shape[axis] // 2
    return (
        lax.slice_in_dim(received[1], 0, half, axis=axis),
        lax.slice_in_dim(received[0], half, 2 * half, axis=axis),
    )


def four_parts(part, near, far, axis):
    return [part, near[0], near[1], jnp.concatenate(far, axis)]


def place_rows(index_ref, *refs):
    parts, out = refs[:-1], refs[-1]
    eighth = parts[0].shape[-2] // 2
    me = index_ref[0]
    for offset, ref in enumerate(parts):
        owner = me ^ offset
        block = ref[0].astype(out.dtype)
        start = pl.multiple_of(first_place(owner) * eighth, eighth)
        out[pl.ds(start, eighth), :] = block[:eighth]
        start = pl.multiple_of((4 + owner) * eighth, eighth)
        out[pl.ds(start, eighth), :] = block[eighth:]


def place_columns(index_ref, *refs):
    parts, out = refs[:-1], refs[-1]
    eighth = parts[0].shape[-1] // 2
    me = index_ref[0]
    for offset, ref in enumerate(parts):
        owner = me ^ offset
        start = pl.multiple_of(first_place(owner) * eighth, eighth)
        out[:, pl.ds(start, eighth)] = ref[:, :eighth].astype(out.dtype)
        start = pl.multiple_of((4 + owner) * eighth, eighth)
        out[:, pl.ds(start, eighth)] = ref[:, eighth:].astype(out.dtype)


def place(body, parts, grid, in_block, in_map, out_shape, out_block, out_map):
    index = lax.axis_index("dp").astype(jnp.int32).reshape(1)
    size = sum(part.size * part.dtype.itemsize for part in parts)
    return pl.pallas_call(
        body,
        out_shape=out_shape,
        grid_spec=pltpu.PrefetchScalarGridSpec(
            num_scalar_prefetch=1,
            grid=grid,
            in_specs=[pl.BlockSpec(in_block, in_map)] * 4,
            out_specs=pl.BlockSpec(out_block, out_map),
        ),
        compiler_params=pltpu.CompilerParams(vmem_limit_bytes=32 << 20),
        cost_estimate=pl.CostEstimate(
            flops=0,
            transcendentals=0,
            bytes_accessed=size + out_shape.size * out_shape.dtype.itemsize,
        ),
    )(index, *parts)


def full_rows(parts, own_rows):
    blocks, size, columns = parts[0].shape
    return place(
        place_rows,
        parts,
        (blocks,),
        (1, size, columns),
        lambda i, index: (i, 0, 0),
        jax.ShapeDtypeStruct((blocks * own_rows, columns), parts[0].dtype),
        (own_rows, columns),
        lambda i, index: (i, 0),
    )


def full_grad(parts, own_rows, groups):
    blocks, size, columns = parts[0].shape
    width = columns // groups
    return place(
        place_rows,
        parts,
        (groups, blocks),
        (1, size, width),
        lambda g, i, index: (i, 0, g),
        jax.ShapeDtypeStruct((own_rows, groups * blocks * width), F32),
        (own_rows, width),
        lambda g, i, index: (0, g * blocks + i),
    )


def full_columns(parts, first, count, block):
    size = parts[0].shape[1]
    return place(
        place_columns,
        parts,
        (count // block,),
        (block, size),
        lambda i, index: (i + first // block, 0),
        jax.ShapeDtypeStruct((count, 4 * size), F32),
        (block, 4 * size),
        lambda i, index: (i, 0),
    )


def rotary_lanes(positions):
    half = ROT // 2
    lane = jnp.arange(LANES, dtype=jnp.int32) % HEAD
    frequency = ROPE_BASE ** (-((lane % half).astype(F32) * 2.0 / ROT))
    angles = positions.astype(F32)[:, None] * frequency
    sine = jnp.sin(angles)
    return (
        jnp.where(lane < ROT, jnp.cos(angles), 1.0),
        jnp.where(lane < half, -sine, 0.0),
        jnp.where((lane >= half) & (lane < ROT), sine, 0.0),
    )


def turn(value, cosine, above, below, sign):
    half = ROT // 2
    size = value.shape[1]
    from_above = pltpu.roll(value, size - half, 1)
    from_below = pltpu.roll(value, half, 1)
    return value * cosine + sign * (from_above * above + from_below * below)


def nt(left, right):
    return lax.dot_general(left, right, (((1,), (1,)), ((), ())), preferred_element_type=F32)


def nn(left, right):
    return lax.dot_general(left, right, (((1,), (0,)), ((), ())), preferred_element_type=F32)


def pair_of(head):
    return slice(head // 2 * LANES, head // 2 * LANES + LANES)


def only(value, head):
    lane = lax.broadcasted_iota(jnp.int32, value.shape, 1)
    return jnp.where((lane // HEAD) == head % 2, value, jnp.zeros_like(value))


def fold(value, op):
    out = value[:, :LANES]
    for start in range(LANES, value.shape[1], LANES):
        out = op(out, value[:, start : start + LANES])
    return out


def attend_kernel(
    heads, scale, joined, bias, cosine, above, below,
    q_out, k_out, v_out, mixed_out, low_out, log_out, max_out,
    k_all, v_all, scores, total,
):
    step = pl.program_id(0)
    block, own = q_out.shape
    copies = own // LANES
    tables = [jnp.concatenate([t[...]] * copies, axis=1) for t in (cosine, above, below)]
    q = turn(joined[:, :own] + bias[:, :own], *tables, 1.0).astype(BF16)
    k = turn(joined[:, own : 2 * own] + bias[:, own : 2 * own], *tables, 1.0).astype(BF16)
    v = (joined[:, 2 * own :] + bias[:, 2 * own :]).astype(BF16)
    q_out[...] = q
    k_out[...] = k
    v_out[...] = v
    here = pl.ds(pl.multiple_of(step * block, block), block)
    k_all[here, :] = k
    v_all[here, :] = v
    queries = [only(q[:, pair_of(h)], h) * jnp.asarray(scale, BF16) for h in range(heads)]
    allowed = lax.broadcasted_iota(jnp.int32, (block, block), 0) >= lax.broadcasted_iota(
        jnp.int32, (block, block), 1
    )

    def score(j, peaks, diagonal):
        spot = pl.ds(pl.multiple_of(j * block, block), block)
        out = []
        for h in range(heads):
            s = nt(queries[h], k_all[spot, pair_of(h)])
            if diagonal:
                s = jnp.where(allowed, s, MASKED)
            scores[h, :, spot] = s
            out.append(jnp.maximum(peaks[h], fold(s, jnp.maximum)))
        return out

    peaks = [jnp.full((block, LANES), MASKED, F32)] * heads
    peaks = lax.fori_loop(0, step, lambda j, c: score(j, c, False), peaks)
    peaks = score(step, peaks, True)
    peaks = [jnp.max(p, axis=1, keepdims=True) for p in peaks]
    total[...] = jnp.zeros_like(total)

    def gather(j, sums):
        spot = pl.ds(pl.multiple_of(j * block, block), block)
        out = []
        for h in range(heads):
            p = jnp.exp(scores[h, :, spot] - peaks[h])
            out.append(sums[h] + fold(p, jnp.add))
            total[h] += nn(p.astype(BF16), v_all[spot, pair_of(h)])
        return out

    sums = lax.fori_loop(0, step + 1, gather, [jnp.zeros((block, LANES), F32)] * heads)
    lane = lax.broadcasted_iota(jnp.int32, (block, LANES), 1)
    logs = jnp.zeros((block, LANES), F32)
    tops = jnp.full((1, LANES), MASKED, F32)
    for h in range(heads):
        amount = jnp.sum(sums[h], axis=1, keepdims=True)
        total[h] = total[h] / amount
        logs = jnp.where(lane == h, peaks[h] + jnp.log(amount), logs)
        tops = jnp.where(lane[:1] == h, jnp.max(peaks[h], axis=0, keepdims=True), tops)
    log_out[...] = logs
    for h in range(0, heads, 2):
        mixed = jnp.where(lane < HEAD, total[h], total[h + 1])
        mixed_out[:, pair_of(h)] = mixed
        low_out[:, pair_of(h)] = mixed.astype(BF16)

    @pl.when(step == 0)
    def _():
        max_out[...] = tops

    @pl.when(step > 0)
    def _():
        max_out[...] = jnp.maximum(max_out[...], tops)


def attend(joined, bias, tables, heads, scale, block):
    length = joined.shape[0]
    own = joined.shape[1] // 3
    row = lambda i: (i, 0)
    zero = lambda i: (0, 0)
    shapes = [
        ((length, own), BF16), ((length, own), BF16), ((length, own), BF16),
        ((length, own), F32), ((length, own), BF16), ((length, LANES), F32),
    ]
    pairs = heads * length * length // 2
    return pl.pallas_call(
        partial(attend_kernel, heads, scale),
        name="attend",
        out_shape=[jax.ShapeDtypeStruct(s, d) for s, d in shapes]
        + [jax.ShapeDtypeStruct((1, LANES), F32)],
        grid_spec=pltpu.PrefetchScalarGridSpec(
            num_scalar_prefetch=0,
            grid=(length // block,),
            in_specs=[pl.BlockSpec((block, 3 * own), row), pl.BlockSpec((1, 3 * own), zero)]
            + [pl.BlockSpec((block, LANES), row)] * 3,
            out_specs=[pl.BlockSpec((block, s[1]), row) for s, d in shapes]
            + [pl.BlockSpec((1, LANES), zero)],
            scratch_shapes=[
                pltpu.VMEM((length, own), BF16),
                pltpu.VMEM((length, own), BF16),
                pltpu.VMEM((heads, block, length), F32),
                pltpu.VMEM((heads, block, LANES), F32),
            ],
        ),
        compiler_params=pltpu.CompilerParams(vmem_limit_bytes=40 << 20),
        cost_estimate=pl.CostEstimate(
            flops=4 * pairs * 2 * LANES, transcendentals=pairs, bytes_accessed=length * own * 26
        ),
    )(joined, bias, *tables)


def attend_back_kernel(
    heads, scale, q, k, v, k_here, grad, mixed, logs, cosine, above, below,
    low_out, sum_out, k_turned, k_total, v_total, q_total,
):
    step = pl.program_id(0)
    block, own = q.shape
    length = k.shape[0]
    copies = own // LANES
    spot_here = pl.ds(pl.multiple_of(step * block, block), block)

    @pl.when(step == 0)
    def _():
        k_total[...] = jnp.zeros_like(k_total)
        v_total[...] = jnp.zeros_like(v_total)

    k_turned[:, spot_here] = k_here[...].T
    q_total[...] = jnp.zeros_like(q_total)
    log_rows = logs[...].T
    product = grad[...].astype(F32) * mixed[...]
    lane = lax.broadcasted_iota(jnp.int32, (block, LANES), 1)
    deltas = jnp.zeros((block, LANES), F32)
    for h in range(heads):
        own_sum = jnp.sum(only(product[:, pair_of(h)], h), axis=1, keepdims=True)
        deltas = jnp.where(lane == h, own_sum, deltas)
    delta_rows = deltas.T
    queries = [only(q[:, pair_of(h)], h) * jnp.asarray(scale, BF16) for h in range(heads)]
    grads = [only(grad[:, pair_of(h)], h) for h in range(heads)]
    allowed = lax.broadcasted_iota(jnp.int32, (block, block), 0) <= lax.broadcasted_iota(
        jnp.int32, (block, block), 1
    )

    def visit(j, diagonal):
        spot = pl.ds(pl.multiple_of(j * block, block), block)
        for h in range(heads):
            s = nt(k[spot, pair_of(h)], queries[h])
            if diagonal:
                s = jnp.where(allowed, s, MASKED)
            p = jnp.exp(s - log_rows[h : h + 1])
            dp = nt(v[spot, pair_of(h)], grads[h])
            ds = (p * (dp - delta_rows[h : h + 1])).astype(BF16)
            v_total[spot, pair_of(h)] += nn(p.astype(BF16), grads[h])
            k_total[spot, pair_of(h)] += nn(ds, queries[h])
            q_total[h] += nn(k_turned[pair_of(h), spot], ds)

    def body(j, carry):
        visit(j, False)
        return carry

    lax.fori_loop(0, step, body, 0)
    visit(step, True)
    row = lax.broadcasted_iota(jnp.int32, (LANES, block), 0)
    tables = (cosine[spot_here, :], above[spot_here, :], below[spot_here, :])
    sums = []
    for h in range(0, heads, 2):
        dq = jnp.where(row < HEAD, q_total[h], q_total[h + 1]).T * scale
        low = turn(dq, *tables, -1.0).astype(BF16)
        low_out[spot_here, pair_of(h)] = low
        sums.append(jnp.sum(low.astype(F32), axis=0, keepdims=True))
    sums = jnp.concatenate(sums, axis=1)

    @pl.when(step == 0)
    def _():
        sum_out[:, :own] = sums

    @pl.when(step > 0)
    def _():
        sum_out[:, :own] += sums

    @pl.when(step == length // block - 1)
    def _():
        wide = [jnp.concatenate([t[...]] * copies, axis=1) for t in (cosine, above, below)]
        low = turn(k_total[...], *wide, -1.0).astype(BF16)
        low_out[:, own : 2 * own] = low
        sum_out[:, own : 2 * own] = jnp.sum(low.astype(F32), axis=0, keepdims=True)
        low = v_total[...].astype(BF16)
        low_out[:, 2 * own :] = low
        sum_out[:, 2 * own :] = jnp.sum(low.astype(F32), axis=0, keepdims=True)


def attend_back(q, k, v, grad, mixed, logs, tables, heads, scale, block):
    length, own = q.shape
    row = lambda i: (i, 0)
    zero = lambda i: (0, 0)
    rows = pl.BlockSpec((block, own), row)
    whole = pl.BlockSpec((length, own), zero)
    pairs = heads * length * length // 2
    return pl.pallas_call(
        partial(attend_back_kernel, heads, scale),
        name="attend_back",
        out_shape=[
            jax.ShapeDtypeStruct((length, 3 * own), BF16),
            jax.ShapeDtypeStruct((1, 3 * own), F32),
        ],
        grid_spec=pltpu.PrefetchScalarGridSpec(
            num_scalar_prefetch=0,
            grid=(length // block,),
            in_specs=[rows, whole, whole, rows, rows, rows, pl.BlockSpec((block, LANES), row)]
            + [pl.BlockSpec((length, LANES), zero)] * 3,
            out_specs=[
                pl.BlockSpec((length, 3 * own), zero),
                pl.BlockSpec((1, 3 * own), zero),
            ],
            scratch_shapes=[
                pltpu.VMEM((own, length), BF16),
                pltpu.VMEM((length, own), F32),
                pltpu.VMEM((length, own), F32),
                pltpu.VMEM((heads, LANES, block), F32),
            ],
        ),
        compiler_params=pltpu.CompilerParams(vmem_limit_bytes=40 << 20),
        cost_estimate=pl.CostEstimate(
            flops=10 * pairs * 2 * LANES, transcendentals=pairs, bytes_accessed=length * own * 20
        ),
    )(q, k, v, k, grad, mixed, logs, *tables)


def to_columns(rows, groups):
    parts = lax.axis_size("ctx")
    count, columns = rows.shape
    width = columns // (groups * parts)
    return (
        rows.reshape(count, groups, parts, width)
        .transpose(2, 0, 1, 3)
        .reshape(parts, count, groups * width)
    )


def exchange(blocks):
    return lax.all_to_all(blocks, "ctx", split_axis=0, concat_axis=0, tiled=True)


def gather_weights(qkv_weight, up_weight):
    own_rows = qkv_weight.shape[0]
    if lax.axis_size("dp") != 4:
        q, u = exchange(to_columns(qkv_weight, 3)), exchange(to_columns(up_weight, 1))
        return q.reshape(-1, q.shape[2]), u.reshape(-1, u.shape[2])
    q = to_columns(my_part(qkv_weight, 0), 3)
    u = to_columns(my_part(up_weight, 0), 1)
    q = exchange(q)
    q, u = lax.optimization_barrier((q, u))
    q_near = along_both((q, q))
    u = exchange(u)
    q_near, u = lax.optimization_barrier((q_near, u))
    u_near = along_both((u, u))
    q_far = along_both(forwarded(q_near, 1))
    q_far, u_near = lax.optimization_barrier((q_far, u_near))
    u_far = along_both(forwarded(u_near, 1))
    return (
        full_rows(four_parts(q, q_near, q_far, 1), own_rows),
        full_rows(four_parts(u, u_near, u_far, 1), own_rows),
    )


def reduce_input_grad(grad, own_rows, groups):
    grad = grad.reshape(lax.axis_size("ctx"), own_rows, grad.shape[1])
    part = exchange(lax.psum_scatter(grad, "dp", scatter_dimension=1, tiled=True))
    rows = lax.all_gather(part, "dp", axis=1, tiled=True)
    return (
        rows.reshape(rows.shape[0], own_rows, groups, -1)
        .transpose(1, 2, 0, 3)
        .reshape(own_rows, -1)
        .astype(F32)
    )


def per_device(
    tokens,
    positions,
    norm_gain,
    norm_bias,
    qkv_weight,
    qkv_bias,
    dense_weight,
    dense_bias,
    up_weight,
    up_bias,
    down_weight,
    down_bias,
    clip_limit,
    cotangent,
):
    seqs, stretch, width = tokens.shape
    heads = clip_limit.shape[0]
    head_dim = width // heads
    rows = seqs * stretch
    parts = lax.axis_size("ctx")
    part = lax.axis_index("ctx")
    own_heads = heads // parts
    own = own_heads * head_dim
    own_rows = qkv_weight.shape[0]
    own_ff = down_weight.shape[0]
    length = stretch * parts
    count = seqs * length
    scale = head_dim ** (-0.5)

    inputs = tokens.reshape(rows, width).astype(F32)
    centre = inputs - jnp.mean(inputs, axis=-1, keepdims=True)
    inv_std = lax.rsqrt(jnp.mean(centre * centre, axis=-1, keepdims=True) + EPSILON)
    normed = centre * inv_std
    hidden_local = (normed * norm_gain + norm_bias).astype(BF16)
    hidden = lax.all_gather(
        hidden_local.reshape(seqs, stretch, width), "ctx", axis=1, tiled=True
    ).reshape(count, width)
    grad_rows = lax.all_gather(cotangent, "ctx", axis=1, tiled=True).reshape(count, width)
    qkv_columns, up_columns = gather_weights(qkv_weight, up_weight)
    positions_all = all_rows(positions.T, "ctx").T

    qkv_own_bias = take(qkv_bias.reshape(3, parts, own), part, 1, 1).reshape(1, 3 * own)
    up_own_bias = take(up_bias, part * own_ff, own_ff, 0)

    joined = dot(hidden, qkv_columns, (1, 0))
    block = 256 if length % 256 == 0 else length
    tables = [rotary_lanes(positions_all[s]) for s in range(seqs)]
    ahead = [
        attend(
            joined[s * length : (s + 1) * length], qkv_own_bias, tables[s], own_heads, scale, block
        )
        for s in range(seqs)
    ]
    attended = jnp.concatenate([a[4] for a in ahead])
    own_maxima = jnp.max(jnp.stack([a[6][0, :own_heads] for a in ahead]), axis=0)
    upward = dot(hidden, up_columns, (1, 0)) + up_own_bias
    activated, gelu_back = jax.vjp(partial(jax.nn.gelu, approximate=True), upward)
    activated = activated.astype(BF16)

    def feed_forward_back(grad_rows):
        act_grad = dot(grad_rows, down_weight, (1, 1))
        up_low = gelu_back(act_grad)[0].astype(BF16)
        return up_low, dot(hidden, up_low, (0, 0)).astype(BF16)

    def attention_back(grad_rows):
        mixed_low = dot(grad_rows, dense_weight, (1, 1)).astype(BF16)
        back = [
            attend_back(
                q, k, v, mixed_low[s * length : (s + 1) * length], mixed, logs, tables[s],
                own_heads, scale, block,
            )
            for s, (q, k, v, mixed, low, logs, tops) in enumerate(ahead)
        ]
        joined_low = jnp.concatenate([b[0] for b in back])
        qkv_raw = dot(hidden, joined_low, (0, 0)).astype(BF16)
        return joined_low, sum(b[1] for b in back), qkv_raw

    def sum_branch(value):
        return lax.psum_scatter(
            value.astype(BF16).reshape(seqs, length, width),
            "ctx",
            scatter_dimension=1,
            tiled=True,
        ).reshape(rows, width)

    def output_part(mixed_out):
        return sum_branch(dot(mixed_out, jnp.concatenate([dense_weight, down_weight]), (1, 0)))

    def input_part(joined_low, up_low):
        return sum_branch(
            dot(joined_low, qkv_columns, (1, 1)) + dot(up_low, up_columns, (1, 1))
        )

    grad_rows, attended, activated = lax.optimization_barrier((grad_rows, attended, activated))
    mixed_out = jnp.concatenate([attended, activated], axis=1)
    out_raw = dot(mixed_out, grad_rows, (0, 0)).astype(BF16)
    if lax.axis_size("dp") == 4:
        o_send = outgoing(out_raw, 1)
        o_got = along_both(o_send)
        up_low, up_raw = feed_forward_back(after(grad_rows, o_send))
        up_raw = up_raw.reshape(parts, own_rows, own_ff)
        u_send = outgoing(up_raw, 1)
        u_got = along_both(u_send)
        joined_low, joined_sum, qkv_raw = attention_back(after(grad_rows, u_send))
        qkv_raw = qkv_raw.reshape(parts, own_rows, 3 * own)
        q_send = outgoing(qkv_raw, 1)
        q_got = along_both(q_send)
        o_sums = first_sums(out_raw, after(o_got, q_send), 1)
        o_send = outgoing_again(o_sums, 1)
        o_got = along_both(o_send)
        branch_sum = output_part(after(mixed_out, o_send))
        u_sums = first_sums(up_raw, after(u_got, o_send), 1)
        u_send = outgoing_again(u_sums, 1)
        u_got = along_both(u_send)
        hidden_grad = input_part(after(joined_low, u_send), up_low)
        q_sums = first_sums(qkv_raw, after(q_got, u_send), 1)
        q_send = outgoing_again(q_sums, 1)
        q_got = along_both(q_send)
        o_part = second_sums(o_sums, after(o_got, q_send), 1)
        o_near = along_both((o_part, o_part))
        u_part = exchange(second_sums(u_sums, after(u_got, o_part), 1))
        q_part = exchange(second_sums(q_sums, after(q_got, u_part), 1))
        u_near = along_both((u_part, u_part))
        o_far = along_both(forwarded(after(o_near, u_part), 1))
        q_near = along_both((q_part, q_part))
        u_far = along_both(forwarded(after(u_near, q_part), 1))
        q_far = along_both(forwarded(q_near, 1))
        o_parts = four_parts(o_part, o_near, o_far, 1)
        dense_grad = full_columns(o_parts, 0, own, own)
        down_grad = full_columns(o_parts, own, own_ff, own)
        up_grad = full_grad(four_parts(u_part, u_near, u_far, 1), own_rows, 1)
        qkv_grad = full_grad(four_parts(q_part, q_near, q_far, 1), own_rows, 3)
    else:
        up_low, up_raw = feed_forward_back(grad_rows)
        joined_low, joined_sum, qkv_raw = attention_back(grad_rows)
        branch_sum = output_part(mixed_out)
        hidden_grad = input_part(joined_low, up_low)
        out_grad = lax.psum(out_raw, "dp").astype(F32)
        dense_grad, down_grad = out_grad[:own], out_grad[own:]
        up_grad = reduce_input_grad(up_raw, own_rows, 1)
        qkv_grad = reduce_input_grad(qkv_raw, own_rows, 3)
        o_part = out_grad
    layer_out = (inputs + branch_sum.astype(F32) + dense_bias + down_bias).astype(BF16)
    hidden_grad = hidden_grad.astype(F32)
    gain_part = jnp.sum(hidden_grad * normed, axis=0)
    shift_part = jnp.sum(hidden_grad, axis=0)
    scaled = hidden_grad * norm_gain
    tokens_grad = cotangent.reshape(rows, width).astype(F32) + inv_std * (
        scaled
        - jnp.mean(scaled, axis=-1, keepdims=True)
        - normed * jnp.mean(scaled * normed, axis=-1, keepdims=True)
    )
    norm_sums = all_sum(jnp.stack([gain_part, shift_part]), ("dp", "ctx"))

    sums = jnp.concatenate(
        [
            joined_sum[0],
            jnp.sum(up_low.astype(F32), axis=0),
            jnp.sum(take(grad_rows, part * own, own, 1).astype(F32), axis=0),
        ]
    )[None]
    sums, own_maxima = after((sums, own_maxima), o_part)
    maxima = own_maxima[None]
    for bit in bits_of("dp"):
        both = swap(jnp.concatenate([sums, maxima], axis=1), "dp", bit)
        sums = sums + both[:, : sums.shape[1]]
        maxima = jnp.maximum(maxima, both[:, sums.shape[1] :])
    both = all_rows(jnp.concatenate([sums, maxima], axis=1), "ctx")
    cut = 3 * own + own_ff
    qkv_bias_grad = (
        both[:, : 3 * own].reshape(parts, 3, own).transpose(1, 0, 2).reshape(3 * width)
    )
    up_bias_grad = both[:, 3 * own : cut].reshape(parts * own_ff)
    out_bias_grad = both[:, cut : cut + own].reshape(width)
    head_maxima = both[:, cut + own :].reshape(heads)

    limits = clip_limit.astype(F32)
    factor = limits / jnp.maximum(head_maxima, limits)
    column_scale = jnp.tile(jnp.repeat(jnp.sqrt(factor), head_dim), 2)
    clipped_weight = qkv_weight[:, : 2 * width].astype(F32) * column_scale
    clipped_bias = qkv_bias[: 2 * width] * column_scale
    return (
        layer_out.reshape(seqs, stretch, width),
        tokens_grad.reshape(seqs, stretch, width),
        norm_sums[0],
        norm_sums[1],
        qkv_grad,
        qkv_bias_grad,
        dense_grad,
        out_bias_grad,
        up_grad,
        up_bias_grad,
        down_grad,
        out_bias_grad,
        head_maxima,
        clipped_weight,
        clipped_bias,
    )


def solution(mesh):
    rows = P("dp", "ctx", None)
    weight = P("ctx", None)
    in_specs = (rows, P("dp", "ctx"), P(), P()) + (weight, P()) * 4 + (P(), rows)
    out_specs = (
        (rows, rows, P(), P()) + (weight, P()) * 4 + (P(), weight, P())
    )
    return jax.shard_map(
        per_device, mesh=mesh, in_specs=in_specs, out_specs=out_specs, check_vma=False
    )
```

```python
from functools import partial

import jax
import jax.numpy as jnp
from jax import lax
from jax.experimental import pallas as pl
from jax.experimental.pallas import tpu as pltpu
from jax.sharding import PartitionSpec as P

ROT = 32
EPSILON = 1e-05
MASKED = -1e30
ROPE_BASE = 10000.0
BF16 = jnp.bfloat16
F32 = jnp.float32
LANES = 128
HEAD = 64
VMEM = 40 << 20
LIGHT = pl.CostEstimate(flops=1, transcendentals=0, bytes_accessed=1)


def dot(left, right, contract):
    return lax.dot_general(
        left, right, ((contract[:1], contract[1:]), ((), ())), preferred_element_type=F32
    )


def swap(value, axis, bit):
    return lax.ppermute(value, axis, [(i, i ^ bit) for i in range(lax.axis_size(axis))])


def take(value, start, size, axis):
    return lax.dynamic_slice_in_dim(value, start, size, axis)


def first_place(index):
    return (index & 1) * 2 + (index >> 1)


def my_part(value, axis):
    index = lax.axis_index("dp")
    size = value.shape[axis] // 8
    return jnp.concatenate(
        [
            take(value, first_place(index) * size, size, axis),
            take(value, (4 + index) * size, size, axis),
        ],
        axis,
    )


def after(value, *others):
    return lax.optimization_barrier((value, others))[0]


def along_both(pair):
    return swap(pair[0], "dp", 1), swap(pair[1], "dp", 2)


def plus(left, right):
    return (left.astype(F32) + right.astype(F32)).astype(BF16)


def outgoing(value, axis):
    index = lax.axis_index("dp")
    size = value.shape[axis] // 8
    return (
        take(value, (1 - (index & 1)) * 2 * size, 2 * size, axis),
        take(value, (4 + (1 - (index >> 1)) * 2) * size, 2 * size, axis),
    )


def dp_index():
    return lax.axis_index("dp").astype(jnp.int32).reshape(1)


def first_sums(value, received, axis):
    index = lax.axis_index("dp")
    low, high = index & 1, index >> 1
    size = value.shape[axis] // 8
    first = plus(take(value, low * 2 * size, 2 * size, axis), received[0])
    second = plus(take(value, (4 + high * 2) * size, 2 * size, axis), received[1])
    send = (
        take(second, (1 - low) * size, size, axis),
        take(first, (1 - high) * size, size, axis),
    )
    keep = jnp.concatenate(
        [take(first, high * size, size, axis), take(second, low * size, size, axis)], axis
    )
    return send, keep


def second_sums(keep, received, axis):
    return plus(keep, jnp.concatenate([received[1], received[0]], axis))


def normalize_kernel(tokens, gain, shift, hidden, stats):
    value = tokens[...].astype(F32)
    mean = jnp.mean(value, axis=1, keepdims=True)
    centre = value - mean
    inv_std = lax.rsqrt(jnp.mean(centre * centre, axis=1, keepdims=True) + EPSILON)
    hidden[...] = (centre * inv_std * gain[...] + shift[...]).astype(BF16)
    lane = lax.broadcasted_iota(jnp.int32, stats.shape, 1)
    stats[...] = jnp.where(lane == 0, mean, inv_std)


def normalize(tokens, gain, shift):
    count, width = tokens.shape[0], gain.shape[0]
    block = 256 if count % 256 == 0 else count
    row = lambda i: (i, 0)
    return pl.pallas_call(
        normalize_kernel,
        name="normalize",
        out_shape=[
            jax.ShapeDtypeStruct((count, width), BF16),
            jax.ShapeDtypeStruct((count, LANES), F32),
        ],
        grid=(count // block,),
        in_specs=[pl.BlockSpec((block, width), row)]
        + [pl.BlockSpec((1, width), lambda i: (0, 0))] * 2,
        out_specs=[pl.BlockSpec((block, width), row), pl.BlockSpec((block, LANES), row)],
        compiler_params=pltpu.CompilerParams(vmem_limit_bytes=VMEM),
        cost_estimate=LIGHT,
    )(tokens, gain[None], shift[None])


def output_kernel(attended, dense, activated, down, out):
    out[...] = (nn(attended[...], dense[...]) + nn(activated[...], down[...])).astype(BF16)


def output_part(attended, dense, activated, down):
    count, width = attended.shape[0], dense.shape[1]
    block = 256
    fixed = lambda i: (0, 0)
    column = lambda i: (0, i)
    return pl.pallas_call(
        output_kernel,
        name="output_part",
        out_shape=jax.ShapeDtypeStruct((count, width), BF16),
        grid=(width // block,),
        in_specs=[
            pl.BlockSpec(attended.shape, fixed),
            pl.BlockSpec((dense.shape[0], block), column),
            pl.BlockSpec(activated.shape, fixed),
            pl.BlockSpec((down.shape[0], block), column),
        ],
        out_specs=pl.BlockSpec((count, block), column),
        compiler_params=pltpu.CompilerParams(vmem_limit_bytes=VMEM),
        cost_estimate=LIGHT,
    )(attended, dense, activated, down)


def input_kernel(joined, qkv, upward, up, tokens, stats, out, sums):
    total = nt(joined[...], qkv[...]) + nt(upward[...], up[...])
    out[...] = total.astype(BF16)
    xhat = (tokens[...].astype(F32) - stats[:, 0:1]) * stats[:, 1:2]
    sums[0:1, :] = jnp.sum(total * xhat, axis=0, keepdims=True)
    sums[1:2, :] = jnp.sum(total, axis=0, keepdims=True)


def input_part(joined, qkv, upward, up, tokens, stats):
    count, width = tokens.shape[0], qkv.shape[0]
    block = 256
    fixed = lambda i: (0, 0)
    column = lambda i: (0, i)
    row = lambda i: (i, 0)
    return pl.pallas_call(
        input_kernel,
        name="input_part",
        out_shape=[
            jax.ShapeDtypeStruct((count, width), BF16),
            jax.ShapeDtypeStruct((2, width), F32),
        ],
        grid=(width // block,),
        in_specs=[
            pl.BlockSpec(joined.shape, fixed),
            pl.BlockSpec((block, qkv.shape[1]), row),
            pl.BlockSpec(upward.shape, fixed),
            pl.BlockSpec((block, up.shape[1]), row),
            pl.BlockSpec((count, block), column),
            pl.BlockSpec(stats.shape, fixed),
        ],
        out_specs=[pl.BlockSpec((count, block), column), pl.BlockSpec((2, block), column)],
        compiler_params=pltpu.CompilerParams(vmem_limit_bytes=VMEM),
        cost_estimate=LIGHT,
    )(joined, qkv, upward, up, tokens, stats)


def finish_kernel(tokens, cotangent, branch, grad, gain, bias, out, tokens_grad):
    value = tokens[...].astype(F32)
    out[...] = (value + branch[...].astype(F32) + bias[...]).astype(BF16)
    centre = value - jnp.mean(value, axis=1, keepdims=True)
    inv_std = lax.rsqrt(jnp.mean(centre * centre, axis=1, keepdims=True) + EPSILON)
    xhat = centre * inv_std
    scaled = grad[...].astype(F32) * gain[...]
    inner = jnp.mean(scaled * xhat, axis=1, keepdims=True)
    scaled = scaled - jnp.mean(scaled, axis=1, keepdims=True) - xhat * inner
    tokens_grad[...] = cotangent[...].astype(F32) + inv_std * scaled


def finish(tokens, cotangent, branch, grad, gain, bias):
    rows, width = tokens.shape
    block = 64 if rows % 64 == 0 else rows
    row = pl.BlockSpec((block, width), lambda i: (i, 0))
    vector = pl.BlockSpec((1, width), lambda i: (0, 0))
    return pl.pallas_call(
        finish_kernel,
        name="finish",
        out_shape=[
            jax.ShapeDtypeStruct((rows, width), BF16),
            jax.ShapeDtypeStruct((rows, width), F32),
        ],
        grid=(rows // block,),
        in_specs=[row] * 4 + [vector] * 2,
        out_specs=[row, row],
        compiler_params=pltpu.CompilerParams(vmem_limit_bytes=VMEM),
        cost_estimate=LIGHT,
    )(tokens, cotangent, branch, grad, gain[None], bias[None])


def clip_kernel(heads, head_dim, maxima, limits, weight, bias, out, bias_out):
    first = lax.rem(pl.program_id(0) * (out.shape[1] // head_dim), heads)
    factor = limits[...] / jnp.maximum(maxima[...], limits[...])
    lane = lax.broadcasted_iota(jnp.int32, (1, heads), 1)
    head = first + lax.broadcasted_iota(jnp.int32, (1, out.shape[1]), 1) // head_dim
    scale = jnp.zeros((1, out.shape[1]), F32)
    for h in range(heads):
        one = jnp.sum(jnp.where(lane == h, factor, 0.0), axis=1, keepdims=True)
        scale = jnp.where(head == h, jnp.sqrt(one), scale)
    out[...] = weight[...].astype(F32) * scale
    bias_out[...] = bias[...] * scale


def clip_columns(weight, bias, maxima, limits, head_dim):
    rows, heads = weight.shape[0], maxima.shape[0]
    columns = 2 * heads * head_dim
    block = heads * head_dim // 2
    column = lambda i: (0, i)
    vector = pl.BlockSpec((1, heads), lambda i: (0, 0))
    wide, thin = pl.BlockSpec((rows, block), column), pl.BlockSpec((1, block), column)
    out, bias_out = pl.pallas_call(
        partial(clip_kernel, heads, head_dim),
        name="clip_columns",
        out_shape=[
            jax.ShapeDtypeStruct((rows, columns), F32),
            jax.ShapeDtypeStruct((1, columns), F32),
        ],
        grid=(columns // block,),
        in_specs=[vector, vector, wide, thin],
        out_specs=[wide, thin],
        compiler_params=pltpu.CompilerParams(vmem_limit_bytes=VMEM),
        cost_estimate=LIGHT,
    )(maxima[None], limits.astype(F32)[None], weight, bias[None])
    return out, bias_out[0]


def forwarded(received, axis):
    half = received[0].shape[axis] // 2
    return (
        lax.slice_in_dim(received[1], 0, half, axis=axis),
        lax.slice_in_dim(received[0], half, 2 * half, axis=axis),
    )


def four_parts(part, near, far):
    return [part, near[0], near[1], far[0], far[1]]


def pieces_of(index_ref, refs, eighth, axis):
    me = index_ref[0]
    first = (slice(None),) * axis + (slice(0, eighth),)
    second = (slice(None),) * axis + (slice(eighth, 2 * eighth),)
    for offset in range(3):
        owner = me ^ offset
        yield first_place(owner), refs[offset], first
        yield 4 + owner, refs[offset], second
    owner = me ^ 3
    yield first_place(owner), refs[3], first
    yield 4 + owner, refs[4], first


def place_rows(index_ref, *refs):
    out = refs[-1]
    blocks, size, width = refs[0].shape
    for spot, ref, cut in pieces_of(index_ref, refs, size // 2, 1):
        rows = pl.ds(pl.multiple_of(spot * (size // 2), size // 2), size // 2)
        for i in range(blocks):
            out[rows, i * width : (i + 1) * width] = ref[(i,) + cut[1:]].astype(out.dtype)


def place_columns(index_ref, *refs):
    out = refs[-1]
    eighth = refs[0].shape[1] // 2
    for spot, ref, cut in pieces_of(index_ref, refs, eighth, 1):
        columns = pl.ds(pl.multiple_of(spot * eighth, eighth), eighth)
        out[:, columns] = ref[cut].astype(out.dtype)


def place(body, parts, axis, grid, in_block, in_map, out_shape, out_block, out_map):
    half = list(in_block)
    half[axis] //= 2
    return pl.pallas_call(
        body,
        out_shape=out_shape,
        grid_spec=pltpu.PrefetchScalarGridSpec(
            num_scalar_prefetch=1,
            grid=grid,
            in_specs=[pl.BlockSpec(in_block, in_map)] * 3
            + [pl.BlockSpec(tuple(half), in_map)] * 2,
            out_specs=pl.BlockSpec(out_block, out_map),
        ),
        compiler_params=pltpu.CompilerParams(vmem_limit_bytes=VMEM),
        cost_estimate=LIGHT,
    )(dp_index(), *parts)


def full_rows(parts, own_rows):
    blocks, size, columns = parts[0].shape
    return place(
        place_rows,
        parts,
        1,
        (blocks,),
        (1, size, columns),
        lambda i, index: (i, 0, 0),
        jax.ShapeDtypeStruct((blocks * own_rows, columns), parts[0].dtype),
        (own_rows, columns),
        lambda i, index: (i, 0),
    )


def full_grad(parts, own_rows, groups):
    blocks, size, columns = parts[0].shape
    width = columns // groups
    several = max(1, min(blocks, 1024 // width))
    steps = blocks // several
    return place(
        place_rows,
        parts,
        1,
        (groups, steps),
        (several, size, width),
        lambda g, i, index: (i, 0, g),
        jax.ShapeDtypeStruct((own_rows, groups * blocks * width), F32),
        (own_rows, several * width),
        lambda g, i, index: (0, g * steps + i),
    )


def full_columns(parts, first, count, block):
    size = parts[0].shape[1]
    return place(
        place_columns,
        parts,
        1,
        (count // block,),
        (block, size),
        lambda i, index: (i + first // block, 0),
        jax.ShapeDtypeStruct((count, 4 * size), F32),
        (block, 4 * size),
        lambda i, index: (i, 0),
    )


def rotary_lanes(positions):
    half = ROT // 2
    lane = jnp.arange(LANES, dtype=jnp.int32) % HEAD
    frequency = ROPE_BASE ** (-((lane % half).astype(F32) * 2.0 / ROT))
    angles = positions.astype(F32)[:, None] * frequency
    sine = jnp.sin(angles)
    return (
        jnp.where(lane < ROT, jnp.cos(angles), 1.0),
        jnp.where(lane < half, -sine, 0.0),
        jnp.where((lane >= half) & (lane < ROT), sine, 0.0),
    )


def turn(value, cosine, above, below, sign):
    half = ROT // 2
    size = value.shape[1]
    from_above = pltpu.roll(value, size - half, 1)
    from_below = pltpu.roll(value, half, 1)
    return value * cosine + sign * (from_above * above + from_below * below)


def nt(left, right):
    return lax.dot_general(left, right, (((1,), (1,)), ((), ())), preferred_element_type=F32)


def nn(left, right):
    return lax.dot_general(left, right, (((1,), (0,)), ((), ())), preferred_element_type=F32)


def pair_of(head):
    return slice(head // 2 * LANES, head // 2 * LANES + LANES)


def only(value, head):
    lane = lax.broadcasted_iota(jnp.int32, value.shape, 1)
    return jnp.where((lane // HEAD) == head % 2, value, jnp.zeros_like(value))


def fold(value, op):
    out = value[:, :LANES]
    for start in range(LANES, value.shape[1], LANES):
        out = op(out, value[:, start : start + LANES])
    return out


def attend_kernel(
    heads, scale, joined, bias, cosine, above, below,
    q_out, k_out, v_out, mixed_out, low_out, log_out, max_out,
    k_all, v_all, scores, total,
):
    step = pl.program_id(0)
    block, own = q_out.shape
    copies = own // LANES
    tables = [jnp.concatenate([t[...]] * copies, axis=1) for t in (cosine, above, below)]
    q = turn(joined[:, :own] + bias[:, :own], *tables, 1.0).astype(BF16)
    k = turn(joined[:, own : 2 * own] + bias[:, own : 2 * own], *tables, 1.0).astype(BF16)
    v = (joined[:, 2 * own :] + bias[:, 2 * own :]).astype(BF16)
    q_out[...] = q
    k_out[...] = k
    v_out[...] = v
    here = pl.ds(pl.multiple_of(step * block, block), block)
    k_all[here, :] = k
    v_all[here, :] = v
    queries = [only(q[:, pair_of(h)], h) * jnp.asarray(scale, BF16) for h in range(heads)]
    allowed = lax.broadcasted_iota(jnp.int32, (block, block), 0) >= lax.broadcasted_iota(
        jnp.int32, (block, block), 1
    )

    def score(j, peaks, diagonal):
        spot = pl.ds(pl.multiple_of(j * block, block), block)
        out = []
        for h in range(heads):
            s = nt(queries[h], k_all[spot, pair_of(h)])
            if diagonal:
                s = jnp.where(allowed, s, MASKED)
            scores[h, :, spot] = s
            out.append(jnp.maximum(peaks[h], fold(s, jnp.maximum)))
        return out

    peaks = [jnp.full((block, LANES), MASKED, F32)] * heads
    peaks = lax.fori_loop(0, step, lambda j, c: score(j, c, False), peaks)
    peaks = score(step, peaks, True)
    peaks = [jnp.max(p, axis=1, keepdims=True) for p in peaks]
    total[...] = jnp.zeros_like(total)

    def gather(j, sums):
        spot = pl.ds(pl.multiple_of(j * block, block), block)
        out = []
        for h in range(heads):
            p = jnp.exp(scores[h, :, spot] - peaks[h])
            out.append(sums[h] + fold(p, jnp.add))
            total[h] += nn(p.astype(BF16), v_all[spot, pair_of(h)])
        return out

    sums = lax.fori_loop(0, step + 1, gather, [jnp.zeros((block, LANES), F32)] * heads)
    lane = lax.broadcasted_iota(jnp.int32, (block, LANES), 1)
    logs = jnp.zeros((block, LANES), F32)
    tops = jnp.full((1, LANES), MASKED, F32)
    for h in range(heads):
        amount = jnp.sum(sums[h], axis=1, keepdims=True)
        total[h] = total[h] / amount
        logs = jnp.where(lane == h, peaks[h] + jnp.log(amount), logs)
        tops = jnp.where(lane[:1] == h, jnp.max(peaks[h], axis=0, keepdims=True), tops)
    log_out[...] = logs
    for h in range(0, heads, 2):
        mixed = jnp.where(lane < HEAD, total[h], total[h + 1])
        mixed_out[:, pair_of(h)] = mixed
        low_out[:, pair_of(h)] = mixed.astype(BF16)

    @pl.when(step == 0)
    def _():
        max_out[...] = tops

    @pl.when(step > 0)
    def _():
        max_out[...] = jnp.maximum(max_out[...], tops)


def attend(joined, bias, tables, heads, scale, block):
    length = joined.shape[0]
    own = joined.shape[1] // 3
    row = lambda i: (i, 0)
    zero = lambda i: (0, 0)
    shapes = [
        ((length, own), BF16), ((length, own), BF16), ((length, own), BF16),
        ((length, own), F32), ((length, own), BF16), ((length, LANES), F32),
    ]
    pairs = heads * length * length // 2
    return pl.pallas_call(
        partial(attend_kernel, heads, scale),
        name="attend",
        out_shape=[jax.ShapeDtypeStruct(s, d) for s, d in shapes]
        + [jax.ShapeDtypeStruct((1, LANES), F32)],
        grid_spec=pltpu.PrefetchScalarGridSpec(
            num_scalar_prefetch=0,
            grid=(length // block,),
            in_specs=[pl.BlockSpec((block, 3 * own), row), pl.BlockSpec((1, 3 * own), zero)]
            + [pl.BlockSpec((block, LANES), row)] * 3,
            out_specs=[pl.BlockSpec((block, s[1]), row) for s, d in shapes]
            + [pl.BlockSpec((1, LANES), zero)],
            scratch_shapes=[
                pltpu.VMEM((length, own), BF16),
                pltpu.VMEM((length, own), BF16),
                pltpu.VMEM((heads, block, length), F32),
                pltpu.VMEM((heads, block, LANES), F32),
            ],
        ),
        compiler_params=pltpu.CompilerParams(vmem_limit_bytes=VMEM),
        cost_estimate=pl.CostEstimate(
            flops=4 * pairs * 2 * LANES, transcendentals=pairs, bytes_accessed=length * own * 26
        ),
    )(joined, bias, *tables)


def attend_back_kernel(
    heads, scale, q, k, v, k_here, grad, mixed, logs, cosine, above, below,
    low_out, sum_out, k_turned, k_total, v_total, q_total,
):
    step = pl.program_id(0)
    block, own = q.shape
    length = k.shape[0]
    copies = own // LANES
    spot_here = pl.ds(pl.multiple_of(step * block, block), block)

    @pl.when(step == 0)
    def _():
        k_total[...] = jnp.zeros_like(k_total)
        v_total[...] = jnp.zeros_like(v_total)

    k_turned[:, spot_here] = k_here[...].T
    q_total[...] = jnp.zeros_like(q_total)
    log_rows = logs[...].T
    product = grad[...].astype(F32) * mixed[...]
    lane = lax.broadcasted_iota(jnp.int32, (block, LANES), 1)
    deltas = jnp.zeros((block, LANES), F32)
    for h in range(heads):
        own_sum = jnp.sum(only(product[:, pair_of(h)], h), axis=1, keepdims=True)
        deltas = jnp.where(lane == h, own_sum, deltas)
    delta_rows = deltas.T
    queries = [only(q[:, pair_of(h)], h) * jnp.asarray(scale, BF16) for h in range(heads)]
    grads = [only(grad[:, pair_of(h)], h) for h in range(heads)]
    allowed = lax.broadcasted_iota(jnp.int32, (block, block), 0) <= lax.broadcasted_iota(
        jnp.int32, (block, block), 1
    )

    def visit(j, diagonal):
        spot = pl.ds(pl.multiple_of(j * block, block), block)
        for h in range(heads):
            s = nt(k[spot, pair_of(h)], queries[h])
            if diagonal:
                s = jnp.where(allowed, s, MASKED)
            p = jnp.exp(s - log_rows[h : h + 1])
            dp = nt(v[spot, pair_of(h)], grads[h])
            ds = (p * (dp - delta_rows[h : h + 1])).astype(BF16)
            v_total[spot, pair_of(h)] += nn(p.astype(BF16), grads[h])
            k_total[spot, pair_of(h)] += nn(ds, queries[h])
            q_total[h] += nn(k_turned[pair_of(h), spot], ds)

    def body(j, carry):
        visit(j, False)
        return carry

    lax.fori_loop(0, step, body, 0)
    visit(step, True)
    row = lax.broadcasted_iota(jnp.int32, (LANES, block), 0)
    tables = (cosine[spot_here, :], above[spot_here, :], below[spot_here, :])
    sums = []
    for h in range(0, heads, 2):
        dq = jnp.where(row < HEAD, q_total[h], q_total[h + 1]).T * scale
        low = turn(dq, *tables, -1.0).astype(BF16)
        low_out[spot_here, pair_of(h)] = low
        sums.append(jnp.sum(low.astype(F32), axis=0, keepdims=True))
    sums = jnp.concatenate(sums, axis=1)

    @pl.when(step == 0)
    def _():
        sum_out[:, :own] = sums

    @pl.when(step > 0)
    def _():
        sum_out[:, :own] += sums

    @pl.when(step == length // block - 1)
    def _():
        wide = [jnp.concatenate([t[...]] * copies, axis=1) for t in (cosine, above, below)]
        low = turn(k_total[...], *wide, -1.0).astype(BF16)
        low_out[:, own : 2 * own] = low
        sum_out[:, own : 2 * own] = jnp.sum(low.astype(F32), axis=0, keepdims=True)
        low = v_total[...].astype(BF16)
        low_out[:, 2 * own :] = low
        sum_out[:, 2 * own :] = jnp.sum(low.astype(F32), axis=0, keepdims=True)


def attend_back(q, k, v, grad, mixed, logs, tables, heads, scale, block):
    length, own = q.shape
    row = lambda i: (i, 0)
    zero = lambda i: (0, 0)
    rows = pl.BlockSpec((block, own), row)
    whole = pl.BlockSpec((length, own), zero)
    pairs = heads * length * length // 2
    return pl.pallas_call(
        partial(attend_back_kernel, heads, scale),
        name="attend_back",
        out_shape=[
            jax.ShapeDtypeStruct((length, 3 * own), BF16),
            jax.ShapeDtypeStruct((1, 3 * own), F32),
        ],
        grid_spec=pltpu.PrefetchScalarGridSpec(
            num_scalar_prefetch=0,
            grid=(length // block,),
            in_specs=[rows, whole, whole, rows, rows, rows, pl.BlockSpec((block, LANES), row)]
            + [pl.BlockSpec((length, LANES), zero)] * 3,
            out_specs=[
                pl.BlockSpec((length, 3 * own), zero),
                pl.BlockSpec((1, 3 * own), zero),
            ],
            scratch_shapes=[
                pltpu.VMEM((own, length), BF16),
                pltpu.VMEM((length, own), F32),
                pltpu.VMEM((length, own), F32),
                pltpu.VMEM((heads, LANES, block), F32),
            ],
        ),
        compiler_params=pltpu.CompilerParams(vmem_limit_bytes=VMEM),
        cost_estimate=pl.CostEstimate(
            flops=10 * pairs * 2 * LANES, transcendentals=pairs, bytes_accessed=length * own * 20
        ),
    )(q, k, v, k, grad, mixed, logs, *tables)


def to_columns(rows, groups):
    parts = lax.axis_size("ctx")
    count, columns = rows.shape
    width = columns // (groups * parts)
    return (
        rows.reshape(count, groups, parts, width)
        .transpose(2, 0, 1, 3)
        .reshape(parts, count, groups * width)
    )


def exchange(blocks):
    return lax.all_to_all(blocks, "ctx", split_axis=0, concat_axis=0, tiled=True)


def gather_weights(qkv_weight, up_weight):
    u = to_columns(my_part(up_weight, 0), 1)
    q = to_columns(my_part(qkv_weight, 0), 3)
    u = exchange(u)
    u, q = lax.optimization_barrier((u, q))
    u_near = along_both((u, u))
    q = exchange(q)
    u_far = along_both(forwarded(u_near, 1))
    q_near = along_both((q, q))
    return q, q_near, u, u_near, u_far


def reduce_input_grad(grad, own_rows, groups):
    grad = grad.reshape(lax.axis_size("ctx"), own_rows, grad.shape[1])
    part = exchange(lax.psum_scatter(grad, "dp", scatter_dimension=1, tiled=True))
    rows = lax.all_gather(part, "dp", axis=1, tiled=True)
    return (
        rows.reshape(rows.shape[0], own_rows, groups, -1)
        .transpose(1, 2, 0, 3)
        .reshape(own_rows, -1)
        .astype(F32)
    )


def per_device(
    tokens,
    positions,
    norm_gain,
    norm_bias,
    qkv_weight,
    qkv_bias,
    dense_weight,
    dense_bias,
    up_weight,
    up_bias,
    down_weight,
    down_bias,
    clip_limit,
    cotangent,
):
    seqs, stretch, width = tokens.shape
    heads = clip_limit.shape[0]
    head_dim = width // heads
    rows = seqs * stretch
    parts = lax.axis_size("ctx")
    part = lax.axis_index("ctx")
    own_heads = heads // parts
    own = own_heads * head_dim
    own_rows = qkv_weight.shape[0]
    own_ff = down_weight.shape[0]
    length = stretch * parts
    count = seqs * length
    scale = head_dim ** (-0.5)

    shared = lax.axis_size("dp") == 4
    digits = jnp.stack([positions // 32, positions % 32], axis=-1)
    marked = jnp.concatenate(
        [tokens, jnp.pad(digits.astype(BF16), ((0, 0), (0, 0), (0, LANES - 2)))], axis=-1
    )
    if shared:
        q, q_near, u, u_near, u_far = gather_weights(qkv_weight, up_weight)
        up_columns = full_rows(four_parts(u, u_near, u_far), own_rows)
        q_far = along_both(forwarded(q_near, 1))
        marked = after(marked, u)
    else:
        q, u = exchange(to_columns(qkv_weight, 3)), exchange(to_columns(up_weight, 1))
        qkv_columns, up_columns = q.reshape(width, -1), u.reshape(width, -1)
    all_tokens = lax.all_gather(marked, "ctx", axis=1, tiled=True).reshape(count, width + LANES)
    grad_rows = lax.all_gather(
        after(cotangent, marked), "ctx", axis=1, tiled=True
    ).reshape(count, width)
    hidden, stats = normalize(all_tokens, norm_gain, norm_bias)
    if shared:
        q_far = after(q_far, up_columns, hidden)
        qkv_columns = full_rows(four_parts(q, q_near, q_far), own_rows)
    digits = all_tokens[:, width : width + 2].astype(F32)
    places = (digits[:, 0] * 32.0 + digits[:, 1]).reshape(seqs, length)
    tables = [rotary_lanes(places[s]) for s in range(seqs)]

    qkv_own_bias = take(qkv_bias.reshape(3, parts, own), part, 1, 1).reshape(1, 3 * own)
    up_own_bias = take(up_bias, part * own_ff, own_ff, 0)

    joined = dot(hidden, qkv_columns, (1, 0))
    block = 256 if length % 256 == 0 else length
    ahead = [
        attend(
            joined[s * length : (s + 1) * length], qkv_own_bias, tables[s], own_heads, scale, block
        )
        for s in range(seqs)
    ]
    attended = jnp.concatenate([a[4] for a in ahead])
    own_maxima = jnp.max(jnp.stack([a[6][0, :own_heads] for a in ahead]), axis=0)
    upward = dot(hidden, up_columns, (1, 0)) + up_own_bias
    activated, gelu_back = jax.vjp(partial(jax.nn.gelu, approximate=True), upward)
    activated = activated.astype(BF16)

    def feed_forward_back(grad_rows):
        act_grad = dot(grad_rows, down_weight, (1, 1))
        up_low = gelu_back(act_grad)[0].astype(BF16)
        return up_low, dot(hidden, up_low, (0, 0)).astype(BF16)

    def attention_back(grad_rows):
        mixed_low = dot(grad_rows, dense_weight, (1, 1)).astype(BF16)
        back = [
            attend_back(
                q, k, v, mixed_low[s * length : (s + 1) * length], mixed, logs, tables[s],
                own_heads, scale, block,
            )
            for s, (q, k, v, mixed, low, logs, tops) in enumerate(ahead)
        ]
        joined_low = jnp.concatenate([b[0] for b in back])
        qkv_raw = dot(hidden, joined_low, (0, 0)).astype(BF16)
        return joined_low, sum(b[1] for b in back), qkv_raw

    def sum_branch(value):
        return lax.psum_scatter(
            value.reshape(seqs, length, width),
            "ctx",
            scatter_dimension=1,
            tiled=True,
        ).reshape(rows, width)

    def own_sums(joined_sum, up_low):
        return jnp.concatenate(
            [
                joined_sum[0],
                jnp.sum(up_low.astype(F32), axis=0),
                jnp.sum(take(grad_rows, part * own, own, 1).astype(F32), axis=0),
            ]
        )

    def small_sums(shifts, mine):
        return jnp.concatenate([shifts.reshape(2 * width), mine])[None], own_maxima[None]

    def finish_rows(branch_sum, hidden_grad):
        return finish(
            tokens.reshape(rows, width),
            cotangent.reshape(rows, width),
            branch_sum,
            hidden_grad,
            norm_gain,
            dense_bias + down_bias,
        )

    def dp_step(small, bit):
        sums, tops = small
        got = swap(jnp.concatenate([sums, tops], axis=1), "dp", bit)
        cut = sums.shape[1]
        return sums + got[:, :cut], jnp.maximum(tops, got[:, cut:])

    def spread(small):
        value = jnp.concatenate(small, axis=1)
        return exchange(jnp.broadcast_to(value[None], (parts,) + value.shape))

    def clip(small):
        head_maxima = small[:, 0, small.shape[2] - own_heads :].reshape(heads)
        return head_maxima, clip_columns(qkv_weight, qkv_bias, head_maxima, clip_limit, head_dim)

    grad_rows, attended, activated = lax.optimization_barrier((grad_rows, attended, activated))
    mixed_out = jnp.concatenate([attended, activated], axis=1)
    out_raw = dot(mixed_out, grad_rows, (0, 0)).astype(BF16)
    if shared:
        together = lax.optimization_barrier
        o_got = along_both(o_send := outgoing(out_raw, 1))
        up_low, up_raw = feed_forward_back(after(grad_rows, o_send))
        up_raw = up_raw.reshape(parts, own_rows, own_ff)
        u_got = along_both(u_send := outgoing(up_raw, 1))
        branch = output_part(after(attended, u_send), dense_weight, activated, down_weight)
        branch_sum = sum_branch(branch)
        o_send, o_keep = first_sums(out_raw, after(o_got, branch), 1)
        o_got = along_both(o_send)
        joined_low, joined_sum, qkv_raw = attention_back(after(grad_rows, o_send))
        qkv_raw = qkv_raw.reshape(parts, own_rows, 3 * own)
        q_send = outgoing(qkv_raw, 1)
        q_send, u_got = together((q_send, u_got))
        q_got = along_both(q_send)
        u_send, u_keep = first_sums(up_raw, u_got, 1)
        u_send, o_got = together((u_send, o_got))
        u_got = along_both(u_send)
        o_part = second_sums(o_keep, o_got, 1)
        hidden_part, shifts = input_part(
            after(joined_low, o_part), qkv_columns, up_low, up_columns, all_tokens, stats
        )
        mine = own_sums(joined_sum, after(up_low, qkv_raw))
        q_got, o_part, shifts, mine = together((q_got, o_part, shifts, mine))
        q_send, q_keep = first_sums(qkv_raw, q_got, 1)
        small = small_sums(shifts, mine)
        q_send, u_got, small = together((q_send, u_got, small))
        u_part = second_sums(u_keep, u_got, 1)
        u_part, o_part, q_send, small = together((u_part, o_part, q_send, small))
        q_got = along_both(q_send)
        o_near = along_both((o_part, o_part))
        u_part = exchange(u_part)
        small = dp_step(small, 1)
        q_got, u_part, o_near, small = together((q_got, u_part, o_near, small))
        hidden_grad = sum_branch(after(hidden_part, u_part))
        u_near = along_both((u_part, u_part))
        o_send = forwarded(o_near, 1)
        q_part = exchange(second_sums(q_keep, q_got, 1))
        o_far = along_both(o_send)
        small = dp_step(small, 2)
        u_near, q_part, o_far, small = together((u_near, q_part, o_far, small))
        q_near = along_both((q_part, q_part))
        u_send = forwarded(u_near, 1)
        u_far = along_both(u_send)
        o_parts = four_parts(o_part, o_near, after(o_far, u_send))
        dense_grad = full_columns(o_parts, 0, own, own)
        down_grad = full_columns(o_parts, own, own_ff, own)
        small = spread(after(small, down_grad))
        q_near, u_far, small, dense_grad, down_grad = together(
            (q_near, u_far, small, dense_grad, down_grad)
        )
        q_send = forwarded(q_near, 1)
        q_far = along_both(q_send)
        u_far, branch_sum, hidden_grad = after((u_far, branch_sum, hidden_grad), q_send)
        up_grad = full_grad(four_parts(u_part, u_near, u_far), own_rows, 1)
        ends = finish_rows(branch_sum, hidden_grad)
        head_maxima, (clipped_weight, clipped_bias) = clip(after(small, q_send))
        q_far, up_grad, ends, clipped_weight = together((q_far, up_grad, ends, clipped_weight))
        qkv_grad = full_grad(four_parts(q_part, q_near, q_far), own_rows, 3)
    else:
        up_low, up_raw = feed_forward_back(grad_rows)
        joined_low, joined_sum, qkv_raw = attention_back(grad_rows)
        branch_sum = sum_branch(output_part(attended, dense_weight, activated, down_weight))
        hidden_part, shifts = input_part(
            joined_low, qkv_columns, up_low, up_columns, all_tokens, stats
        )
        hidden_grad = sum_branch(hidden_part)
        out_grad = lax.psum(out_raw, "dp").astype(F32)
        dense_grad, down_grad = out_grad[:own], out_grad[own:]
        up_grad = reduce_input_grad(up_raw, own_rows, 1)
        qkv_grad = reduce_input_grad(qkv_raw, own_rows, 3)
        small = small_sums(shifts, own_sums(joined_sum, up_low))
        small = spread((lax.psum(small[0], "dp"), lax.pmax(small[1], "dp")))
        head_maxima, (clipped_weight, clipped_bias) = clip(small)
        ends = finish_rows(branch_sum, hidden_grad)
    layer_out, tokens_grad = ends
    shifts = jnp.sum(small[:, 0, : 2 * width], axis=0)
    both = small[:, 0, 2 * width :]
    cut = 3 * own + own_ff
    qkv_bias_grad = (
        both[:, : 3 * own].reshape(parts, 3, own).transpose(1, 0, 2).reshape(3 * width)
    )
    up_bias_grad = both[:, 3 * own : cut].reshape(parts * own_ff)
    out_bias_grad = both[:, cut : cut + own].reshape(width)

    return (
        layer_out.reshape(seqs, stretch, width),
        tokens_grad.reshape(seqs, stretch, width),
        shifts[:width],
        shifts[width:],
        qkv_grad,
        qkv_bias_grad,
        dense_grad,
        out_bias_grad,
        up_grad,
        up_bias_grad,
        down_grad,
        out_bias_grad,
        head_maxima,
        clipped_weight,
        clipped_bias,
    )


def solution(mesh):
    rows = P("dp", "ctx", None)
    weight = P("ctx", None)
    in_specs = (rows, P("dp", "ctx"), P(), P()) + (weight, P()) * 4 + (P(), rows)
    out_specs = (
        (rows, rows, P(), P()) + (weight, P()) * 4 + (P(), weight, P())
    )
    return jax.shard_map(
        per_device, mesh=mesh, in_specs=in_specs, out_specs=out_specs, check_vma=False
    )
```

```python
from functools import partial

import jax
import jax.numpy as jnp
from jax import lax
from jax.experimental import pallas as pl
from jax.experimental.pallas import tpu as pltpu
from jax.sharding import PartitionSpec as P

ROT = 32
EPSILON = 1e-05
MASKED = -1e30
ROPE_BASE = 10000.0
BF16 = jnp.bfloat16
F32 = jnp.float32
LANES = 128
HEAD = 64
VMEM = 40 << 20
LIGHT = pl.CostEstimate(flops=1, transcendentals=0, bytes_accessed=1)


def dot(left, right, contract):
    return lax.dot_general(
        left, right, ((contract[:1], contract[1:]), ((), ())), preferred_element_type=F32
    )


def swap(value, axis, bit):
    return lax.ppermute(value, axis, [(i, i ^ bit) for i in range(lax.axis_size(axis))])


def take(value, start, size, axis):
    return lax.dynamic_slice_in_dim(value, start, size, axis)


def first_place(index):
    return (index & 1) * 2 + (index >> 1)


def my_part(value, axis):
    index = lax.axis_index("dp")
    size = value.shape[axis] // 8
    return jnp.concatenate(
        [
            take(value, first_place(index) * size, size, axis),
            take(value, (4 + index) * size, size, axis),
        ],
        axis,
    )


def after(value, *others):
    return lax.optimization_barrier((value, others))[0]


def along_both(pair):
    return swap(pair[0], "dp", 1), swap(pair[1], "dp", 2)


def plus(left, right):
    return (left.astype(F32) + right.astype(F32)).astype(BF16)


def outgoing(value, axis):
    index = lax.axis_index("dp")
    size = value.shape[axis] // 8
    return (
        take(value, (1 - (index & 1)) * 2 * size, 2 * size, axis),
        take(value, (4 + (1 - (index >> 1)) * 2) * size, 2 * size, axis),
    )


def dp_index():
    return lax.axis_index("dp").astype(jnp.int32).reshape(1)


def first_sums(value, received, axis):
    index = lax.axis_index("dp")
    low, high = index & 1, index >> 1
    size = value.shape[axis] // 8
    first = plus(take(value, low * 2 * size, 2 * size, axis), received[0])
    second = plus(take(value, (4 + high * 2) * size, 2 * size, axis), received[1])
    send = (
        take(second, (1 - low) * size, size, axis),
        take(first, (1 - high) * size, size, axis),
    )
    keep = jnp.concatenate(
        [take(first, high * size, size, axis), take(second, low * size, size, axis)], axis
    )
    return send, keep


def second_sums(keep, received, axis):
    return plus(keep, jnp.concatenate([received[1], received[0]], axis))


def normalize_kernel(tokens, gain, shift, hidden, stats):
    value = tokens[...].astype(F32)
    mean = jnp.mean(value, axis=1, keepdims=True)
    centre = value - mean
    inv_std = lax.rsqrt(jnp.mean(centre * centre, axis=1, keepdims=True) + EPSILON)
    hidden[...] = (centre * inv_std * gain[...] + shift[...]).astype(BF16)
    lane = lax.broadcasted_iota(jnp.int32, stats.shape, 1)
    stats[...] = jnp.where(lane == 0, mean, inv_std)


def normalize(tokens, gain, shift):
    count, width = tokens.shape[0], gain.shape[0]
    block = 256 if count % 256 == 0 else count
    row = lambda i: (i, 0)
    return pl.pallas_call(
        normalize_kernel,
        name="normalize",
        out_shape=[
            jax.ShapeDtypeStruct((count, width), BF16),
            jax.ShapeDtypeStruct((count, LANES), F32),
        ],
        grid=(count // block,),
        in_specs=[pl.BlockSpec((block, width), row)]
        + [pl.BlockSpec((1, width), lambda i: (0, 0))] * 2,
        out_specs=[pl.BlockSpec((block, width), row), pl.BlockSpec((block, LANES), row)],
        compiler_params=pltpu.CompilerParams(vmem_limit_bytes=VMEM),
        cost_estimate=LIGHT,
    )(tokens, gain[None], shift[None])


def output_kernel(attended, dense, activated, down, out):
    out[...] = (nn(attended[...], dense[...]) + nn(activated[...], down[...])).astype(BF16)


def output_part(attended, dense, activated, down):
    count, width = attended.shape[0], dense.shape[1]
    block = 256
    fixed = lambda i: (0, 0)
    column = lambda i: (0, i)
    return pl.pallas_call(
        output_kernel,
        name="output_part",
        out_shape=jax.ShapeDtypeStruct((count, width), BF16),
        grid=(width // block,),
        in_specs=[
            pl.BlockSpec(attended.shape, fixed),
            pl.BlockSpec((dense.shape[0], block), column),
            pl.BlockSpec(activated.shape, fixed),
            pl.BlockSpec((down.shape[0], block), column),
        ],
        out_specs=pl.BlockSpec((count, block), column),
        compiler_params=pltpu.CompilerParams(vmem_limit_bytes=VMEM),
        cost_estimate=LIGHT,
    )(attended, dense, activated, down)


def input_kernel(joined, qkv, upward, up, tokens, stats, out, sums, up_sum):
    total = nt(joined[...], qkv[...]) + nt(upward[...], up[...])
    out[...] = total.astype(BF16)
    xhat = (tokens[...].astype(F32) - stats[:, 0:1]) * stats[:, 1:2]
    sums[0:1, :] = jnp.sum(total * xhat, axis=0, keepdims=True)
    sums[1:2, :] = jnp.sum(total, axis=0, keepdims=True)

    @pl.when(pl.program_id(0) == 0)
    def _():
        up_sum[...] = jnp.sum(upward[...].astype(F32), axis=0, keepdims=True)


def input_part(joined, qkv, upward, up, tokens, stats):
    count, width = tokens.shape[0], qkv.shape[0]
    block = 256
    fixed = lambda i: (0, 0)
    column = lambda i: (0, i)
    row = lambda i: (i, 0)
    return pl.pallas_call(
        input_kernel,
        name="input_part",
        out_shape=[
            jax.ShapeDtypeStruct((count, width), BF16),
            jax.ShapeDtypeStruct((2, width), F32),
            jax.ShapeDtypeStruct((1, upward.shape[1]), F32),
        ],
        grid=(width // block,),
        in_specs=[
            pl.BlockSpec(joined.shape, fixed),
            pl.BlockSpec((block, qkv.shape[1]), row),
            pl.BlockSpec(upward.shape, fixed),
            pl.BlockSpec((block, up.shape[1]), row),
            pl.BlockSpec((count, block), column),
            pl.BlockSpec(stats.shape, fixed),
        ],
        out_specs=[
            pl.BlockSpec((count, block), column),
            pl.BlockSpec((2, block), column),
            pl.BlockSpec((1, upward.shape[1]), fixed),
        ],
        compiler_params=pltpu.CompilerParams(vmem_limit_bytes=VMEM),
        cost_estimate=LIGHT,
    )(joined, qkv, upward, up, tokens, stats)


def finish_kernel(tokens, cotangent, branch, grad, gain, bias, out, tokens_grad):
    value = tokens[...].astype(F32)
    out[...] = (value + branch[...].astype(F32) + bias[...]).astype(BF16)
    centre = value - jnp.mean(value, axis=1, keepdims=True)
    inv_std = lax.rsqrt(jnp.mean(centre * centre, axis=1, keepdims=True) + EPSILON)
    xhat = centre * inv_std
    scaled = grad[...].astype(F32) * gain[...]
    inner = jnp.mean(scaled * xhat, axis=1, keepdims=True)
    scaled = scaled - jnp.mean(scaled, axis=1, keepdims=True) - xhat * inner
    tokens_grad[...] = cotangent[...].astype(F32) + inv_std * scaled


def finish(tokens, cotangent, branch, grad, gain, bias):
    rows, width = tokens.shape
    block = 64 if rows % 64 == 0 else rows
    row = pl.BlockSpec((block, width), lambda i: (i, 0))
    vector = pl.BlockSpec((1, width), lambda i: (0, 0))
    return pl.pallas_call(
        finish_kernel,
        name="finish",
        out_shape=[
            jax.ShapeDtypeStruct((rows, width), BF16),
            jax.ShapeDtypeStruct((rows, width), F32),
        ],
        grid=(rows // block,),
        in_specs=[row] * 4 + [vector] * 2,
        out_specs=[row, row],
        compiler_params=pltpu.CompilerParams(vmem_limit_bytes=VMEM),
        cost_estimate=LIGHT,
    )(tokens, cotangent, branch, grad, gain[None], bias[None])


def clip_kernel(own_heads, head_dim, tops, limits, weight, bias, out, bias_out):
    parts = tops.shape[0]
    heads = parts * own_heads
    first = lax.rem(pl.program_id(0) * (out.shape[1] // head_dim), heads)
    lane = lax.broadcasted_iota(jnp.int32, (1, LANES), 1)
    head = first + lax.broadcasted_iota(jnp.int32, (1, out.shape[1]), 1) // head_dim
    scale = jnp.zeros((1, out.shape[1]), F32)
    for part in range(parts):
        limit = limits[part : part + 1, :]
        factor = jnp.sqrt(limit / jnp.maximum(tops[part], limit))
        for h in range(own_heads):
            one = jnp.sum(jnp.where(lane == h, factor, 0.0), axis=1, keepdims=True)
            scale = jnp.where(head == part * own_heads + h, one, scale)
    out[...] = weight[...].astype(F32) * scale
    bias_out[...] = bias[...] * scale


def clip_columns(weight, bias, small, limits, own_heads, head_dim):
    rows, parts = weight.shape[0], small.shape[0]
    columns = 2 * parts * own_heads * head_dim
    block = columns // 4
    column = lambda i: (0, i)
    wide, thin = pl.BlockSpec((rows, block), column), pl.BlockSpec((1, block), column)
    limits = jnp.pad(
        limits.astype(F32).reshape(parts, own_heads),
        ((0, 0), (0, LANES - own_heads)),
        constant_values=1.0,
    )
    return pl.pallas_call(
        partial(clip_kernel, own_heads, head_dim),
        name="clip_columns",
        out_shape=[
            jax.ShapeDtypeStruct((rows, columns), F32),
            jax.ShapeDtypeStruct((1, columns), F32),
        ],
        grid=(columns // block,),
        in_specs=[
            pl.BlockSpec((parts, 1, LANES), lambda i: (0, 0, small.shape[2] // LANES - 1)),
            pl.BlockSpec((parts, LANES), lambda i: (0, 0)),
            wide,
            thin,
        ],
        out_specs=[wide, thin],
        compiler_params=pltpu.CompilerParams(vmem_limit_bytes=VMEM),
        cost_estimate=LIGHT,
    )(small, limits, weight, bias[None])


def unpack_kernel(common, own, own_ff, own_heads, small, *outs):
    *shifts, qkv_bias, up_bias, maxima = outs
    parts = small.shape[0]
    width = common // len(shifts)
    for i, out in enumerate(shifts):
        total = small[0, :, i * width : (i + 1) * width]
        for part in range(1, parts):
            total = total + small[part, :, i * width : (i + 1) * width]
        out[...] = total
    lane = lax.broadcasted_iota(jnp.int32, maxima.shape, 1)
    tops = jnp.zeros(maxima.shape, F32)
    for part in range(parts):
        for group in range(3):
            spot = (group * parts + part) * own
            qkv_bias[:, spot : spot + own] = small[
                part, :, common + group * own : common + (group + 1) * own
            ]
        start = common + 3 * own
        up_bias[:, part * own_ff : (part + 1) * own_ff] = small[part, :, start : start + own_ff]
        for h in range(own_heads):
            one = small[part, :, start + own_ff + h : start + own_ff + h + 1]
            tops = jnp.where(lane == part * own_heads + h, one, tops)
    maxima[...] = tops


def unpack(small, common, own, own_ff, own_heads):
    parts = small.shape[0]
    shapes = [common // 3] * 3 + [3 * parts * own, parts * own_ff, parts * own_heads]
    *shifts, qkv_bias, up_bias, maxima = pl.pallas_call(
        partial(unpack_kernel, common, own, own_ff, own_heads),
        name="unpack",
        out_shape=[jax.ShapeDtypeStruct((1, n), F32) for n in shapes],
        compiler_params=pltpu.CompilerParams(vmem_limit_bytes=VMEM),
        cost_estimate=LIGHT,
    )(small)
    return shifts, qkv_bias, up_bias, maxima


def forwarded(received, axis):
    half = received[0].shape[axis] // 2
    return (
        lax.slice_in_dim(received[1], 0, half, axis=axis),
        lax.slice_in_dim(received[0], half, 2 * half, axis=axis),
    )


def four_parts(part, near, far):
    return [part, near[0], near[1], far[0], far[1]]


def pieces_of(index_ref, refs, eighth, axis):
    me = index_ref[0]
    first = (slice(None),) * axis + (slice(0, eighth),)
    second = (slice(None),) * axis + (slice(eighth, 2 * eighth),)
    for offset in range(3):
        owner = me ^ offset
        yield first_place(owner), refs[offset], first
        yield 4 + owner, refs[offset], second
    if len(refs) > 3:
        owner = me ^ 3
        yield first_place(owner), refs[3], first
        yield 4 + owner, refs[4], first


def place_rows(index_ref, *refs):
    out = refs[-1]
    blocks, size, width = refs[0].shape
    for spot, ref, cut in pieces_of(index_ref, refs[:-1], size // 2, 1):
        rows = pl.ds(pl.multiple_of(spot * (size // 2), size // 2), size // 2)
        for i in range(blocks):
            out[rows, i * width : (i + 1) * width] = ref[(i,) + cut[1:]].astype(out.dtype)


def place_columns(index_ref, *refs):
    out = refs[-1]
    eighth = refs[0].shape[1] // 2
    for spot, ref, cut in pieces_of(index_ref, refs[:-1], eighth, 1):
        columns = pl.ds(pl.multiple_of(spot * eighth, eighth), eighth)
        out[:, columns] = ref[cut].astype(out.dtype)


def place(body, parts, axis, grid, in_block, in_map, out_shape, out_block, out_map):
    half = list(in_block)
    half[axis] //= 2
    return pl.pallas_call(
        body,
        out_shape=out_shape,
        grid_spec=pltpu.PrefetchScalarGridSpec(
            num_scalar_prefetch=1,
            grid=grid,
            in_specs=[pl.BlockSpec(in_block, in_map)] * 3
            + [pl.BlockSpec(tuple(half), in_map)] * (len(parts) - 3),
            out_specs=pl.BlockSpec(out_block, out_map),
        ),
        compiler_params=pltpu.CompilerParams(vmem_limit_bytes=VMEM),
        cost_estimate=LIGHT,
    )(dp_index(), *parts)


def full_rows(parts, own_rows):
    blocks, size, columns = parts[0].shape
    return place(
        place_rows,
        parts,
        1,
        (blocks,),
        (1, size, columns),
        lambda i, index: (i, 0, 0),
        jax.ShapeDtypeStruct((blocks * own_rows, columns), parts[0].dtype),
        (own_rows, columns),
        lambda i, index: (i, 0),
    )


def full_grad(parts, own_rows, groups):
    blocks, size, columns = parts[0].shape
    width = columns // groups
    several = max(1, min(blocks, 1024 // width))
    steps = blocks // several
    return place(
        place_rows,
        parts,
        1,
        (groups, steps),
        (several, size, width),
        lambda g, i, index: (i, 0, g),
        jax.ShapeDtypeStruct((own_rows, groups * blocks * width), F32),
        (own_rows, several * width),
        lambda g, i, index: (0, g * steps + i),
    )


def full_columns(parts, first, count, block):
    size = parts[0].shape[1]
    return place(
        place_columns,
        parts,
        1,
        (count // block,),
        (block, size),
        lambda i, index: (i + first // block, 0),
        jax.ShapeDtypeStruct((count, 4 * size), F32),
        (block, 4 * size),
        lambda i, index: (i, 0),
    )


def rotary_lanes(positions):
    half = ROT // 2
    lane = jnp.arange(LANES, dtype=jnp.int32) % HEAD
    frequency = ROPE_BASE ** (-((lane % half).astype(F32) * 2.0 / ROT))
    angles = positions.astype(F32)[:, None] * frequency
    sine = jnp.sin(angles)
    return (
        jnp.where(lane < ROT, jnp.cos(angles), 1.0),
        jnp.where(lane < half, -sine, 0.0),
        jnp.where((lane >= half) & (lane < ROT), sine, 0.0),
    )


def turn(value, cosine, above, below, sign):
    half = ROT // 2
    size = value.shape[1]
    from_above = pltpu.roll(value, size - half, 1)
    from_below = pltpu.roll(value, half, 1)
    return value * cosine + sign * (from_above * above + from_below * below)


def nt(left, right):
    return lax.dot_general(left, right, (((1,), (1,)), ((), ())), preferred_element_type=F32)


def nn(left, right):
    return lax.dot_general(left, right, (((1,), (0,)), ((), ())), preferred_element_type=F32)


def pair_of(head):
    return slice(head // 2 * LANES, head // 2 * LANES + LANES)


def only(value, head):
    lane = lax.broadcasted_iota(jnp.int32, value.shape, 1)
    return jnp.where((lane // HEAD) == head % 2, value, jnp.zeros_like(value))


def fold(value, op):
    out = value[:, :LANES]
    for start in range(LANES, value.shape[1], LANES):
        out = op(out, value[:, start : start + LANES])
    return out


def attend_kernel(
    heads, scale, joined, bias, cosine, above, below,
    q_out, k_out, v_out, mixed_out, low_out, log_out, max_out,
    k_all, v_all, scores, total,
):
    step = pl.program_id(0)
    block, own = q_out.shape
    copies = own // LANES
    tables = [jnp.concatenate([t[...]] * copies, axis=1) for t in (cosine, above, below)]
    q = turn(joined[:, :own] + bias[:, :own], *tables, 1.0).astype(BF16)
    k = turn(joined[:, own : 2 * own] + bias[:, own : 2 * own], *tables, 1.0).astype(BF16)
    v = (joined[:, 2 * own :] + bias[:, 2 * own :]).astype(BF16)
    q_out[...] = q
    k_out[...] = k
    v_out[...] = v
    here = pl.ds(pl.multiple_of(step * block, block), block)
    k_all[here, :] = k
    v_all[here, :] = v
    queries = [only(q[:, pair_of(h)], h) * jnp.asarray(scale, BF16) for h in range(heads)]
    allowed = lax.broadcasted_iota(jnp.int32, (block, block), 0) >= lax.broadcasted_iota(
        jnp.int32, (block, block), 1
    )

    def score(j, peaks, diagonal):
        spot = pl.ds(pl.multiple_of(j * block, block), block)
        out = []
        for h in range(heads):
            s = nt(queries[h], k_all[spot, pair_of(h)])
            if diagonal:
                s = jnp.where(allowed, s, MASKED)
            scores[h, :, spot] = s
            out.append(jnp.maximum(peaks[h], fold(s, jnp.maximum)))
        return out

    peaks = [jnp.full((block, LANES), MASKED, F32)] * heads
    peaks = lax.fori_loop(0, step, lambda j, c: score(j, c, False), peaks)
    peaks = score(step, peaks, True)
    peaks = [jnp.max(p, axis=1, keepdims=True) for p in peaks]
    total[...] = jnp.zeros_like(total)

    def gather(j, sums):
        spot = pl.ds(pl.multiple_of(j * block, block), block)
        out = []
        for h in range(heads):
            p = jnp.exp(scores[h, :, spot] - peaks[h])
            out.append(sums[h] + fold(p, jnp.add))
            total[h] += nn(p.astype(BF16), v_all[spot, pair_of(h)])
        return out

    sums = lax.fori_loop(0, step + 1, gather, [jnp.zeros((block, LANES), F32)] * heads)
    lane = lax.broadcasted_iota(jnp.int32, (block, LANES), 1)
    logs = jnp.zeros((block, LANES), F32)
    tops = jnp.full((1, LANES), MASKED, F32)
    for h in range(heads):
        amount = jnp.sum(sums[h], axis=1, keepdims=True)
        total[h] = total[h] / amount
        logs = jnp.where(lane == h, peaks[h] + jnp.log(amount), logs)
        tops = jnp.where(lane[:1] == h, jnp.max(peaks[h], axis=0, keepdims=True), tops)
    log_out[...] = logs
    for h in range(0, heads, 2):
        mixed = jnp.where(lane < HEAD, total[h], total[h + 1])
        mixed_out[:, pair_of(h)] = mixed
        low_out[:, pair_of(h)] = mixed.astype(BF16)

    @pl.when(step == 0)
    def _():
        max_out[...] = tops

    @pl.when(step > 0)
    def _():
        max_out[...] = jnp.maximum(max_out[...], tops)


def attend(joined, bias, tables, heads, scale, block):
    length = joined.shape[0]
    own = joined.shape[1] // 3
    row = lambda i: (i, 0)
    zero = lambda i: (0, 0)
    shapes = [
        ((length, own), BF16), ((length, own), BF16), ((length, own), BF16),
        ((length, own), F32), ((length, own), BF16), ((length, LANES), F32),
    ]
    pairs = heads * length * length // 2
    return pl.pallas_call(
        partial(attend_kernel, heads, scale),
        name="attend",
        out_shape=[jax.ShapeDtypeStruct(s, d) for s, d in shapes]
        + [jax.ShapeDtypeStruct((1, LANES), F32)],
        grid_spec=pltpu.PrefetchScalarGridSpec(
            num_scalar_prefetch=0,
            grid=(length // block,),
            in_specs=[pl.BlockSpec((block, 3 * own), row), pl.BlockSpec((1, 3 * own), zero)]
            + [pl.BlockSpec((block, LANES), row)] * 3,
            out_specs=[pl.BlockSpec((block, s[1]), row) for s, d in shapes]
            + [pl.BlockSpec((1, LANES), zero)],
            scratch_shapes=[
                pltpu.VMEM((length, own), BF16),
                pltpu.VMEM((length, own), BF16),
                pltpu.VMEM((heads, block, length), F32),
                pltpu.VMEM((heads, block, LANES), F32),
            ],
        ),
        compiler_params=pltpu.CompilerParams(vmem_limit_bytes=VMEM),
        cost_estimate=pl.CostEstimate(
            flops=4 * pairs * 2 * LANES, transcendentals=pairs, bytes_accessed=length * own * 26
        ),
    )(joined, bias, *tables)


def attend_back_kernel(
    heads, scale, q, k, v, k_here, grad, mixed, logs, cosine, above, below,
    low_out, sum_out, k_turned, k_total, v_total, q_total,
):
    step = pl.program_id(0)
    block, own = q.shape
    length = k.shape[0]
    copies = own // LANES
    spot_here = pl.ds(pl.multiple_of(step * block, block), block)

    @pl.when(step == 0)
    def _():
        k_total[...] = jnp.zeros_like(k_total)
        v_total[...] = jnp.zeros_like(v_total)

    k_turned[:, spot_here] = k_here[...].T
    q_total[...] = jnp.zeros_like(q_total)
    log_rows = logs[...].T
    product = grad[...].astype(F32) * mixed[...]
    lane = lax.broadcasted_iota(jnp.int32, (block, LANES), 1)
    deltas = jnp.zeros((block, LANES), F32)
    for h in range(heads):
        own_sum = jnp.sum(only(product[:, pair_of(h)], h), axis=1, keepdims=True)
        deltas = jnp.where(lane == h, own_sum, deltas)
    delta_rows = deltas.T
    queries = [only(q[:, pair_of(h)], h) * jnp.asarray(scale, BF16) for h in range(heads)]
    grads = [only(grad[:, pair_of(h)], h) for h in range(heads)]
    allowed = lax.broadcasted_iota(jnp.int32, (block, block), 0) <= lax.broadcasted_iota(
        jnp.int32, (block, block), 1
    )

    def visit(j, diagonal):
        spot = pl.ds(pl.multiple_of(j * block, block), block)
        for h in range(heads):
            s = nt(k[spot, pair_of(h)], queries[h])
            if diagonal:
                s = jnp.where(allowed, s, MASKED)
            p = jnp.exp(s - log_rows[h : h + 1])
            dp = nt(v[spot, pair_of(h)], grads[h])
            ds = (p * (dp - delta_rows[h : h + 1])).astype(BF16)
            v_total[spot, pair_of(h)] += nn(p.astype(BF16), grads[h])
            k_total[spot, pair_of(h)] += nn(ds, queries[h])
            q_total[h] += nn(k_turned[pair_of(h), spot], ds)

    def body(j, carry):
        visit(j, False)
        return carry

    lax.fori_loop(0, step, body, 0)
    visit(step, True)
    row = lax.broadcasted_iota(jnp.int32, (LANES, block), 0)
    tables = (cosine[spot_here, :], above[spot_here, :], below[spot_here, :])
    sums = []
    for h in range(0, heads, 2):
        dq = jnp.where(row < HEAD, q_total[h], q_total[h + 1]).T * scale
        low = turn(dq, *tables, -1.0).astype(BF16)
        low_out[spot_here, pair_of(h)] = low
        sums.append(jnp.sum(low.astype(F32), axis=0, keepdims=True))
    sums = jnp.concatenate(sums, axis=1)

    @pl.when(step == 0)
    def _():
        sum_out[:, :own] = sums

    @pl.when(step > 0)
    def _():
        sum_out[:, :own] += sums

    @pl.when(step == length // block - 1)
    def _():
        wide = [jnp.concatenate([t[...]] * copies, axis=1) for t in (cosine, above, below)]
        low = turn(k_total[...], *wide, -1.0).astype(BF16)
        low_out[:, own : 2 * own] = low
        sum_out[:, own : 2 * own] = jnp.sum(low.astype(F32), axis=0, keepdims=True)
        low = v_total[...].astype(BF16)
        low_out[:, 2 * own :] = low
        sum_out[:, 2 * own :] = jnp.sum(low.astype(F32), axis=0, keepdims=True)


def attend_back(q, k, v, grad, mixed, logs, tables, heads, scale, block):
    length, own = q.shape
    row = lambda i: (i, 0)
    zero = lambda i: (0, 0)
    rows = pl.BlockSpec((block, own), row)
    whole = pl.BlockSpec((length, own), zero)
    pairs = heads * length * length // 2
    return pl.pallas_call(
        partial(attend_back_kernel, heads, scale),
        name="attend_back",
        out_shape=[
            jax.ShapeDtypeStruct((length, 3 * own), BF16),
            jax.ShapeDtypeStruct((1, 3 * own), F32),
        ],
        grid_spec=pltpu.PrefetchScalarGridSpec(
            num_scalar_prefetch=0,
            grid=(length // block,),
            in_specs=[rows, whole, whole, rows, rows, rows, pl.BlockSpec((block, LANES), row)]
            + [pl.BlockSpec((length, LANES), zero)] * 3,
            out_specs=[
                pl.BlockSpec((length, 3 * own), zero),
                pl.BlockSpec((1, 3 * own), zero),
            ],
            scratch_shapes=[
                pltpu.VMEM((own, length), BF16),
                pltpu.VMEM((length, own), F32),
                pltpu.VMEM((length, own), F32),
                pltpu.VMEM((heads, LANES, block), F32),
            ],
        ),
        compiler_params=pltpu.CompilerParams(vmem_limit_bytes=VMEM),
        cost_estimate=pl.CostEstimate(
            flops=10 * pairs * 2 * LANES, transcendentals=pairs, bytes_accessed=length * own * 20
        ),
    )(q, k, v, k, grad, mixed, logs, *tables)


def to_columns(rows, groups):
    parts = lax.axis_size("ctx")
    count, columns = rows.shape
    width = columns // (groups * parts)
    return (
        rows.reshape(count, groups, parts, width)
        .transpose(2, 0, 1, 3)
        .reshape(parts, count, groups * width)
    )


def exchange(blocks):
    return lax.all_to_all(blocks, "ctx", split_axis=0, concat_axis=0, tiled=True)


def gather_weights(qkv_weight, up_weight):
    u = to_columns(my_part(up_weight, 0), 1)
    q = to_columns(my_part(qkv_weight, 0), 3)
    u = exchange(u)
    u, q = lax.optimization_barrier((u, q))
    u_near = along_both((u, u))
    q = exchange(q)
    u_far = along_both(forwarded(u_near, 1))
    q, u_far = lax.optimization_barrier((q, u_far))
    q_near = along_both((q, q))
    return q, q_near, u, u_near, u_far


def reduce_input_grad(grad, own_rows, groups):
    grad = grad.reshape(lax.axis_size("ctx"), own_rows, grad.shape[1])
    part = exchange(lax.psum_scatter(grad, "dp", scatter_dimension=1, tiled=True))
    rows = lax.all_gather(part, "dp", axis=1, tiled=True)
    return (
        rows.reshape(rows.shape[0], own_rows, groups, -1)
        .transpose(1, 2, 0, 3)
        .reshape(own_rows, -1)
        .astype(F32)
    )


def per_device(
    tokens,
    positions,
    norm_gain,
    norm_bias,
    qkv_weight,
    qkv_bias,
    dense_weight,
    dense_bias,
    up_weight,
    up_bias,
    down_weight,
    down_bias,
    clip_limit,
    cotangent,
):
    seqs, stretch, width = tokens.shape
    heads = clip_limit.shape[0]
    head_dim = width // heads
    rows = seqs * stretch
    parts = lax.axis_size("ctx")
    part = lax.axis_index("ctx")
    own_heads = heads // parts
    own = own_heads * head_dim
    own_rows = qkv_weight.shape[0]
    own_ff = down_weight.shape[0]
    length = stretch * parts
    count = seqs * length
    scale = head_dim ** (-0.5)

    shared = lax.axis_size("dp") == 4
    cotangent_sum = jnp.sum(cotangent.astype(F32), axis=(0, 1))[None]
    digits = jnp.stack([positions // 32, positions % 32], axis=-1)
    marked = jnp.concatenate(
        [tokens, jnp.pad(digits.astype(BF16), ((0, 0), (0, 0), (0, LANES - 2)))], axis=-1
    )
    if shared:
        q, q_near, u, u_near, u_far = gather_weights(qkv_weight, up_weight)
        up_columns = full_rows(four_parts(u, u_near, u_far), own_rows)
        q_send = forwarded(after(q_near, up_columns), 1)
        q_far = along_both(q_send)
        marked = after(marked, u)
    else:
        q, u = exchange(to_columns(qkv_weight, 3)), exchange(to_columns(up_weight, 1))
        qkv_columns, up_columns = q.reshape(width, -1), u.reshape(width, -1)
    all_tokens = lax.all_gather(marked, "ctx", axis=1, tiled=True).reshape(count, width + LANES)
    grad_rows = lax.all_gather(
        after(cotangent, marked), "ctx", axis=1, tiled=True
    ).reshape(count, width)
    if shared:
        all_tokens = after(all_tokens, q_send)
    hidden, stats = normalize(all_tokens, norm_gain, norm_bias)
    digits = all_tokens[:, width : width + 2].astype(F32)
    places = (digits[:, 0] * 32.0 + digits[:, 1]).reshape(seqs, length)
    tables = [rotary_lanes(places[s]) for s in range(seqs)]
    if shared:
        q_far = after(q_far, hidden, tables)
        qkv_columns = full_rows(four_parts(q, q_near, q_far), own_rows)

    qkv_own_bias = take(qkv_bias.reshape(3, parts, own), part, 1, 1).reshape(1, 3 * own)
    up_own_bias = take(up_bias, part * own_ff, own_ff, 0)

    joined = dot(hidden, qkv_columns, (1, 0))
    block = 256 if length % 256 == 0 else length
    ahead = [
        attend(
            joined[s * length : (s + 1) * length], qkv_own_bias, tables[s], own_heads, scale, block
        )
        for s in range(seqs)
    ]
    attended = jnp.concatenate([a[4] for a in ahead])
    own_maxima = jnp.max(jnp.stack([a[6] for a in ahead]), axis=0)
    upward = dot(after(hidden, attended), up_columns, (1, 0)) + up_own_bias
    activated, gelu_back = jax.vjp(partial(jax.nn.gelu, approximate=True), upward)
    activated = activated.astype(BF16)

    def feed_forward_back(grad_rows):
        act_grad = dot(grad_rows, down_weight, (1, 1))
        up_low = gelu_back(act_grad)[0].astype(BF16)
        return up_low, dot(hidden, up_low, (0, 0)).astype(BF16)

    def attention_back(grad_rows):
        mixed_low = dot(grad_rows, dense_weight, (1, 1)).astype(BF16)
        back = [
            attend_back(
                q, k, v, mixed_low[s * length : (s + 1) * length], mixed, logs, tables[s],
                own_heads, scale, block,
            )
            for s, (q, k, v, mixed, low, logs, tops) in enumerate(ahead)
        ]
        joined_low = jnp.concatenate([b[0] for b in back])
        qkv_raw = dot(hidden, joined_low, (0, 0)).astype(BF16)
        return joined_low, sum(b[1] for b in back), qkv_raw

    def sum_branch(value):
        return lax.psum_scatter(
            value.reshape(seqs, length, width),
            "ctx",
            scatter_dimension=1,
            tiled=True,
        ).reshape(rows, width)

    def small_sums(shifts, joined_sum, up_sum):
        everyone = [shifts.reshape(1, 2 * width), cotangent_sum]
        return jnp.concatenate(everyone + [joined_sum, up_sum], axis=1), own_maxima

    def finish_rows(branch_sum, hidden_grad):
        return finish(
            tokens.reshape(rows, width),
            cotangent.reshape(rows, width),
            branch_sum,
            hidden_grad,
            norm_gain,
            dense_bias + down_bias,
        )

    def dp_step(small, bit):
        sums, tops = small
        got = swap(jnp.concatenate([sums, tops], axis=1), "dp", bit)
        cut = sums.shape[1]
        return sums + got[:, :cut], jnp.maximum(tops, got[:, cut:])

    def spread(small):
        value = jnp.concatenate(small, axis=1)
        return exchange(jnp.broadcast_to(value[None], (parts,) + value.shape))

    grad_rows, attended, activated = lax.optimization_barrier((grad_rows, attended, activated))
    mixed_out = jnp.concatenate([attended, activated], axis=1)
    out_raw = dot(mixed_out, grad_rows, (0, 0)).astype(BF16)
    if shared:
        together = lax.optimization_barrier
        o_got = along_both(o_send := outgoing(out_raw, 1))
        up_low, up_raw = feed_forward_back(after(grad_rows, o_send))
        up_raw = up_raw.reshape(parts, own_rows, own_ff)
        u_got = along_both(u_send := outgoing(up_raw, 1))
        branch = output_part(after(attended, u_send), dense_weight, activated, down_weight)
        branch_sum = sum_branch(branch)
        o_send, o_keep = first_sums(out_raw, after(o_got, branch), 1)
        o_got = along_both(o_send)
        joined_low, joined_sum, qkv_raw = attention_back(after(grad_rows, o_send))
        qkv_raw = qkv_raw.reshape(parts, own_rows, 3 * own)
        q_send = outgoing(qkv_raw, 1)
        q_send, u_got = together((q_send, u_got))
        q_got = along_both(q_send)
        u_send, u_keep = first_sums(up_raw, u_got, 1)
        u_send, o_got = together((u_send, o_got))
        u_got = along_both(u_send)
        o_part = second_sums(o_keep, o_got, 1)
        hidden_part, shifts, up_sum = input_part(
            after(joined_low, o_part), qkv_columns, up_low, up_columns, all_tokens, stats
        )
        small = small_sums(shifts, joined_sum, up_sum)
        u_part = second_sums(u_keep, after(u_got, shifts), 1)
        q_got, o_part, small = after((q_got, o_part, small), u_part)
        u_part = exchange(u_part)
        q_send, q_keep = first_sums(qkv_raw, q_got, 1)
        q_send, o_part, small = together((q_send, o_part, small))
        q_got = along_both(q_send)
        o_near = along_both((o_part, o_part))
        small = dp_step(small, 1)
        q_got, u_part, o_near, small = together((q_got, u_part, o_near, small))
        hidden_grad = sum_branch(after(hidden_part, u_part))
        u_near = along_both((u_part, u_part))
        o_send = forwarded(o_near, 1)
        q_part = exchange(second_sums(q_keep, q_got, 1))
        o_far = along_both(o_send)
        small = dp_step(small, 2)
        u_near, q_part, o_far, small = together((u_near, q_part, o_far, small))
        q_near = along_both((q_part, q_part))
        u_send = forwarded(u_near, 1)
        u_far = along_both(u_send)
        o_parts = four_parts(o_part, o_near, after(o_far, u_send))
        dense_grad = full_columns(o_parts, 0, own, own)
        down_grad = full_columns(o_parts, own, own_ff, own)
        small = spread(after(small, down_grad))
        q_near, u_far, small, down_grad = together((q_near, u_far, small, down_grad))
        q_send = forwarded(q_near, 1)
        q_far = along_both(q_send)
        u_far, branch_sum, hidden_grad, small = after(
            (u_far, branch_sum, hidden_grad, small), q_send
        )
        up_grad = full_grad(four_parts(u_part, u_near, u_far), own_rows, 1)
        ends = finish_rows(branch_sum, hidden_grad)
        clipped = clip_columns(qkv_weight, qkv_bias, small, clip_limit, own_heads, head_dim)
        vectors = unpack(small, 3 * width, own, own_ff, own_heads)
        q_far, up_grad, ends, clipped, vectors = together(
            (q_far, up_grad, ends, clipped, vectors)
        )
        qkv_grad = full_grad(four_parts(q_part, q_near, q_far), own_rows, 3)
    else:
        up_low, up_raw = feed_forward_back(grad_rows)
        joined_low, joined_sum, qkv_raw = attention_back(grad_rows)
        branch_sum = sum_branch(output_part(attended, dense_weight, activated, down_weight))
        hidden_part, shifts, up_sum = input_part(
            joined_low, qkv_columns, up_low, up_columns, all_tokens, stats
        )
        hidden_grad = sum_branch(hidden_part)
        out_grad = lax.psum(out_raw, "dp").astype(F32)
        dense_grad, down_grad = out_grad[:own], out_grad[own:]
        up_grad = reduce_input_grad(up_raw, own_rows, 1)
        qkv_grad = reduce_input_grad(qkv_raw, own_rows, 3)
        small = small_sums(shifts, joined_sum, up_sum)
        small = spread((lax.psum(small[0], "dp"), lax.pmax(small[1], "dp")))
        clipped = clip_columns(qkv_weight, qkv_bias, small, clip_limit, own_heads, head_dim)
        vectors = unpack(small, 3 * width, own, own_ff, own_heads)
        ends = finish_rows(branch_sum, hidden_grad)
    layer_out, tokens_grad = ends
    clipped_weight, clipped_bias = clipped
    shifts, qkv_bias_grad, up_bias_grad, head_maxima = vectors
    return (
        layer_out.reshape(seqs, stretch, width),
        tokens_grad.reshape(seqs, stretch, width),
        shifts[0].reshape(width),
        shifts[1].reshape(width),
        qkv_grad,
        qkv_bias_grad.reshape(3 * width),
        dense_grad,
        shifts[2].reshape(width),
        up_grad,
        up_bias_grad.reshape(parts * own_ff),
        down_grad,
        shifts[2].reshape(width),
        head_maxima.reshape(heads),
        clipped_weight,
        clipped_bias.reshape(2 * width),
    )


def solution(mesh):
    rows = P("dp", "ctx", None)
    weight = P("ctx", None)
    in_specs = (rows, P("dp", "ctx"), P(), P()) + (weight, P()) * 4 + (P(), rows)
    out_specs = (
        (rows, rows, P(), P()) + (weight, P()) * 4 + (P(), weight, P())
    )
    return jax.shard_map(
        per_device, mesh=mesh, in_specs=in_specs, out_specs=out_specs, check_vma=False
    )
```

```python
from functools import partial

import jax
import jax.numpy as jnp
from jax import lax
from jax.experimental import pallas as pl
from jax.experimental.pallas import tpu as pltpu
from jax.sharding import PartitionSpec as P

ROT = 32
EPSILON = 1e-05
MASKED = -1e30
ROPE_BASE = 10000.0
BF16 = jnp.bfloat16
F32 = jnp.float32
LANES = 128
HEAD = 64
VMEM = 40 << 20
MOST_VMEM = 58 << 20
LIGHT = pl.CostEstimate(flops=1, transcendentals=0, bytes_accessed=1)


def dot(left, right, contract):
    return lax.dot_general(
        left, right, ((contract[:1], contract[1:]), ((), ())), preferred_element_type=F32
    )


def swap(value, axis, bit):
    return lax.ppermute(value, axis, [(i, i ^ bit) for i in range(lax.axis_size(axis))])


def take(value, start, size, axis):
    return lax.dynamic_slice_in_dim(value, start, size, axis)


def first_place(index):
    return (index & 1) * 2 + (index >> 1)


def my_part(value, axis):
    index = lax.axis_index("dp")
    size = value.shape[axis] // 8
    return jnp.concatenate(
        [
            take(value, first_place(index) * size, size, axis),
            take(value, (4 + index) * size, size, axis),
        ],
        axis,
    )


def after(value, *others):
    return lax.optimization_barrier((value, others))[0]


def along_both(pair):
    return swap(pair[0], "dp", 1), swap(pair[1], "dp", 2)


def plus(left, right):
    return (left.astype(F32) + right.astype(F32)).astype(BF16)


def outgoing(value, axis):
    index = lax.axis_index("dp")
    size = value.shape[axis] // 8
    return (
        take(value, (1 - (index & 1)) * 2 * size, 2 * size, axis),
        take(value, (4 + (1 - (index >> 1)) * 2) * size, 2 * size, axis),
    )


def dp_index():
    return lax.axis_index("dp").astype(jnp.int32).reshape(1)


def first_sums(value, received, axis):
    index = lax.axis_index("dp")
    low, high = index & 1, index >> 1
    size = value.shape[axis] // 8
    first = plus(take(value, low * 2 * size, 2 * size, axis), received[0])
    second = plus(take(value, (4 + high * 2) * size, 2 * size, axis), received[1])
    send = (
        take(second, (1 - low) * size, size, axis),
        take(first, (1 - high) * size, size, axis),
    )
    keep = jnp.concatenate(
        [take(first, high * size, size, axis), take(second, low * size, size, axis)], axis
    )
    return send, keep


def second_sums(keep, received, axis):
    return plus(keep, jnp.concatenate([received[1], received[0]], axis))


def normalize_kernel(tokens, gain, shift, hidden, stats):
    value = tokens[...].astype(F32)
    mean = jnp.mean(value, axis=1, keepdims=True)
    centre = value - mean
    inv_std = lax.rsqrt(jnp.mean(centre * centre, axis=1, keepdims=True) + EPSILON)
    hidden[...] = (centre * inv_std * gain[...] + shift[...]).astype(BF16)
    lane = lax.broadcasted_iota(jnp.int32, stats.shape, 1)
    stats[...] = jnp.where(lane == 0, mean, inv_std)


def normalize(tokens, gain, shift):
    count, width = tokens.shape[0], gain.shape[0]
    block = 256 if count % 256 == 0 else count
    row = lambda i: (i, 0)
    return pl.pallas_call(
        normalize_kernel,
        name="normalize",
        out_shape=[
            jax.ShapeDtypeStruct((count, width), BF16),
            jax.ShapeDtypeStruct((count, LANES), F32),
        ],
        grid=(count // block,),
        in_specs=[pl.BlockSpec((block, width), row)]
        + [pl.BlockSpec((1, width), lambda i: (0, 0))] * 2,
        out_specs=[pl.BlockSpec((block, width), row), pl.BlockSpec((block, LANES), row)],
        compiler_params=pltpu.CompilerParams(vmem_limit_bytes=VMEM),
        cost_estimate=LIGHT,
    )(tokens, gain[None], shift[None])


def output_kernel(attended, dense, activated, down, out):
    out[...] = (nn(attended[...], dense[...]) + nn(activated[...], down[...])).astype(BF16)


def output_part(attended, dense, activated, down):
    count, width = attended.shape[0], dense.shape[1]
    block = 256
    fixed = lambda i: (0, 0)
    column = lambda i: (0, i)
    return pl.pallas_call(
        output_kernel,
        name="output_part",
        out_shape=jax.ShapeDtypeStruct((count, width), BF16),
        grid=(width // block,),
        in_specs=[
            pl.BlockSpec(attended.shape, fixed),
            pl.BlockSpec((dense.shape[0], block), column),
            pl.BlockSpec(activated.shape, fixed),
            pl.BlockSpec((down.shape[0], block), column),
        ],
        out_specs=pl.BlockSpec((count, block), column),
        compiler_params=pltpu.CompilerParams(vmem_limit_bytes=VMEM),
        cost_estimate=LIGHT,
    )(attended, dense, activated, down)


def input_kernel(joined, qkv, upward, up, tokens, stats, out, sums, up_sum):
    total = nt(joined[...], qkv[...]) + nt(upward[...], up[...])
    out[...] = total.astype(BF16)
    xhat = (tokens[...].astype(F32) - stats[:, 0:1]) * stats[:, 1:2]
    sums[0:1, :] = jnp.sum(total * xhat, axis=0, keepdims=True)
    sums[1:2, :] = jnp.sum(total, axis=0, keepdims=True)

    @pl.when(pl.program_id(0) == 0)
    def _():
        up_sum[...] = jnp.sum(upward[...].astype(F32), axis=0, keepdims=True)


def input_part(joined, qkv, upward, up, tokens, stats):
    count, width = tokens.shape[0], qkv.shape[0]
    block = 256
    fixed = lambda i: (0, 0)
    column = lambda i: (0, i)
    row = lambda i: (i, 0)
    return pl.pallas_call(
        input_kernel,
        name="input_part",
        out_shape=[
            jax.ShapeDtypeStruct((count, width), BF16),
            jax.ShapeDtypeStruct((2, width), F32),
            jax.ShapeDtypeStruct((1, upward.shape[1]), F32),
        ],
        grid=(width // block,),
        in_specs=[
            pl.BlockSpec(joined.shape, fixed),
            pl.BlockSpec((block, qkv.shape[1]), row),
            pl.BlockSpec(upward.shape, fixed),
            pl.BlockSpec((block, up.shape[1]), row),
            pl.BlockSpec((count, block), column),
            pl.BlockSpec(stats.shape, fixed),
        ],
        out_specs=[
            pl.BlockSpec((count, block), column),
            pl.BlockSpec((2, block), column),
            pl.BlockSpec((1, upward.shape[1]), fixed),
        ],
        compiler_params=pltpu.CompilerParams(vmem_limit_bytes=VMEM),
        cost_estimate=LIGHT,
    )(joined, qkv, upward, up, tokens, stats)


def finish_kernel(tokens, cotangent, branch, grad, gain, bias, out, tokens_grad):
    value = tokens[...].astype(F32)
    out[...] = (value + branch[...].astype(F32) + bias[...]).astype(BF16)
    centre = value - jnp.mean(value, axis=1, keepdims=True)
    inv_std = lax.rsqrt(jnp.mean(centre * centre, axis=1, keepdims=True) + EPSILON)
    xhat = centre * inv_std
    scaled = grad[...].astype(F32) * gain[...]
    inner = jnp.mean(scaled * xhat, axis=1, keepdims=True)
    scaled = scaled - jnp.mean(scaled, axis=1, keepdims=True) - xhat * inner
    tokens_grad[...] = cotangent[...].astype(F32) + inv_std * scaled


def finish(tokens, cotangent, branch, grad, gain, bias):
    rows, width = tokens.shape
    block = 64 if rows % 64 == 0 else rows
    row = pl.BlockSpec((block, width), lambda i: (i, 0))
    vector = pl.BlockSpec((1, width), lambda i: (0, 0))
    return pl.pallas_call(
        finish_kernel,
        name="finish",
        out_shape=[
            jax.ShapeDtypeStruct((rows, width), BF16),
            jax.ShapeDtypeStruct((rows, width), F32),
        ],
        grid=(rows // block,),
        in_specs=[row] * 4 + [vector] * 2,
        out_specs=[row, row],
        compiler_params=pltpu.CompilerParams(vmem_limit_bytes=VMEM),
        cost_estimate=LIGHT,
    )(tokens, cotangent, branch, grad, gain[None], bias[None])


def clip_kernel(own_heads, head_dim, tops, limits, weight, bias, out, bias_out):
    parts = tops.shape[0]
    heads = parts * own_heads
    first = lax.rem(pl.program_id(0) * (out.shape[1] // head_dim), heads)
    lane = lax.broadcasted_iota(jnp.int32, (1, LANES), 1)
    head = first + lax.broadcasted_iota(jnp.int32, (1, out.shape[1]), 1) // head_dim
    scale = jnp.zeros((1, out.shape[1]), F32)
    for part in range(parts):
        limit = limits[part : part + 1, :]
        factor = jnp.sqrt(limit / jnp.maximum(tops[part], limit))
        for h in range(own_heads):
            one = jnp.sum(jnp.where(lane == h, factor, 0.0), axis=1, keepdims=True)
            scale = jnp.where(head == part * own_heads + h, one, scale)
    out[...] = weight[...].astype(F32) * scale
    bias_out[...] = bias[...] * scale


def clip_columns(weight, bias, small, limits, own_heads, head_dim):
    rows, parts = weight.shape[0], small.shape[0]
    columns = 2 * parts * own_heads * head_dim
    block = columns // 4
    column = lambda i: (0, i)
    wide, thin = pl.BlockSpec((rows, block), column), pl.BlockSpec((1, block), column)
    limits = jnp.pad(
        limits.astype(F32).reshape(parts, own_heads),
        ((0, 0), (0, LANES - own_heads)),
        constant_values=1.0,
    )
    return pl.pallas_call(
        partial(clip_kernel, own_heads, head_dim),
        name="clip_columns",
        out_shape=[
            jax.ShapeDtypeStruct((rows, columns), F32),
            jax.ShapeDtypeStruct((1, columns), F32),
        ],
        grid=(columns // block,),
        in_specs=[
            pl.BlockSpec((parts, 1, LANES), lambda i: (0, 0, small.shape[2] // LANES - 1)),
            pl.BlockSpec((parts, LANES), lambda i: (0, 0)),
            wide,
            thin,
        ],
        out_specs=[wide, thin],
        compiler_params=pltpu.CompilerParams(vmem_limit_bytes=VMEM),
        cost_estimate=LIGHT,
    )(small, limits, weight, bias[None])


def unpack_kernel(common, own, own_ff, own_heads, small, *outs):
    *shifts, qkv_bias, up_bias, maxima = outs
    parts = small.shape[0]
    width = common // len(shifts)
    for i, out in enumerate(shifts):
        total = small[0, :, i * width : (i + 1) * width]
        for part in range(1, parts):
            total = total + small[part, :, i * width : (i + 1) * width]
        out[...] = total
    lane = lax.broadcasted_iota(jnp.int32, maxima.shape, 1)
    tops = jnp.zeros(maxima.shape, F32)
    for part in range(parts):
        for group in range(3):
            spot = (group * parts + part) * own
            qkv_bias[:, spot : spot + own] = small[
                part, :, common + group * own : common + (group + 1) * own
            ]
        start = common + 3 * own
        up_bias[:, part * own_ff : (part + 1) * own_ff] = small[part, :, start : start + own_ff]
        for h in range(own_heads):
            one = small[part, :, start + own_ff + h : start + own_ff + h + 1]
            tops = jnp.where(lane == part * own_heads + h, one, tops)
    maxima[...] = tops


def unpack(small, common, own, own_ff, own_heads):
    parts = small.shape[0]
    shapes = [common // 3] * 3 + [3 * parts * own, parts * own_ff, parts * own_heads]
    *shifts, qkv_bias, up_bias, maxima = pl.pallas_call(
        partial(unpack_kernel, common, own, own_ff, own_heads),
        name="unpack",
        out_shape=[jax.ShapeDtypeStruct((1, n), F32) for n in shapes],
        compiler_params=pltpu.CompilerParams(vmem_limit_bytes=VMEM),
        cost_estimate=LIGHT,
    )(small)
    return shifts, qkv_bias, up_bias, maxima


def forwarded(received, axis):
    half = received[0].shape[axis] // 2
    return (
        lax.slice_in_dim(received[1], 0, half, axis=axis),
        lax.slice_in_dim(received[0], half, 2 * half, axis=axis),
    )


def four_parts(part, near, far):
    return [part, near[0], near[1], far[0], far[1]]


def pieces_of(index_ref, refs, eighth, axis):
    me = index_ref[0]
    first = (slice(None),) * axis + (slice(0, eighth),)
    second = (slice(None),) * axis + (slice(eighth, 2 * eighth),)
    for offset in range(3):
        owner = me ^ offset
        yield first_place(owner), refs[offset], first
        yield 4 + owner, refs[offset], second
    if len(refs) > 3:
        owner = me ^ 3
        yield first_place(owner), refs[3], first
        yield 4 + owner, refs[4], first


def place_rows(index_ref, *refs):
    out = refs[-1]
    blocks, size, width = refs[0].shape
    for spot, ref, cut in pieces_of(index_ref, refs[:-1], size // 2, 1):
        rows = pl.ds(pl.multiple_of(spot * (size // 2), size // 2), size // 2)
        for i in range(blocks):
            out[rows, i * width : (i + 1) * width] = ref[(i,) + cut[1:]].astype(out.dtype)


def place_columns(index_ref, *refs):
    out = refs[-1]
    eighth = refs[0].shape[1] // 2
    for spot, ref, cut in pieces_of(index_ref, refs[:-1], eighth, 1):
        columns = pl.ds(pl.multiple_of(spot * eighth, eighth), eighth)
        out[:, columns] = ref[cut].astype(out.dtype)


def place(
    body, vmem, parts, axis, grid, in_block, in_map, out_shape, out_block, out_map, cost=LIGHT
):
    half = list(in_block)
    half[axis] //= 2
    return pl.pallas_call(
        body,
        out_shape=out_shape,
        grid_spec=pltpu.PrefetchScalarGridSpec(
            num_scalar_prefetch=1,
            grid=grid,
            in_specs=[pl.BlockSpec(in_block, in_map)] * 3
            + [pl.BlockSpec(tuple(half), in_map)] * (len(parts) - 3),
            out_specs=pl.BlockSpec(out_block, out_map),
        ),
        compiler_params=pltpu.CompilerParams(vmem_limit_bytes=vmem),
        cost_estimate=cost,
    )(dp_index(), *parts)


def full_rows(parts, own_rows):
    blocks, size, columns = parts[0].shape
    return place(
        place_rows,
        VMEM,
        parts,
        1,
        (blocks,),
        (1, size, columns),
        lambda i, index: (i, 0, 0),
        jax.ShapeDtypeStruct((blocks * own_rows, columns), parts[0].dtype),
        (own_rows, columns),
        lambda i, index: (i, 0),
    )


def full_grad(parts, own_rows, groups, cost=LIGHT):
    blocks, size, columns = parts[0].shape
    width = columns // groups
    several = max(1, min(blocks, 1024 // width))
    steps = blocks // several
    return place(
        place_rows,
        MOST_VMEM,
        parts,
        1,
        (groups, steps),
        (several, size, width),
        lambda g, i, index: (i, 0, g),
        jax.ShapeDtypeStruct((own_rows, groups * blocks * width), F32),
        (own_rows, several * width),
        lambda g, i, index: (0, g * steps + i),
        cost,
    )


def full_columns(parts, first, count, block):
    size = parts[0].shape[1]
    return place(
        place_columns,
        MOST_VMEM,
        parts,
        1,
        (count // block,),
        (block, size),
        lambda i, index: (i + first // block, 0),
        jax.ShapeDtypeStruct((count, 4 * size), F32),
        (block, 4 * size),
        lambda i, index: (i, 0),
    )


def rotary_lanes(positions):
    half = ROT // 2
    lane = jnp.arange(LANES, dtype=jnp.int32) % HEAD
    frequency = ROPE_BASE ** (-((lane % half).astype(F32) * 2.0 / ROT))
    angles = positions.astype(F32)[:, None] * frequency
    sine = jnp.sin(angles)
    return (
        jnp.where(lane < ROT, jnp.cos(angles), 1.0),
        jnp.where(lane < half, -sine, 0.0),
        jnp.where((lane >= half) & (lane < ROT), sine, 0.0),
    )


def turn(value, cosine, above, below, sign):
    half = ROT // 2
    size = value.shape[1]
    from_above = pltpu.roll(value, size - half, 1)
    from_below = pltpu.roll(value, half, 1)
    return value * cosine + sign * (from_above * above + from_below * below)


def nt(left, right):
    return lax.dot_general(left, right, (((1,), (1,)), ((), ())), preferred_element_type=F32)


def nn(left, right):
    return lax.dot_general(left, right, (((1,), (0,)), ((), ())), preferred_element_type=F32)


def pair_of(head):
    return slice(head // 2 * LANES, head // 2 * LANES + LANES)


def only(value, head):
    lane = lax.broadcasted_iota(jnp.int32, value.shape, 1)
    return jnp.where((lane // HEAD) == head % 2, value, jnp.zeros_like(value))


def fold(value, op):
    out = value[:, :LANES]
    for start in range(LANES, value.shape[1], LANES):
        out = op(out, value[:, start : start + LANES])
    return out


def attend_kernel(
    heads, scale, joined, bias, cosine, above, below,
    q_out, k_out, v_out, mixed_out, low_out, log_out, max_out,
    k_all, v_all, scores, total,
):
    step = pl.program_id(0)
    block, own = q_out.shape
    copies = own // LANES
    tables = [jnp.concatenate([t[...]] * copies, axis=1) for t in (cosine, above, below)]
    q = turn(joined[:, :own] + bias[:, :own], *tables, 1.0).astype(BF16)
    k = turn(joined[:, own : 2 * own] + bias[:, own : 2 * own], *tables, 1.0).astype(BF16)
    v = (joined[:, 2 * own :] + bias[:, 2 * own :]).astype(BF16)
    q_out[...] = q
    k_out[...] = k
    v_out[...] = v
    here = pl.ds(pl.multiple_of(step * block, block), block)
    k_all[here, :] = k
    v_all[here, :] = v
    queries = [only(q[:, pair_of(h)], h) * jnp.asarray(scale, BF16) for h in range(heads)]
    allowed = lax.broadcasted_iota(jnp.int32, (block, block), 0) >= lax.broadcasted_iota(
        jnp.int32, (block, block), 1
    )

    def score(j, peaks, diagonal):
        spot = pl.ds(pl.multiple_of(j * block, block), block)
        out = []
        for h in range(heads):
            s = nt(queries[h], k_all[spot, pair_of(h)])
            if diagonal:
                s = jnp.where(allowed, s, MASKED)
            scores[h, :, spot] = s
            out.append(jnp.maximum(peaks[h], fold(s, jnp.maximum)))
        return out

    peaks = [jnp.full((block, LANES), MASKED, F32)] * heads
    peaks = lax.fori_loop(0, step, lambda j, c: score(j, c, False), peaks)
    peaks = score(step, peaks, True)
    peaks = [jnp.max(p, axis=1, keepdims=True) for p in peaks]
    total[...] = jnp.zeros_like(total)

    def gather(j, sums):
        spot = pl.ds(pl.multiple_of(j * block, block), block)
        out = []
        for h in range(heads):
            p = jnp.exp(scores[h, :, spot] - peaks[h])
            out.append(sums[h] + fold(p, jnp.add))
            total[h] += nn(p.astype(BF16), v_all[spot, pair_of(h)])
        return out

    sums = lax.fori_loop(0, step + 1, gather, [jnp.zeros((block, LANES), F32)] * heads)
    lane = lax.broadcasted_iota(jnp.int32, (block, LANES), 1)
    logs = jnp.zeros((block, LANES), F32)
    tops = jnp.full((1, LANES), MASKED, F32)
    for h in range(heads):
        amount = jnp.sum(sums[h], axis=1, keepdims=True)
        total[h] = total[h] / amount
        logs = jnp.where(lane == h, peaks[h] + jnp.log(amount), logs)
        tops = jnp.where(lane[:1] == h, jnp.max(peaks[h], axis=0, keepdims=True), tops)
    log_out[...] = logs
    for h in range(0, heads, 2):
        mixed = jnp.where(lane < HEAD, total[h], total[h + 1])
        mixed_out[:, pair_of(h)] = mixed
        low_out[:, pair_of(h)] = mixed.astype(BF16)

    @pl.when(step == 0)
    def _():
        max_out[...] = tops

    @pl.when(step > 0)
    def _():
        max_out[...] = jnp.maximum(max_out[...], tops)


def attend(joined, bias, tables, heads, scale, block):
    length = joined.shape[0]
    own = joined.shape[1] // 3
    row = lambda i: (i, 0)
    zero = lambda i: (0, 0)
    shapes = [
        ((length, own), BF16), ((length, own), BF16), ((length, own), BF16),
        ((length, own), F32), ((length, own), BF16), ((length, LANES), F32),
    ]
    pairs = heads * length * length // 2
    return pl.pallas_call(
        partial(attend_kernel, heads, scale),
        name="attend",
        out_shape=[pltpu.HBM(s, d) for s, d in shapes] + [jax.ShapeDtypeStruct((1, LANES), F32)],
        grid_spec=pltpu.PrefetchScalarGridSpec(
            num_scalar_prefetch=0,
            grid=(length // block,),
            in_specs=[pl.BlockSpec((block, 3 * own), row), pl.BlockSpec((1, 3 * own), zero)]
            + [pl.BlockSpec((block, LANES), row)] * 3,
            out_specs=[pl.BlockSpec((block, s[1]), row) for s, d in shapes]
            + [pl.BlockSpec((1, LANES), zero)],
            scratch_shapes=[
                pltpu.VMEM((length, own), BF16),
                pltpu.VMEM((length, own), BF16),
                pltpu.VMEM((heads, block, length), F32),
                pltpu.VMEM((heads, block, LANES), F32),
            ],
        ),
        compiler_params=pltpu.CompilerParams(vmem_limit_bytes=VMEM),
        cost_estimate=pl.CostEstimate(
            flops=4 * pairs * 2 * LANES, transcendentals=pairs, bytes_accessed=length * own * 26
        ),
    )(joined, bias, *tables)


def attend_back_kernel(
    heads, scale, q, k, v, k_here, grad, mixed, logs, cosine, above, below,
    low_out, sum_out, k_turned, k_total, v_total, q_total,
):
    step = pl.program_id(0)
    block, own = q.shape
    length = k.shape[0]
    copies = own // LANES
    spot_here = pl.ds(pl.multiple_of(step * block, block), block)

    @pl.when(step == 0)
    def _():
        k_total[...] = jnp.zeros_like(k_total)
        v_total[...] = jnp.zeros_like(v_total)

    k_turned[:, spot_here] = k_here[...].T
    q_total[...] = jnp.zeros_like(q_total)
    log_rows = logs[...].T
    product = grad[...].astype(F32) * mixed[...]
    lane = lax.broadcasted_iota(jnp.int32, (block, LANES), 1)
    deltas = jnp.zeros((block, LANES), F32)
    for h in range(heads):
        own_sum = jnp.sum(only(product[:, pair_of(h)], h), axis=1, keepdims=True)
        deltas = jnp.where(lane == h, own_sum, deltas)
    delta_rows = deltas.T
    queries = [only(q[:, pair_of(h)], h) * jnp.asarray(scale, BF16) for h in range(heads)]
    grads = [only(grad[:, pair_of(h)], h) for h in range(heads)]
    allowed = lax.broadcasted_iota(jnp.int32, (block, block), 0) <= lax.broadcasted_iota(
        jnp.int32, (block, block), 1
    )

    def visit(j, diagonal):
        spot = pl.ds(pl.multiple_of(j * block, block), block)
        for h in range(heads):
            s = nt(k[spot, pair_of(h)], queries[h])
            if diagonal:
                s = jnp.where(allowed, s, MASKED)
            p = jnp.exp(s - log_rows[h : h + 1])
            dp = nt(v[spot, pair_of(h)], grads[h])
            ds = (p * (dp - delta_rows[h : h + 1])).astype(BF16)
            v_total[spot, pair_of(h)] += nn(p.astype(BF16), grads[h])
            k_total[spot, pair_of(h)] += nn(ds, queries[h])
            q_total[h] += nn(k_turned[pair_of(h), spot], ds)

    def body(j, carry):
        visit(j, False)
        return carry

    lax.fori_loop(0, step, body, 0)
    visit(step, True)
    row = lax.broadcasted_iota(jnp.int32, (LANES, block), 0)
    tables = (cosine[spot_here, :], above[spot_here, :], below[spot_here, :])
    sums = []
    for h in range(0, heads, 2):
        dq = jnp.where(row < HEAD, q_total[h], q_total[h + 1]).T * scale
        low = turn(dq, *tables, -1.0).astype(BF16)
        low_out[spot_here, pair_of(h)] = low
        sums.append(jnp.sum(low.astype(F32), axis=0, keepdims=True))
    sums = jnp.concatenate(sums, axis=1)

    @pl.when(step == 0)
    def _():
        sum_out[:, :own] = sums

    @pl.when(step > 0)
    def _():
        sum_out[:, :own] += sums

    @pl.when(step == length // block - 1)
    def _():
        wide = [jnp.concatenate([t[...]] * copies, axis=1) for t in (cosine, above, below)]
        low = turn(k_total[...], *wide, -1.0).astype(BF16)
        low_out[:, own : 2 * own] = low
        sum_out[:, own : 2 * own] = jnp.sum(low.astype(F32), axis=0, keepdims=True)
        low = v_total[...].astype(BF16)
        low_out[:, 2 * own :] = low
        sum_out[:, 2 * own :] = jnp.sum(low.astype(F32), axis=0, keepdims=True)


def attend_back(q, k, v, grad, mixed, logs, tables, heads, scale, block):
    length, own = q.shape
    row = lambda i: (i, 0)
    zero = lambda i: (0, 0)
    rows = pl.BlockSpec((block, own), row)
    whole = pl.BlockSpec((length, own), zero)
    pairs = heads * length * length // 2
    return pl.pallas_call(
        partial(attend_back_kernel, heads, scale),
        name="attend_back",
        out_shape=[
            jax.ShapeDtypeStruct((length, 3 * own), BF16),
            jax.ShapeDtypeStruct((1, 3 * own), F32),
        ],
        grid_spec=pltpu.PrefetchScalarGridSpec(
            num_scalar_prefetch=0,
            grid=(length // block,),
            in_specs=[rows, whole, whole, rows, rows, rows, pl.BlockSpec((block, LANES), row)]
            + [pl.BlockSpec((length, LANES), zero)] * 3,
            out_specs=[
                pl.BlockSpec((length, 3 * own), zero),
                pl.BlockSpec((1, 3 * own), zero),
            ],
            scratch_shapes=[
                pltpu.VMEM((own, length), BF16),
                pltpu.VMEM((length, own), F32),
                pltpu.VMEM((length, own), F32),
                pltpu.VMEM((heads, LANES, block), F32),
            ],
        ),
        compiler_params=pltpu.CompilerParams(vmem_limit_bytes=VMEM),
        cost_estimate=pl.CostEstimate(
            flops=10 * pairs * 2 * LANES, transcendentals=pairs, bytes_accessed=length * own * 20
        ),
    )(q, k, v, k, grad, mixed, logs, *tables)


def to_columns(rows, groups):
    parts = lax.axis_size("ctx")
    count, columns = rows.shape
    width = columns // (groups * parts)
    return (
        rows.reshape(count, groups, parts, width)
        .transpose(2, 0, 1, 3)
        .reshape(parts, count, groups * width)
    )


def exchange(blocks):
    return lax.all_to_all(blocks, "ctx", split_axis=0, concat_axis=0, tiled=True)


def gather_weights(qkv_weight, up_weight):
    u = to_columns(my_part(up_weight, 0), 1)
    q = to_columns(my_part(qkv_weight, 0), 3)
    u = exchange(u)
    u, q = lax.optimization_barrier((u, q))
    u_near = along_both((u, u))
    q = exchange(q)
    u_far = along_both(forwarded(u_near, 1))
    q, u_far = lax.optimization_barrier((q, u_far))
    q_near = along_both((q, q))
    return q, q_near, u, u_near, u_far


def reduce_input_grad(grad, own_rows, groups):
    grad = grad.reshape(lax.axis_size("ctx"), own_rows, grad.shape[1])
    part = exchange(lax.psum_scatter(grad, "dp", scatter_dimension=1, tiled=True))
    rows = lax.all_gather(part, "dp", axis=1, tiled=True)
    return (
        rows.reshape(rows.shape[0], own_rows, groups, -1)
        .transpose(1, 2, 0, 3)
        .reshape(own_rows, -1)
        .astype(F32)
    )


def per_device(
    tokens,
    positions,
    norm_gain,
    norm_bias,
    qkv_weight,
    qkv_bias,
    dense_weight,
    dense_bias,
    up_weight,
    up_bias,
    down_weight,
    down_bias,
    clip_limit,
    cotangent,
):
    seqs, stretch, width = tokens.shape
    heads = clip_limit.shape[0]
    head_dim = width // heads
    rows = seqs * stretch
    parts = lax.axis_size("ctx")
    part = lax.axis_index("ctx")
    own_heads = heads // parts
    own = own_heads * head_dim
    own_rows = qkv_weight.shape[0]
    own_ff = down_weight.shape[0]
    length = stretch * parts
    count = seqs * length
    scale = head_dim ** (-0.5)

    shared = lax.axis_size("dp") == 4
    cotangent_sum = jnp.sum(cotangent.astype(F32), axis=(0, 1))[None]
    digits = jnp.stack([positions // 32, positions % 32], axis=-1)
    marked = jnp.concatenate(
        [tokens, jnp.pad(digits.astype(BF16), ((0, 0), (0, 0), (0, LANES - 2)))], axis=-1
    )
    if shared:
        q, q_near, u, u_near, u_far = gather_weights(qkv_weight, up_weight)
        up_columns = full_rows(four_parts(u, u_near, u_far), own_rows)
        q_send = forwarded(after(q_near, up_columns), 1)
        q_far = along_both(q_send)
        marked = after(marked, u)
    else:
        q, u = exchange(to_columns(qkv_weight, 3)), exchange(to_columns(up_weight, 1))
        qkv_columns, up_columns = q.reshape(width, -1), u.reshape(width, -1)
    all_tokens = lax.all_gather(marked, "ctx", axis=1, tiled=True).reshape(count, width + LANES)
    grad_rows = lax.all_gather(
        after(cotangent, marked), "ctx", axis=1, tiled=True
    ).reshape(count, width)
    if shared:
        all_tokens = after(all_tokens, q_send)
    hidden, stats = normalize(all_tokens, norm_gain, norm_bias)
    digits = all_tokens[:, width : width + 2].astype(F32)
    places = (digits[:, 0] * 32.0 + digits[:, 1]).reshape(seqs, length)
    tables = [rotary_lanes(places[s]) for s in range(seqs)]
    if shared:
        q_far = after(q_far, hidden, tables)
        qkv_columns = full_rows(four_parts(q, q_near, q_far), own_rows)

    qkv_own_bias = take(qkv_bias.reshape(3, parts, own), part, 1, 1).reshape(1, 3 * own)
    up_own_bias = take(up_bias, part * own_ff, own_ff, 0)

    joined = dot(hidden, qkv_columns, (1, 0))
    block = 256 if length % 256 == 0 else length
    ahead = [
        attend(
            joined[s * length : (s + 1) * length], qkv_own_bias, tables[s], own_heads, scale, block
        )
        for s in range(seqs)
    ]
    attended = jnp.concatenate([a[4] for a in ahead])
    own_maxima = jnp.max(jnp.stack([a[6] for a in ahead]), axis=0)
    upward = dot(after(hidden, attended), up_columns, (1, 0)) + up_own_bias
    activated, gelu_back = jax.vjp(partial(jax.nn.gelu, approximate=True), upward)
    activated = activated.astype(BF16)

    def feed_forward_back(grad_rows):
        act_grad = dot(grad_rows, down_weight, (1, 1))
        up_low = gelu_back(act_grad)[0].astype(BF16)
        return up_low, dot(hidden, up_low, (0, 0)).astype(BF16)

    def attention_back(grad_rows):
        mixed_low = dot(grad_rows, dense_weight, (1, 1)).astype(BF16)
        back = [
            attend_back(
                q, k, v, mixed_low[s * length : (s + 1) * length], mixed, logs, tables[s],
                own_heads, scale, block,
            )
            for s, (q, k, v, mixed, low, logs, tops) in enumerate(ahead)
        ]
        joined_low = jnp.concatenate([b[0] for b in back])
        qkv_raw = dot(hidden, joined_low, (0, 0)).astype(BF16)
        return joined_low, sum(b[1] for b in back), qkv_raw

    def sum_branch(value):
        return lax.psum_scatter(
            value.reshape(seqs, length, width),
            "ctx",
            scatter_dimension=1,
            tiled=True,
        ).reshape(rows, width)

    def small_sums(shifts, joined_sum, up_sum):
        everyone = [shifts.reshape(1, 2 * width), cotangent_sum]
        return jnp.concatenate(everyone + [joined_sum, up_sum], axis=1), own_maxima

    def finish_rows(branch_sum, hidden_grad):
        return finish(
            tokens.reshape(rows, width),
            cotangent.reshape(rows, width),
            branch_sum,
            hidden_grad,
            norm_gain,
            dense_bias + down_bias,
        )

    def dp_step(small, bit):
        sums, tops = small
        got = swap(jnp.concatenate([sums, tops], axis=1), "dp", bit)
        cut = sums.shape[1]
        return sums + got[:, :cut], jnp.maximum(tops, got[:, cut:])

    def spread(small):
        value = jnp.concatenate(small, axis=1)
        return exchange(jnp.broadcast_to(value[None], (parts,) + value.shape))

    grad_rows, attended, activated = lax.optimization_barrier((grad_rows, attended, activated))
    mixed_out = jnp.concatenate([attended, activated], axis=1)
    out_raw = dot(mixed_out, grad_rows, (0, 0)).astype(BF16)
    if shared:
        together = lax.optimization_barrier
        o_got = along_both(o_send := outgoing(out_raw, 1))
        up_low, up_raw = feed_forward_back(after(grad_rows, o_send))
        up_raw = up_raw.reshape(parts, own_rows, own_ff)
        u_got = along_both(u_send := outgoing(up_raw, 1))
        branch = output_part(after(attended, u_send), dense_weight, activated, down_weight)
        branch_sum = sum_branch(branch)
        o_send, o_keep = first_sums(out_raw, after(o_got, branch), 1)
        o_got = along_both(o_send)
        joined_low, joined_sum, qkv_raw = attention_back(after(grad_rows, o_send))
        qkv_raw = qkv_raw.reshape(parts, own_rows, 3 * own)
        q_send = outgoing(qkv_raw, 1)
        q_send, u_got = together((q_send, u_got))
        q_got = along_both(q_send)
        u_send, u_keep = first_sums(up_raw, u_got, 1)
        u_send, o_got = together((u_send, o_got))
        u_got = along_both(u_send)
        o_part = second_sums(o_keep, o_got, 1)
        hidden_part, shifts, up_sum = input_part(
            after(joined_low, o_part), qkv_columns, up_low, up_columns, all_tokens, stats
        )
        small = small_sums(shifts, joined_sum, up_sum)
        u_part = second_sums(u_keep, after(u_got, shifts), 1)
        q_got, o_part, small = after((q_got, o_part, small), u_part)
        q_send, q_keep = first_sums(qkv_raw, q_got, 1)
        u_part = exchange(after(u_part, q_send))
        q_got = along_both(q_send)
        o_part, small = after((o_part, small), q_send)
        o_near = along_both((o_part, o_part))
        small = dp_step(small, 1)
        q_got, u_part, o_near, small = together((q_got, u_part, o_near, small))
        u_near = along_both((u_part, u_part))
        o_send = forwarded(o_near, 1)
        q_part = exchange(second_sums(q_keep, q_got, 1))
        o_far = along_both(o_send)
        small = dp_step(small, 2)
        u_near, q_part, o_far, small = together((u_near, q_part, o_far, small))
        hidden_grad = sum_branch(after(hidden_part, q_part))
        q_near = along_both((q_part, q_part))
        u_send = forwarded(u_near, 1)
        u_far = along_both(u_send)
        o_parts = four_parts(o_part, o_near, after(o_far, u_send))
        down_grad = full_columns(o_parts, own, own_ff, own)
        small = spread(after(small, down_grad))
        dense_grad = full_columns(after(o_parts, down_grad), 0, own, own)
        q_near, u_far, small, dense_grad = together((q_near, u_far, small, dense_grad))
        q_send = forwarded(q_near, 1)
        q_far = along_both(q_send)
        u_far, small = after((u_far, small), q_send)
        up_grad = full_grad(four_parts(u_part, u_near, u_far), own_rows, 1)
        small = after(small, up_grad)
        clipped = clip_columns(qkv_weight, qkv_bias, small, clip_limit, own_heads, head_dim)
        vectors = unpack(small, 3 * width, own, own_ff, own_heads)
        q_far, clipped, vectors = together((q_far, clipped, vectors))
        qkv_grad = full_grad(four_parts(q_part, q_near, q_far), own_rows, 3)
        ends = finish_rows(*after((branch_sum, hidden_grad), qkv_grad))
    else:
        up_low, up_raw = feed_forward_back(grad_rows)
        joined_low, joined_sum, qkv_raw = attention_back(grad_rows)
        branch_sum = sum_branch(output_part(attended, dense_weight, activated, down_weight))
        hidden_part, shifts, up_sum = input_part(
            joined_low, qkv_columns, up_low, up_columns, all_tokens, stats
        )
        hidden_grad = sum_branch(hidden_part)
        out_grad = lax.psum(out_raw, "dp").astype(F32)
        dense_grad, down_grad = out_grad[:own], out_grad[own:]
        up_grad = reduce_input_grad(up_raw, own_rows, 1)
        qkv_grad = reduce_input_grad(qkv_raw, own_rows, 3)
        small = small_sums(shifts, joined_sum, up_sum)
        small = spread((lax.psum(small[0], "dp"), lax.pmax(small[1], "dp")))
        clipped = clip_columns(qkv_weight, qkv_bias, small, clip_limit, own_heads, head_dim)
        vectors = unpack(small, 3 * width, own, own_ff, own_heads)
        ends = finish_rows(branch_sum, hidden_grad)
    layer_out, tokens_grad = ends
    clipped_weight, clipped_bias = clipped
    shifts, qkv_bias_grad, up_bias_grad, head_maxima = vectors
    return (
        layer_out.reshape(seqs, stretch, width),
        tokens_grad.reshape(seqs, stretch, width),
        shifts[0].reshape(width),
        shifts[1].reshape(width),
        qkv_grad,
        qkv_bias_grad.reshape(3 * width),
        dense_grad,
        shifts[2].reshape(width),
        up_grad,
        up_bias_grad.reshape(parts * own_ff),
        down_grad,
        shifts[2].reshape(width),
        head_maxima.reshape(heads),
        clipped_weight,
        clipped_bias.reshape(2 * width),
    )


def solution(mesh):
    rows = P("dp", "ctx", None)
    weight = P("ctx", None)
    in_specs = (rows, P("dp", "ctx"), P(), P()) + (weight, P()) * 4 + (P(), rows)
    out_specs = (
        (rows, rows, P(), P()) + (weight, P()) * 4 + (P(), weight, P())
    )
    return jax.shard_map(
        per_device, mesh=mesh, in_specs=in_specs, out_specs=out_specs, check_vma=False
    )
```

```python
from functools import partial

import jax
import jax.numpy as jnp
from jax import lax
from jax.experimental import pallas as pl
from jax.experimental.pallas import tpu as pltpu
from jax.sharding import PartitionSpec as P

ROT = 32
EPSILON = 1e-05
MASKED = -1e30
ROPE_BASE = 10000.0
BF16 = jnp.bfloat16
F32 = jnp.float32
LANES = 128
HEAD = 64
VMEM = 40 << 20
MOST_VMEM = 58 << 20
LIGHT = pl.CostEstimate(flops=1, transcendentals=0, bytes_accessed=1)


def dot(left, right, contract):
    return lax.dot_general(
        left, right, ((contract[:1], contract[1:]), ((), ())), preferred_element_type=F32
    )


def swap(value, axis, bit):
    return lax.ppermute(value, axis, [(i, i ^ bit) for i in range(lax.axis_size(axis))])


def take(value, start, size, axis):
    return lax.dynamic_slice_in_dim(value, start, size, axis)


def first_place(index):
    return (index & 1) * 2 + (index >> 1)


def my_part(value, axis):
    index = lax.axis_index("dp")
    size = value.shape[axis] // 8
    return jnp.concatenate(
        [
            take(value, first_place(index) * size, size, axis),
            take(value, (4 + index) * size, size, axis),
        ],
        axis,
    )


def after(value, *others):
    return lax.optimization_barrier((value, others))[0]


def along_both(pair):
    return swap(pair[0], "dp", 1), swap(pair[1], "dp", 2)


def plus(left, right):
    return (left.astype(F32) + right.astype(F32)).astype(BF16)


def outgoing(value, axis):
    index = lax.axis_index("dp")
    size = value.shape[axis] // 8
    return (
        take(value, (1 - (index & 1)) * 2 * size, 2 * size, axis),
        take(value, (4 + (1 - (index >> 1)) * 2) * size, 2 * size, axis),
    )


def dp_index():
    return lax.axis_index("dp").astype(jnp.int32).reshape(1)


def first_sums(value, received, axis):
    index = lax.axis_index("dp")
    low, high = index & 1, index >> 1
    size = value.shape[axis] // 8
    first = plus(take(value, low * 2 * size, 2 * size, axis), received[0])
    second = plus(take(value, (4 + high * 2) * size, 2 * size, axis), received[1])
    send = (
        take(second, (1 - low) * size, size, axis),
        take(first, (1 - high) * size, size, axis),
    )
    keep = jnp.concatenate(
        [take(first, high * size, size, axis), take(second, low * size, size, axis)], axis
    )
    return send, keep


def second_sums(keep, received, axis):
    return plus(keep, jnp.concatenate([received[1], received[0]], axis))


def normalize_kernel(tokens, gain, shift, hidden, stats):
    value = tokens[...].astype(F32)
    mean = jnp.mean(value, axis=1, keepdims=True)
    centre = value - mean
    inv_std = lax.rsqrt(jnp.mean(centre * centre, axis=1, keepdims=True) + EPSILON)
    hidden[...] = (centre * inv_std * gain[...] + shift[...]).astype(BF16)
    lane = lax.broadcasted_iota(jnp.int32, stats.shape, 1)
    stats[...] = jnp.where(lane == 0, mean, inv_std)


def normalize(tokens, gain, shift):
    count, width = tokens.shape[0], gain.shape[0]
    block = 256 if count % 256 == 0 else count
    row = lambda i: (i, 0)
    return pl.pallas_call(
        normalize_kernel,
        name="normalize",
        out_shape=[
            jax.ShapeDtypeStruct((count, width), BF16),
            jax.ShapeDtypeStruct((count, LANES), F32),
        ],
        grid=(count // block,),
        in_specs=[pl.BlockSpec((block, width), row)]
        + [pl.BlockSpec((1, width), lambda i: (0, 0))] * 2,
        out_specs=[pl.BlockSpec((block, width), row), pl.BlockSpec((block, LANES), row)],
        compiler_params=pltpu.CompilerParams(vmem_limit_bytes=VMEM),
        cost_estimate=LIGHT,
    )(tokens, gain[None], shift[None])


def output_kernel(attended, dense, activated, down, out):
    out[...] = (nn(attended[...], dense[...]) + nn(activated[...], down[...])).astype(BF16)


def output_part(attended, dense, activated, down):
    count, width = attended.shape[0], dense.shape[1]
    block = 256
    fixed = lambda i: (0, 0)
    column = lambda i: (0, i)
    return pl.pallas_call(
        output_kernel,
        name="output_part",
        out_shape=jax.ShapeDtypeStruct((count, width), BF16),
        grid=(width // block,),
        in_specs=[
            pl.BlockSpec(attended.shape, fixed),
            pl.BlockSpec((dense.shape[0], block), column),
            pl.BlockSpec(activated.shape, fixed),
            pl.BlockSpec((down.shape[0], block), column),
        ],
        out_specs=pl.BlockSpec((count, block), column),
        compiler_params=pltpu.CompilerParams(vmem_limit_bytes=VMEM),
        cost_estimate=LIGHT,
    )(attended, dense, activated, down)


def input_kernel(joined, qkv, upward, up, tokens, stats, out, sums, up_sum):
    total = nt(joined[...], qkv[...]) + nt(upward[...], up[...])
    out[...] = total.astype(BF16)
    xhat = (tokens[...].astype(F32) - stats[:, 0:1]) * stats[:, 1:2]
    sums[0:1, :] = jnp.sum(total * xhat, axis=0, keepdims=True)
    sums[1:2, :] = jnp.sum(total, axis=0, keepdims=True)

    @pl.when(pl.program_id(0) == 0)
    def _():
        up_sum[...] = jnp.sum(upward[...].astype(F32), axis=0, keepdims=True)


def input_part(joined, qkv, upward, up, tokens, stats):
    count, width = tokens.shape[0], qkv.shape[0]
    block = 256
    fixed = lambda i: (0, 0)
    column = lambda i: (0, i)
    row = lambda i: (i, 0)
    return pl.pallas_call(
        input_kernel,
        name="input_part",
        out_shape=[
            jax.ShapeDtypeStruct((count, width), BF16),
            jax.ShapeDtypeStruct((2, width), F32),
            jax.ShapeDtypeStruct((1, upward.shape[1]), F32),
        ],
        grid=(width // block,),
        in_specs=[
            pl.BlockSpec(joined.shape, fixed),
            pl.BlockSpec((block, qkv.shape[1]), row),
            pl.BlockSpec(upward.shape, fixed),
            pl.BlockSpec((block, up.shape[1]), row),
            pl.BlockSpec((count, block), column),
            pl.BlockSpec(stats.shape, fixed),
        ],
        out_specs=[
            pl.BlockSpec((count, block), column),
            pl.BlockSpec((2, block), column),
            pl.BlockSpec((1, upward.shape[1]), fixed),
        ],
        compiler_params=pltpu.CompilerParams(vmem_limit_bytes=VMEM),
        cost_estimate=LIGHT,
    )(joined, qkv, upward, up, tokens, stats)


def finish_kernel(tokens, cotangent, branch, grad, gain, bias, out, tokens_grad):
    value = tokens[...].astype(F32)
    out[...] = (value + branch[...].astype(F32) + bias[...]).astype(BF16)
    centre = value - jnp.mean(value, axis=1, keepdims=True)
    inv_std = lax.rsqrt(jnp.mean(centre * centre, axis=1, keepdims=True) + EPSILON)
    xhat = centre * inv_std
    scaled = grad[...].astype(F32) * gain[...]
    inner = jnp.mean(scaled * xhat, axis=1, keepdims=True)
    scaled = scaled - jnp.mean(scaled, axis=1, keepdims=True) - xhat * inner
    tokens_grad[...] = cotangent[...].astype(F32) + inv_std * scaled


def finish(tokens, cotangent, branch, grad, gain, bias):
    rows, width = tokens.shape
    block = 64 if rows % 64 == 0 else rows
    row = pl.BlockSpec((block, width), lambda i: (i, 0))
    vector = pl.BlockSpec((1, width), lambda i: (0, 0))
    return pl.pallas_call(
        finish_kernel,
        name="finish",
        out_shape=[
            jax.ShapeDtypeStruct((rows, width), BF16),
            jax.ShapeDtypeStruct((rows, width), F32),
        ],
        grid=(rows // block,),
        in_specs=[row] * 4 + [vector] * 2,
        out_specs=[row, row],
        compiler_params=pltpu.CompilerParams(vmem_limit_bytes=VMEM),
        cost_estimate=LIGHT,
    )(tokens, cotangent, branch, grad, gain[None], bias[None])


def clip_kernel(own_heads, head_dim, tops, limits, weight, bias, out, bias_out):
    parts = tops.shape[0]
    heads = parts * own_heads
    first = lax.rem(pl.program_id(0) * (out.shape[1] // head_dim), heads)
    lane = lax.broadcasted_iota(jnp.int32, (1, LANES), 1)
    head = first + lax.broadcasted_iota(jnp.int32, (1, out.shape[1]), 1) // head_dim
    scale = jnp.zeros((1, out.shape[1]), F32)
    for part in range(parts):
        limit = limits[part : part + 1, :]
        factor = jnp.sqrt(limit / jnp.maximum(tops[part], limit))
        for h in range(own_heads):
            one = jnp.sum(jnp.where(lane == h, factor, 0.0), axis=1, keepdims=True)
            scale = jnp.where(head == part * own_heads + h, one, scale)
    out[...] = weight[...].astype(F32) * scale
    bias_out[...] = bias[...] * scale


def clip_columns(weight, bias, small, limits, own_heads, head_dim):
    rows, parts = weight.shape[0], small.shape[0]
    columns = 2 * parts * own_heads * head_dim
    block = columns // 4
    column = lambda i: (0, i)
    wide, thin = pl.BlockSpec((rows, block), column), pl.BlockSpec((1, block), column)
    limits = jnp.pad(
        limits.astype(F32).reshape(parts, own_heads),
        ((0, 0), (0, LANES - own_heads)),
        constant_values=1.0,
    )
    return pl.pallas_call(
        partial(clip_kernel, own_heads, head_dim),
        name="clip_columns",
        out_shape=[
            jax.ShapeDtypeStruct((rows, columns), F32),
            jax.ShapeDtypeStruct((1, columns), F32),
        ],
        grid=(columns // block,),
        in_specs=[
            pl.BlockSpec((parts, 1, LANES), lambda i: (0, 0, small.shape[2] // LANES - 1)),
            pl.BlockSpec((parts, LANES), lambda i: (0, 0)),
            wide,
            thin,
        ],
        out_specs=[wide, thin],
        compiler_params=pltpu.CompilerParams(vmem_limit_bytes=VMEM),
        cost_estimate=LIGHT,
    )(small, limits, weight, bias[None])


def unpack_kernel(common, own, own_ff, own_heads, small, *outs):
    *shifts, qkv_bias, up_bias, maxima = outs
    parts = small.shape[0]
    width = common // len(shifts)
    for i, out in enumerate(shifts):
        total = small[0, :, i * width : (i + 1) * width]
        for part in range(1, parts):
            total = total + small[part, :, i * width : (i + 1) * width]
        out[...] = total
    lane = lax.broadcasted_iota(jnp.int32, maxima.shape, 1)
    tops = jnp.zeros(maxima.shape, F32)
    for part in range(parts):
        for group in range(3):
            spot = (group * parts + part) * own
            qkv_bias[:, spot : spot + own] = small[
                part, :, common + group * own : common + (group + 1) * own
            ]
        start = common + 3 * own
        up_bias[:, part * own_ff : (part + 1) * own_ff] = small[part, :, start : start + own_ff]
        for h in range(own_heads):
            one = small[part, :, start + own_ff + h : start + own_ff + h + 1]
            tops = jnp.where(lane == part * own_heads + h, one, tops)
    maxima[...] = tops


def unpack(small, common, own, own_ff, own_heads):
    parts = small.shape[0]
    shapes = [common // 3] * 3 + [3 * parts * own, parts * own_ff, parts * own_heads]
    *shifts, qkv_bias, up_bias, maxima = pl.pallas_call(
        partial(unpack_kernel, common, own, own_ff, own_heads),
        name="unpack",
        out_shape=[jax.ShapeDtypeStruct((1, n), F32) for n in shapes],
        compiler_params=pltpu.CompilerParams(vmem_limit_bytes=VMEM),
        cost_estimate=LIGHT,
    )(small)
    return shifts, qkv_bias, up_bias, maxima


def forwarded(received, axis):
    half = received[0].shape[axis] // 2
    return (
        lax.slice_in_dim(received[1], 0, half, axis=axis),
        lax.slice_in_dim(received[0], half, 2 * half, axis=axis),
    )


def four_parts(part, near, far):
    return [part, near[0], near[1], far[0], far[1]]


def pieces_of(index_ref, refs, eighth, axis):
    me = index_ref[0]
    first = (slice(None),) * axis + (slice(0, eighth),)
    second = (slice(None),) * axis + (slice(eighth, 2 * eighth),)
    for offset in range(3):
        owner = me ^ offset
        yield first_place(owner), refs[offset], first
        yield 4 + owner, refs[offset], second
    if len(refs) > 3:
        owner = me ^ 3
        yield first_place(owner), refs[3], first
        yield 4 + owner, refs[4], first


def place_rows(index_ref, *refs):
    out = refs[-1]
    blocks, size, width = refs[0].shape
    for spot, ref, cut in pieces_of(index_ref, refs[:-1], size // 2, 1):
        rows = pl.ds(pl.multiple_of(spot * (size // 2), size // 2), size // 2)
        for i in range(blocks):
            out[rows, i * width : (i + 1) * width] = ref[(i,) + cut[1:]].astype(out.dtype)


def place_columns(index_ref, *refs):
    out = refs[-1]
    eighth = refs[0].shape[1] // 2
    for spot, ref, cut in pieces_of(index_ref, refs[:-1], eighth, 1):
        columns = pl.ds(pl.multiple_of(spot * eighth, eighth), eighth)
        out[:, columns] = ref[cut].astype(out.dtype)


def place(
    body, vmem, parts, axis, grid, in_block, in_map, out_shape, out_block, out_map, cost=LIGHT
):
    half = list(in_block)
    half[axis] //= 2
    return pl.pallas_call(
        body,
        out_shape=out_shape,
        grid_spec=pltpu.PrefetchScalarGridSpec(
            num_scalar_prefetch=1,
            grid=grid,
            in_specs=[pl.BlockSpec(in_block, in_map)] * 3
            + [pl.BlockSpec(tuple(half), in_map)] * (len(parts) - 3),
            out_specs=pl.BlockSpec(out_block, out_map),
        ),
        compiler_params=pltpu.CompilerParams(vmem_limit_bytes=vmem),
        cost_estimate=cost,
    )(dp_index(), *parts)


def full_rows(parts, own_rows):
    blocks, size, columns = parts[0].shape
    return place(
        place_rows,
        VMEM,
        parts,
        1,
        (blocks,),
        (1, size, columns),
        lambda i, index: (i, 0, 0),
        jax.ShapeDtypeStruct((blocks * own_rows, columns), parts[0].dtype),
        (own_rows, columns),
        lambda i, index: (i, 0),
    )


def full_grad(parts, own_rows, groups, cost=LIGHT):
    blocks, size, columns = parts[0].shape
    width = columns // groups
    several = max(1, min(blocks, 1024 // width))
    steps = blocks // several
    return place(
        place_rows,
        MOST_VMEM,
        parts,
        1,
        (groups, steps),
        (several, size, width),
        lambda g, i, index: (i, 0, g),
        jax.ShapeDtypeStruct((own_rows, groups * blocks * width), F32),
        (own_rows, several * width),
        lambda g, i, index: (0, g * steps + i),
        cost,
    )


def full_columns(parts, first, count, block):
    size = parts[0].shape[1]
    return place(
        place_columns,
        MOST_VMEM,
        parts,
        1,
        (count // block,),
        (block, size),
        lambda i, index: (i + first // block, 0),
        jax.ShapeDtypeStruct((count, 4 * size), F32),
        (block, 4 * size),
        lambda i, index: (i, 0),
    )


def rotary_lanes(positions):
    half = ROT // 2
    lane = jnp.arange(LANES, dtype=jnp.int32) % HEAD
    frequency = ROPE_BASE ** (-((lane % half).astype(F32) * 2.0 / ROT))
    angles = positions.astype(F32)[:, None] * frequency
    sine = jnp.sin(angles)
    return (
        jnp.where(lane < ROT, jnp.cos(angles), 1.0),
        jnp.where(lane < half, -sine, 0.0),
        jnp.where((lane >= half) & (lane < ROT), sine, 0.0),
    )


def turn(value, cosine, above, below, sign):
    half = ROT // 2
    size = value.shape[1]
    from_above = pltpu.roll(value, size - half, 1)
    from_below = pltpu.roll(value, half, 1)
    return value * cosine + sign * (from_above * above + from_below * below)


def nt(left, right):
    return lax.dot_general(left, right, (((1,), (1,)), ((), ())), preferred_element_type=F32)


def nn(left, right):
    return lax.dot_general(left, right, (((1,), (0,)), ((), ())), preferred_element_type=F32)


def pair_of(head):
    return slice(head // 2 * LANES, head // 2 * LANES + LANES)


def only(value, head):
    lane = lax.broadcasted_iota(jnp.int32, value.shape, 1)
    return jnp.where((lane // HEAD) == head % 2, value, jnp.zeros_like(value))


def fold(value, op):
    out = value[:, :LANES]
    for start in range(LANES, value.shape[1], LANES):
        out = op(out, value[:, start : start + LANES])
    return out


def attend_kernel(
    heads, scale, joined, bias, cosine, above, below,
    q_out, k_out, v_out, mixed_out, low_out, log_out, max_out,
    k_all, v_all, scores, total,
):
    step = pl.program_id(0)
    block, own = q_out.shape
    copies = own // LANES
    tables = [jnp.concatenate([t[...]] * copies, axis=1) for t in (cosine, above, below)]
    q = turn(joined[:, :own] + bias[:, :own], *tables, 1.0).astype(BF16)
    k = turn(joined[:, own : 2 * own] + bias[:, own : 2 * own], *tables, 1.0).astype(BF16)
    v = (joined[:, 2 * own :] + bias[:, 2 * own :]).astype(BF16)
    q_out[...] = q
    k_out[...] = k
    v_out[...] = v
    here = pl.ds(pl.multiple_of(step * block, block), block)
    k_all[here, :] = k
    v_all[here, :] = v
    queries = [only(q[:, pair_of(h)], h) * jnp.asarray(scale, BF16) for h in range(heads)]
    allowed = lax.broadcasted_iota(jnp.int32, (block, block), 0) >= lax.broadcasted_iota(
        jnp.int32, (block, block), 1
    )

    def score(j, peaks, diagonal):
        spot = pl.ds(pl.multiple_of(j * block, block), block)
        out = []
        for h in range(heads):
            s = nt(queries[h], k_all[spot, pair_of(h)])
            if diagonal:
                s = jnp.where(allowed, s, MASKED)
            scores[h, :, spot] = s
            out.append(jnp.maximum(peaks[h], fold(s, jnp.maximum)))
        return out

    peaks = [jnp.full((block, LANES), MASKED, F32)] * heads
    peaks = lax.fori_loop(0, step, lambda j, c: score(j, c, False), peaks)
    peaks = score(step, peaks, True)
    peaks = [jnp.max(p, axis=1, keepdims=True) for p in peaks]
    total[...] = jnp.zeros_like(total)

    def gather(j, sums):
        spot = pl.ds(pl.multiple_of(j * block, block), block)
        out = []
        for h in range(heads):
            p = jnp.exp(scores[h, :, spot] - peaks[h])
            out.append(sums[h] + fold(p, jnp.add))
            total[h] += nn(p.astype(BF16), v_all[spot, pair_of(h)])
        return out

    sums = lax.fori_loop(0, step + 1, gather, [jnp.zeros((block, LANES), F32)] * heads)
    lane = lax.broadcasted_iota(jnp.int32, (block, LANES), 1)
    logs = jnp.zeros((block, LANES), F32)
    tops = jnp.full((1, LANES), MASKED, F32)
    for h in range(heads):
        amount = jnp.sum(sums[h], axis=1, keepdims=True)
        total[h] = total[h] / amount
        logs = jnp.where(lane == h, peaks[h] + jnp.log(amount), logs)
        tops = jnp.where(lane[:1] == h, jnp.max(peaks[h], axis=0, keepdims=True), tops)
    log_out[...] = logs
    for h in range(0, heads, 2):
        mixed = jnp.where(lane < HEAD, total[h], total[h + 1])
        mixed_out[:, pair_of(h)] = mixed
        low_out[:, pair_of(h)] = mixed.astype(BF16)

    @pl.when(step == 0)
    def _():
        max_out[...] = tops

    @pl.when(step > 0)
    def _():
        max_out[...] = jnp.maximum(max_out[...], tops)


def attend(joined, bias, tables, heads, scale, block):
    length = joined.shape[0]
    own = joined.shape[1] // 3
    row = lambda i: (i, 0)
    zero = lambda i: (0, 0)
    shapes = [
        ((length, own), BF16), ((length, own), BF16), ((length, own), BF16),
        ((length, own), F32), ((length, own), BF16), ((length, LANES), F32),
    ]
    pairs = heads * length * length // 2
    return pl.pallas_call(
        partial(attend_kernel, heads, scale),
        name="attend",
        out_shape=[pltpu.HBM(s, d) for s, d in shapes] + [jax.ShapeDtypeStruct((1, LANES), F32)],
        grid_spec=pltpu.PrefetchScalarGridSpec(
            num_scalar_prefetch=0,
            grid=(length // block,),
            in_specs=[pl.BlockSpec((block, 3 * own), row), pl.BlockSpec((1, 3 * own), zero)]
            + [pl.BlockSpec((block, LANES), row)] * 3,
            out_specs=[pl.BlockSpec((block, s[1]), row) for s, d in shapes]
            + [pl.BlockSpec((1, LANES), zero)],
            scratch_shapes=[
                pltpu.VMEM((length, own), BF16),
                pltpu.VMEM((length, own), BF16),
                pltpu.VMEM((heads, block, length), F32),
                pltpu.VMEM((heads, block, LANES), F32),
            ],
        ),
        compiler_params=pltpu.CompilerParams(vmem_limit_bytes=VMEM),
        cost_estimate=pl.CostEstimate(
            flops=4 * pairs * 2 * LANES, transcendentals=pairs, bytes_accessed=length * own * 26
        ),
    )(joined, bias, *tables)


def attend_back_kernel(
    heads, scale, q, k, v, k_here, grad, mixed, logs, cosine, above, below,
    low_out, sum_out, k_turned, k_total, v_total, q_total,
):
    step = pl.program_id(0)
    block, own = q.shape
    length = k.shape[0]
    copies = own // LANES
    spot_here = pl.ds(pl.multiple_of(step * block, block), block)

    @pl.when(step == 0)
    def _():
        k_total[...] = jnp.zeros_like(k_total)
        v_total[...] = jnp.zeros_like(v_total)

    k_turned[:, spot_here] = k_here[...].T
    q_total[...] = jnp.zeros_like(q_total)
    log_rows = logs[...].T
    product = grad[...].astype(F32) * mixed[...]
    lane = lax.broadcasted_iota(jnp.int32, (block, LANES), 1)
    deltas = jnp.zeros((block, LANES), F32)
    for h in range(heads):
        own_sum = jnp.sum(only(product[:, pair_of(h)], h), axis=1, keepdims=True)
        deltas = jnp.where(lane == h, own_sum, deltas)
    delta_rows = deltas.T
    queries = [only(q[:, pair_of(h)], h) * jnp.asarray(scale, BF16) for h in range(heads)]
    grads = [only(grad[:, pair_of(h)], h) for h in range(heads)]
    allowed = lax.broadcasted_iota(jnp.int32, (block, block), 0) <= lax.broadcasted_iota(
        jnp.int32, (block, block), 1
    )

    def visit(j, diagonal):
        spot = pl.ds(pl.multiple_of(j * block, block), block)
        for h in range(heads):
            s = nt(k[spot, pair_of(h)], queries[h])
            if diagonal:
                s = jnp.where(allowed, s, MASKED)
            p = jnp.exp(s - log_rows[h : h + 1])
            dp = nt(v[spot, pair_of(h)], grads[h])
            ds = (p * (dp - delta_rows[h : h + 1])).astype(BF16)
            v_total[spot, pair_of(h)] += nn(p.astype(BF16), grads[h])
            k_total[spot, pair_of(h)] += nn(ds, queries[h])
            q_total[h] += nn(k_turned[pair_of(h), spot], ds)

    def body(j, carry):
        visit(j, False)
        return carry

    lax.fori_loop(0, step, body, 0)
    visit(step, True)
    row = lax.broadcasted_iota(jnp.int32, (LANES, block), 0)
    tables = (cosine[spot_here, :], above[spot_here, :], below[spot_here, :])
    sums = []
    for h in range(0, heads, 2):
        dq = jnp.where(row < HEAD, q_total[h], q_total[h + 1]).T * scale
        low = turn(dq, *tables, -1.0).astype(BF16)
        low_out[spot_here, pair_of(h)] = low
        sums.append(jnp.sum(low.astype(F32), axis=0, keepdims=True))
    sums = jnp.concatenate(sums, axis=1)

    @pl.when(step == 0)
    def _():
        sum_out[:, :own] = sums

    @pl.when(step > 0)
    def _():
        sum_out[:, :own] += sums

    @pl.when(step == length // block - 1)
    def _():
        wide = [jnp.concatenate([t[...]] * copies, axis=1) for t in (cosine, above, below)]
        low = turn(k_total[...], *wide, -1.0).astype(BF16)
        low_out[:, own : 2 * own] = low
        sum_out[:, own : 2 * own] = jnp.sum(low.astype(F32), axis=0, keepdims=True)
        low = v_total[...].astype(BF16)
        low_out[:, 2 * own :] = low
        sum_out[:, 2 * own :] = jnp.sum(low.astype(F32), axis=0, keepdims=True)


def attend_back(q, k, v, grad, mixed, logs, tables, heads, scale, block):
    length, own = q.shape
    row = lambda i: (i, 0)
    zero = lambda i: (0, 0)
    rows = pl.BlockSpec((block, own), row)
    whole = pl.BlockSpec((length, own), zero)
    pairs = heads * length * length // 2
    return pl.pallas_call(
        partial(attend_back_kernel, heads, scale),
        name="attend_back",
        out_shape=[
            jax.ShapeDtypeStruct((length, 3 * own), BF16),
            jax.ShapeDtypeStruct((1, 3 * own), F32),
        ],
        grid_spec=pltpu.PrefetchScalarGridSpec(
            num_scalar_prefetch=0,
            grid=(length // block,),
            in_specs=[rows, whole, whole, rows, rows, rows, pl.BlockSpec((block, LANES), row)]
            + [pl.BlockSpec((length, LANES), zero)] * 3,
            out_specs=[
                pl.BlockSpec((length, 3 * own), zero),
                pl.BlockSpec((1, 3 * own), zero),
            ],
            scratch_shapes=[
                pltpu.VMEM((own, length), BF16),
                pltpu.VMEM((length, own), F32),
                pltpu.VMEM((length, own), F32),
                pltpu.VMEM((heads, LANES, block), F32),
            ],
        ),
        compiler_params=pltpu.CompilerParams(vmem_limit_bytes=VMEM),
        cost_estimate=pl.CostEstimate(
            flops=10 * pairs * 2 * LANES, transcendentals=pairs, bytes_accessed=length * own * 20
        ),
    )(q, k, v, k, grad, mixed, logs, *tables)


def to_columns(rows, groups):
    parts = lax.axis_size("ctx")
    count, columns = rows.shape
    width = columns // (groups * parts)
    return (
        rows.reshape(count, groups, parts, width)
        .transpose(2, 0, 1, 3)
        .reshape(parts, count, groups * width)
    )


def exchange(blocks):
    return lax.all_to_all(blocks, "ctx", split_axis=0, concat_axis=0, tiled=True)


def gather_weights(qkv_weight, up_weight):
    u = to_columns(my_part(up_weight, 0), 1)
    q = to_columns(my_part(qkv_weight, 0), 3)
    u = exchange(u)
    u, q = lax.optimization_barrier((u, q))
    u_near = along_both((u, u))
    q = exchange(q)
    u_far = along_both(forwarded(u_near, 1))
    q, u_far = lax.optimization_barrier((q, u_far))
    q_near = along_both((q, q))
    return q, q_near, u, u_near, u_far


def reduce_input_grad(grad, own_rows, groups):
    grad = grad.reshape(lax.axis_size("ctx"), own_rows, grad.shape[1])
    part = exchange(lax.psum_scatter(grad, "dp", scatter_dimension=1, tiled=True))
    rows = lax.all_gather(part, "dp", axis=1, tiled=True)
    return (
        rows.reshape(rows.shape[0], own_rows, groups, -1)
        .transpose(1, 2, 0, 3)
        .reshape(own_rows, -1)
        .astype(F32)
    )


def per_device(
    tokens,
    positions,
    norm_gain,
    norm_bias,
    qkv_weight,
    qkv_bias,
    dense_weight,
    dense_bias,
    up_weight,
    up_bias,
    down_weight,
    down_bias,
    clip_limit,
    cotangent,
):
    seqs, stretch, width = tokens.shape
    heads = clip_limit.shape[0]
    head_dim = width // heads
    rows = seqs * stretch
    parts = lax.axis_size("ctx")
    part = lax.axis_index("ctx")
    own_heads = heads // parts
    own = own_heads * head_dim
    own_rows = qkv_weight.shape[0]
    own_ff = down_weight.shape[0]
    length = stretch * parts
    count = seqs * length
    scale = head_dim ** (-0.5)

    shared = lax.axis_size("dp") == 4
    cotangent_sum = jnp.sum(cotangent.astype(F32), axis=(0, 1))[None]
    digits = jnp.stack([positions // 32, positions % 32], axis=-1)
    marked = jnp.concatenate(
        [tokens, jnp.pad(digits.astype(BF16), ((0, 0), (0, 0), (0, LANES - 2)))], axis=-1
    )
    if shared:
        q, q_near, u, u_near, u_far = gather_weights(qkv_weight, up_weight)
        up_columns = full_rows(four_parts(u, u_near, u_far), own_rows)
        q_send = forwarded(after(q_near, up_columns), 1)
        q_far = along_both(q_send)
        marked = after(marked, u)
    else:
        q, u = exchange(to_columns(qkv_weight, 3)), exchange(to_columns(up_weight, 1))
        qkv_columns, up_columns = q.reshape(width, -1), u.reshape(width, -1)
    all_tokens = lax.all_gather(marked, "ctx", axis=1, tiled=True).reshape(count, width + LANES)
    grad_rows = lax.all_gather(
        after(cotangent, marked), "ctx", axis=1, tiled=True
    ).reshape(count, width)
    if shared:
        all_tokens = after(all_tokens, q_send)
    hidden, stats = normalize(all_tokens, norm_gain, norm_bias)
    digits = all_tokens[:, width : width + 2].astype(F32)
    places = (digits[:, 0] * 32.0 + digits[:, 1]).reshape(seqs, length)
    tables = [rotary_lanes(places[s]) for s in range(seqs)]
    if shared:
        q_far = after(q_far, hidden, tables)
        qkv_columns = full_rows(four_parts(q, q_near, q_far), own_rows)

    qkv_own_bias = take(qkv_bias.reshape(3, parts, own), part, 1, 1).reshape(1, 3 * own)
    up_own_bias = take(up_bias, part * own_ff, own_ff, 0)

    joined = dot(hidden, qkv_columns, (1, 0))
    block = 256 if length % 256 == 0 else length
    ahead = [
        attend(
            joined[s * length : (s + 1) * length], qkv_own_bias, tables[s], own_heads, scale, block
        )
        for s in range(seqs)
    ]
    attended = jnp.concatenate([a[4] for a in ahead])
    own_maxima = jnp.max(jnp.stack([a[6] for a in ahead]), axis=0)
    upward = dot(after(hidden, attended), up_columns, (1, 0)) + up_own_bias
    activated, gelu_back = jax.vjp(partial(jax.nn.gelu, approximate=True), upward)
    activated = activated.astype(BF16)

    def feed_forward_back(grad_rows):
        act_grad = dot(grad_rows, down_weight, (1, 1))
        up_low = gelu_back(act_grad)[0].astype(BF16)
        return up_low, dot(hidden, up_low, (0, 0)).astype(BF16)

    def attention_back(grad_rows):
        mixed_low = dot(grad_rows, dense_weight, (1, 1)).astype(BF16)
        back = [
            attend_back(
                q, k, v, mixed_low[s * length : (s + 1) * length], mixed, logs, tables[s],
                own_heads, scale, block,
            )
            for s, (q, k, v, mixed, low, logs, tops) in enumerate(ahead)
        ]
        joined_low = jnp.concatenate([b[0] for b in back])
        qkv_raw = dot(hidden, joined_low, (0, 0)).astype(BF16)
        return joined_low, sum(b[1] for b in back), qkv_raw

    def sum_branch(value):
        return lax.psum_scatter(
            value.reshape(seqs, length, width),
            "ctx",
            scatter_dimension=1,
            tiled=True,
        ).reshape(rows, width)

    def small_sums(shifts, joined_sum, up_sum):
        everyone = [shifts.reshape(1, 2 * width), cotangent_sum]
        return jnp.concatenate(everyone + [joined_sum, up_sum], axis=1), own_maxima

    def finish_rows(branch_sum, hidden_grad):
        return finish(
            tokens.reshape(rows, width),
            cotangent.reshape(rows, width),
            branch_sum,
            hidden_grad,
            norm_gain,
            dense_bias + down_bias,
        )

    def dp_step(small, bit):
        sums, tops = small
        got = swap(jnp.concatenate([sums, tops], axis=1), "dp", bit)
        cut = sums.shape[1]
        return sums + got[:, :cut], jnp.maximum(tops, got[:, cut:])

    def spread(small):
        value = jnp.concatenate(small, axis=1)
        return exchange(jnp.broadcast_to(value[None], (parts,) + value.shape))

    grad_rows, attended, activated = lax.optimization_barrier((grad_rows, attended, activated))
    mixed_out = jnp.concatenate([attended, activated], axis=1)
    out_raw = dot(mixed_out, grad_rows, (0, 0)).astype(BF16)
    if shared:
        together = lax.optimization_barrier
        o_got = along_both(o_send := outgoing(out_raw, 1))
        up_low, up_raw = feed_forward_back(after(grad_rows, o_send))
        up_raw = up_raw.reshape(parts, own_rows, own_ff)
        u_got = along_both(u_send := outgoing(up_raw, 1))
        branch = output_part(after(attended, u_send), dense_weight, activated, down_weight)
        branch_sum = sum_branch(branch)
        o_send, o_keep = first_sums(out_raw, after(o_got, branch), 1)
        o_got = along_both(o_send)
        joined_low, joined_sum, qkv_raw = attention_back(after(grad_rows, o_send))
        qkv_raw = qkv_raw.reshape(parts, own_rows, 3 * own)
        q_send = outgoing(qkv_raw, 1)
        q_send, u_got = together((q_send, u_got))
        q_got = along_both(q_send)
        u_send, u_keep = first_sums(up_raw, u_got, 1)
        u_send, o_got = together((u_send, o_got))
        u_got = along_both(u_send)
        o_part = second_sums(o_keep, o_got, 1)
        hidden_part, shifts, up_sum = input_part(
            after(joined_low, o_part), qkv_columns, up_low, up_columns, all_tokens, stats
        )
        small = small_sums(shifts, joined_sum, up_sum)
        u_part = second_sums(u_keep, after(u_got, shifts), 1)
        q_got, o_part, small = after((q_got, o_part, small), u_part)
        q_send, q_keep = first_sums(qkv_raw, q_got, 1)
        u_part = exchange(after(u_part, q_send))
        q_got = along_both(q_send)
        o_part, small = after((o_part, small), q_send)
        o_near = along_both((o_part, o_part))
        small = dp_step(small, 1)
        q_got, u_part, o_near, small = together((q_got, u_part, o_near, small))
        u_near = along_both((u_part, u_part))
        o_send = forwarded(o_near, 1)
        q_part = exchange(second_sums(q_keep, q_got, 1))
        o_far = along_both(o_send)
        small = dp_step(small, 2)
        u_near, q_part, o_far, small = together((u_near, q_part, o_far, small))
        hidden_grad = sum_branch(after(hidden_part, q_part))
        q_near = along_both((q_part, q_part))
        u_send = forwarded(u_near, 1)
        u_far = along_both(u_send)
        o_parts = four_parts(o_part, o_near, after(o_far, u_send))
        down_grad = full_columns(o_parts, own, own_ff, own)
        small = spread(after(small, u_send))
        dense_grad = full_columns(after(o_parts, down_grad), 0, own, own)
        small = after(small, dense_grad)
        clipped = clip_columns(qkv_weight, qkv_bias, small, clip_limit, own_heads, head_dim)
        small, clipped = together((small, clipped))
        q_near, u_far, small, dense_grad = together((q_near, u_far, small, dense_grad))
        q_send = forwarded(q_near, 1)
        q_far = along_both(q_send)
        u_far, small = after((u_far, small), q_send)
        up_grad = full_grad(four_parts(u_part, u_near, u_far), own_rows, 1)
        small = after(small, up_grad)
        vectors = unpack(small, 3 * width, own, own_ff, own_heads)
        q_far, clipped, vectors = together((q_far, clipped, vectors))
        qkv_grad = full_grad(four_parts(q_part, q_near, q_far), own_rows, 3)
        ends = finish_rows(*after((branch_sum, hidden_grad), qkv_grad))
    else:
        up_low, up_raw = feed_forward_back(grad_rows)
        joined_low, joined_sum, qkv_raw = attention_back(grad_rows)
        branch_sum = sum_branch(output_part(attended, dense_weight, activated, down_weight))
        hidden_part, shifts, up_sum = input_part(
            joined_low, qkv_columns, up_low, up_columns, all_tokens, stats
        )
        hidden_grad = sum_branch(hidden_part)
        out_grad = lax.psum(out_raw, "dp").astype(F32)
        dense_grad, down_grad = out_grad[:own], out_grad[own:]
        up_grad = reduce_input_grad(up_raw, own_rows, 1)
        qkv_grad = reduce_input_grad(qkv_raw, own_rows, 3)
        small = small_sums(shifts, joined_sum, up_sum)
        small = spread((lax.psum(small[0], "dp"), lax.pmax(small[1], "dp")))
        clipped = clip_columns(qkv_weight, qkv_bias, small, clip_limit, own_heads, head_dim)
        vectors = unpack(small, 3 * width, own, own_ff, own_heads)
        ends = finish_rows(branch_sum, hidden_grad)
    layer_out, tokens_grad = ends
    clipped_weight, clipped_bias = clipped
    shifts, qkv_bias_grad, up_bias_grad, head_maxima = vectors
    return (
        layer_out.reshape(seqs, stretch, width),
        tokens_grad.reshape(seqs, stretch, width),
        shifts[0].reshape(width),
        shifts[1].reshape(width),
        qkv_grad,
        qkv_bias_grad.reshape(3 * width),
        dense_grad,
        shifts[2].reshape(width),
        up_grad,
        up_bias_grad.reshape(parts * own_ff),
        down_grad,
        shifts[2].reshape(width),
        head_maxima.reshape(heads),
        clipped_weight,
        clipped_bias.reshape(2 * width),
    )


def solution(mesh):
    rows = P("dp", "ctx", None)
    weight = P("ctx", None)
    in_specs = (rows, P("dp", "ctx"), P(), P()) + (weight, P()) * 4 + (P(), rows)
    out_specs = (
        (rows, rows, P(), P()) + (weight, P()) * 4 + (P(), weight, P())
    )
    return jax.shard_map(
        per_device, mesh=mesh, in_specs=in_specs, out_specs=out_specs, check_vma=False
    )
```
